32 devices in a mesh: vol: 8 (over z, x), nar: 4 (over y, core).
Axes of the slice: x: 2, y: 2, z: 4, core: 2. Of those that a mesh axis runs over, the one named last changes fastest.
Arguments:
- series: bfloat16 [2048, 2048], P(('vol', 'nar')), may hold values from -6 to 6
- send_rows: int32 [8, 4, 16], P('vol', 'nar'), may hold values from -1 to 63, as said below
- bin_counts: int32 [4], replicated, may hold values from 1 to 128, 256 in all
- observer_cells: int32 [2, 512], replicated, may hold values from 0 to 127
Outputs:
- spectra_out: float32 [4, 128, 2, 512], P('nar', 'vol')
The draws below stay inside these ranges and needn't reach their ends.
Inputs may be any that keep to these rules, and one draw needn't show every extreme that they name: `send_rows`: entry (u, n, k) names the row of device (u, n)'s 64 rows of series for slot k mod 2 bound for the patch owner at vol index k // 2 and nar index n, or is -1 for an empty slot; one device never names a row twice. Nar index m owns bin_counts[m] bins in order, from the sum of the counts before m on; some owner holds exactly 128 bins. `observer_cells`: row 0 holds polar indices, row 1 azimuthal indices.
All inputs are finite; a program needn't handle non-finite values.
Results may differ from the reference program's by a relative error of at most 0.0043.
Values may be sent and summed in bfloat16 or wider, within the bound.
No kernel may reach another device: no remote copies, remote signals or barrier semaphores. Data moves between devices by JAX's collectives and lax.ppermute only.
A program may use at most 64 MiB of HBM per device.

```python
import math
import jax
import jax.numpy as jnp
import numpy as np
from jax import lax

NT = 512
NF = 256
NQ = 4
CAP = 2
VROWS = 64
OBS = 512
FCAP = 128
N_VOL = 8
N_NAR = 4


def draw_send_rows(key, part):
    slot_total = N_VOL * CAP
    key_list = jax.random.split(jax.random.fold_in(key, 11), N_VOL * N_NAR)
    chosen = jax.vmap(lambda single: jax.random.permutation(single, VROWS)[:slot_total])(key_list)
    occupied = jax.random.randint(jax.random.fold_in(key, 12), (N_VOL * N_NAR, slot_total), 0, 5) < 3
    return jnp.where(occupied, chosen, -1).astype(jnp.int32).reshape(N_VOL, N_NAR, slot_total)


def plant(drawn, key, smallest, top_value):
    longest = drawn.shape.index(max(drawn.shape))
    spots = []
    for shift in (0, 1):
        where = [jax.random.randint(jax.random.fold_in(key, axis), (), 0, length) for axis, length in enumerate(drawn.shape)]
        where[longest] = (where[longest] + shift) % drawn.shape[longest]
        spots.append(tuple(where))
    return drawn.at[spots[0]].set(smallest).at[spots[1]].set(top_value)


def level_of(key, dims, shards, smallest, high):
    level, own = 1.0, jax.random.fold_in(key, 6)
    for axis_at, blocks in shards:
        draws = jnp.exp(jax.random.uniform(jax.random.fold_in(own, axis_at), (blocks,), jnp.float32, smallest / len(shards), high / len(shards)))
        level = level * jnp.repeat(draws, dims[axis_at] // blocks).reshape([-1 if axis == axis_at else 1 for axis in range(len(dims))])
    return level


def length_profile(amount, total, reach, slope):
    weights = [(1 << 20) // math.isqrt(standing ** slope) + 1 for standing in range(2, amount + 1)]
    surplus, counts = total - reach - (amount - 1), [1] * (amount - 1)
    while surplus > 0:
        movable = [i for i in range(amount - 1) if counts[i] < reach]
        mass, budget = sum([weights[i] for i in movable]), surplus
        for i in movable:
            more = min(reach - counts[i], max(1, budget * weights[i] // mass), surplus)
            counts[i] = counts[i] + more
            surplus = surplus - more
    return np.array([reach] + counts)


def uneven(stream_key, count, total, bound, slope):
    if count == 2:
        one = jax.random.randint(stream_key, (), max(1, total - bound), min(bound, total - 1) + 1)
        return jnp.stack([one, total - one])
    tallies = jnp.asarray(length_profile(count, total, bound, slope), jnp.int32)
    twos = (count - 1) // 2
    donor, sink = tallies[1:1 + 2 * twos:2], tallies[2:2 + 2 * twos:2]
    room = jnp.minimum(donor - 1, bound - sink)
    moved = jax.random.randint(jax.random.fold_in(stream_key, 1), (twos,), 0, 1 << 20) % (room + 1)
    tallies = tallies.at[1:1 + 2 * twos:2].set(donor - moved).at[2:2 + 2 * twos:2].set(sink + moved)
    return tallies[jax.random.permutation(jax.random.fold_in(stream_key, 2), count)]


def normal_values(rng, extent, scale, limit, cuts=(), held_as=jnp.bfloat16):
    loudness = level_of(rng, extent, cuts, -0.22, 0.18) if cuts else 1.0
    entries = jax.random.normal(rng, extent, jnp.float32) * scale * loudness
    return jnp.minimum(jnp.maximum(entries, -limit), limit).astype(held_as)


def setup_inputs(seed: int = 0) -> dict:
    arg_keys = jax.random.split(jax.random.key(seed), 5)
    series = normal_values(arg_keys[0], (N_VOL * N_NAR * VROWS, NQ * NT), 1.0, 6.0, ((0, 32),))
    send_rows = draw_send_rows(jax.random.fold_in(arg_keys[4], 71), 0)
    bin_counts = uneven(arg_keys[2], N_NAR, NF, FCAP, 2).astype(jnp.int32)
    observer_cells = plant(jax.random.randint(arg_keys[3], (2, OBS), 0, 128), jax.random.fold_in(arg_keys[3], 1), 0, 127).astype(jnp.int32)
    return dict(series=series, send_rows=send_rows, bin_counts=bin_counts, observer_cells=observer_cells)


WAVE_STEP = 0.05

def dft_table(bin_ids, keep_bin, time_len):
    time_steps = jnp.arange(time_len, dtype=jnp.int32)
    frequency = bin_ids.astype(jnp.int32) + 1
    phase_turns = time_steps[:, None] * frequency[None, :] % time_len
    angle_grid = phase_turns.astype(jnp.float32) * (2.0 * math.pi / time_len)
    dft_grid = jnp.stack([jnp.cos(angle_grid), -jnp.sin(angle_grid)], axis=-1)
    dft_grid = jnp.where(keep_bin[None, :, None], dft_grid, jnp.float32(0.0))
    return dft_grid.reshape(time_len, 2 * bin_ids.shape[0]).astype(jnp.bfloat16)

def positions(point_list):
    point_list = point_list.astype(jnp.int32)
    beside_all = (point_list * 1597 % 8191).astype(jnp.float32) * (2.0 * math.pi / 8191.0)
    jitter = (point_list * 613 % 127).astype(jnp.float32) * (0.37 / 127.0)
    axial = (point_list // 128).astype(jnp.float32) * 0.5 + jitter
    return (20.0 * jnp.cos(beside_all), 20.0 * jnp.sin(beside_all), axial)

def directions(obs_cells):
    polar_angle = (obs_cells[0].astype(jnp.float32) + 0.5) * (math.pi / 128.0)
    azimuth = obs_cells[1].astype(jnp.float32) * (2.0 * math.pi / 128.0)
    return (jnp.sin(polar_angle) * jnp.cos(azimuth), jnp.sin(polar_angle) * jnp.sin(azimuth), jnp.cos(polar_angle))

def project(facing, place_xyz):
    dotted = facing[0][:, None] * place_xyz[0][None, :] + facing[1][:, None] * place_xyz[1][None, :]
    return dotted + facing[2][:, None] * place_xyz[2][None, :]

def kernels(bin_ids, dotted):
    wavenumber = (bin_ids.astype(jnp.float32) + 1.0) * WAVE_STEP
    phase_grid = wavenumber[:, None, None] * dotted[None]
    return jnp.concatenate([jnp.cos(phase_grid), jnp.sin(phase_grid)], axis=1).astype(jnp.bfloat16)

def combine(products, bin_ids, facing, norm_scale):
    observers = facing[0].shape[0]
    bin_total = bin_ids.shape[0]
    cos_part = products[:, :observers].reshape(bin_total, observers, NQ, 2)
    sine_part = products[:, observers:].reshape(bin_total, observers, NQ, 2)
    real_part = cos_part[..., 0] + sine_part[..., 1]
    imag_part = cos_part[..., 1] - sine_part[..., 0]
    weights = jnp.stack([jnp.ones_like(facing[0]), facing[0], facing[1], facing[2]], axis=-1)
    real_sum = lax.optimization_barrier(jnp.sum(real_part * weights[None], axis=-1))
    imag_sum = lax.optimization_barrier(jnp.sum(imag_part * weights[None], axis=-1))
    amplitude = (bin_ids.astype(jnp.float32) + 1.0) * (norm_scale / NF)
    return jnp.stack([-amplitude[:, None] * imag_sum, amplitude[:, None] * real_sum], axis=1)

def reference(series, send_rows, bin_counts, observer_cells):
    slot_total = send_rows.shape[2]
    listing = send_rows.reshape(-1)
    point_total = listing.shape[0]
    point_ids = jnp.arange(point_total, dtype=jnp.int32)
    source_rows = point_ids // slot_total * VROWS + jnp.maximum(listing, 0)
    surface_rows = jnp.where((listing >= 0)[:, None], series[source_rows], jnp.zeros((), series.dtype))
    time_len = series.shape[1] // NQ
    all_bins = jnp.arange(NF, dtype=jnp.int32)
    dft_grid = dft_table(all_bins, all_bins >= 0, time_len)
    spectra = jnp.dot(surface_rows.reshape(point_total * NQ, time_len), dft_grid, preferred_element_type=jnp.float32)
    spectra = (spectra * (1.0 / math.sqrt(time_len))).astype(jnp.bfloat16)
    spectra = spectra.reshape(point_total, NQ, NF, 2).transpose(2, 1, 3, 0).reshape(NF, 2 * NQ, point_total)
    facing = directions(observer_cells)
    dotted = project(facing, positions(point_ids))
    norm_scale = 1.0 / math.sqrt(point_total)

    def one_bin(bin_id):
        one_id = bin_id[None]
        green_grid = kernels(one_id, dotted).astype(jnp.float32)
        spec_one = lax.dynamic_index_in_dim(spectra, bin_id, 0, keepdims=True).astype(jnp.float32)
        products = jnp.einsum('bxp,bcp->bxc', green_grid, spec_one, precision=lax.Precision.HIGHEST)
        return combine(products, one_id, facing, norm_scale)[0]
    full_spectra = lax.map(one_bin, all_bins)
    starts = jnp.cumsum(bin_counts) - bin_counts
    slot_ids = jnp.arange(N_NAR * FCAP, dtype=jnp.int32)
    owner_slot = slot_ids // FCAP
    within = slot_ids % FCAP
    chosen_bin = jnp.minimum(starts[owner_slot] + within, NF - 1)
    valid_slot = within < bin_counts[owner_slot]
    result = jnp.where(valid_slot[:, None, None], full_spectra[chosen_bin], jnp.float32(0.0))
    return result.reshape(N_NAR, FCAP, 2, full_spectra.shape[-1])
```

```python
import math

import jax
import jax.numpy as jnp
import numpy as np
from jax import lax
from jax.experimental import pallas as pl
from jax.experimental.pallas import tpu as pltpu
from jax.sharding import PartitionSpec as P

NF = 256
NQ = 4


WAVE_STEP = 0.05


def dft_table(bin_ids, keep_bin, time_len):
    time_steps = jnp.arange(time_len, dtype=jnp.int32)
    frequency = bin_ids + 1
    phase_turns = time_steps[:, None] * frequency[None, :] % time_len
    angle_grid = phase_turns.astype(jnp.float32) * (2.0 * math.pi / time_len)
    dft_grid = jnp.stack([jnp.cos(angle_grid), -jnp.sin(angle_grid)], axis=-1)
    dft_grid = jnp.where(keep_bin[None, :, None], dft_grid, jnp.float32(0.0))
    return dft_grid.reshape(time_len, 2 * bin_ids.shape[0]).astype(jnp.bfloat16)


def positions(point_list):
    beside_all = (point_list * 1597 % 8191).astype(jnp.float32) * (2.0 * math.pi / 8191.0)
    jitter = (point_list * 613 % 127).astype(jnp.float32) * (0.37 / 127.0)
    axial = (point_list // 128).astype(jnp.float32) * 0.5 + jitter
    return (20.0 * jnp.cos(beside_all), 20.0 * jnp.sin(beside_all), axial)


def directions(obs_cells):
    polar_angle = (obs_cells[0].astype(jnp.float32) + 0.5) * (math.pi / 128.0)
    azimuth = obs_cells[1].astype(jnp.float32) * (2.0 * math.pi / 128.0)
    return (
        jnp.sin(polar_angle) * jnp.cos(azimuth),
        jnp.sin(polar_angle) * jnp.sin(azimuth),
        jnp.cos(polar_angle),
    )


def project(facing, place_xyz):
    dotted = facing[0][:, None] * place_xyz[0][None, :] + facing[1][:, None] * place_xyz[1][None, :]
    return dotted + facing[2][:, None] * place_xyz[2][None, :]


def kernels(bin_ids, dotted):
    wavenumber = (bin_ids.astype(jnp.float32) + 1.0) * WAVE_STEP
    phase_grid = wavenumber[:, None, None] * dotted[None]
    return jnp.concatenate([jnp.cos(phase_grid), jnp.sin(phase_grid)], axis=1).astype(jnp.bfloat16)


def combine(products, bin_ids, facing, norm_scale):
    observers = facing[0].shape[0]
    bin_total = bin_ids.shape[0]
    cos_part = products[:, :observers].reshape(bin_total, observers, NQ, 2)
    sine_part = products[:, observers:].reshape(bin_total, observers, NQ, 2)
    real_part = cos_part[..., 0] + sine_part[..., 1]
    imag_part = cos_part[..., 1] - sine_part[..., 0]
    weights = jnp.stack([jnp.ones_like(facing[0]), facing[0], facing[1], facing[2]], axis=-1)
    real_sum = jnp.sum(real_part * weights[None], axis=-1)
    imag_sum = jnp.sum(imag_part * weights[None], axis=-1)
    amplitude = (bin_ids.astype(jnp.float32) + 1.0) * (norm_scale / NF)
    return jnp.stack([-amplitude[:, None] * imag_sum, amplitude[:, None] * real_sum], axis=1)


def apply_green(bin_ids, spec_block, dotted, facing, norm_scale):
    green_grid = kernels(bin_ids, dotted)
    products = jnp.einsum(
        "bxp,bcp->bxc", green_grid, spec_block, preferred_element_type=jnp.float32
    )
    return combine(products, bin_ids, facing, norm_scale)


def per_device_general(series, send_rows, bin_counts, observer_cells):
    vol_count = lax.axis_size("vol")
    nar_count = lax.axis_size("nar")
    vol_index = lax.axis_index("vol")
    nar_index = lax.axis_index("nar")
    bin_cap = vol_count * max(1, 2 * NF // (nar_count * vol_count))
    time_len = series.shape[1] // NQ
    slot_total = send_rows.shape[2]
    slot_width = slot_total // vol_count
    listing = send_rows.reshape(-1)
    picked = jnp.take(series, jnp.maximum(listing, 0), axis=0)
    packed = jnp.where((listing >= 0)[:, None], picked, jnp.zeros((), series.dtype))
    arrived = lax.all_to_all(packed, "vol", split_axis=0, concat_axis=0, tiled=True)
    starts = jnp.cumsum(bin_counts) - bin_counts
    own_start = starts[nar_index]
    own_count = bin_counts[nar_index]
    dft_scale = 1.0 / math.sqrt(time_len)
    within = jnp.arange(bin_cap, dtype=jnp.int32)
    own_table = dft_table(own_start + within, within < own_count, time_len)
    row_piece = lax.all_gather(arrived, "nar", axis=0, tiled=True)
    rows_here = row_piece.shape[0]
    spectral = jnp.dot(
        row_piece.reshape(rows_here * NQ, time_len), own_table, preferred_element_type=jnp.float32
    )
    spectral = (spectral * dft_scale).astype(jnp.bfloat16).reshape(rows_here, NQ, bin_cap, 2)
    spectra = spectral.transpose(2, 1, 3, 0).reshape(bin_cap, 2 * NQ, rows_here)
    local_points = nar_count * slot_total

    def point_ids(vol_owner, flat_index):
        nar_source = flat_index // slot_total
        remain = flat_index % slot_total
        vol_source = remain // slot_width
        within_slot = remain % slot_width
        return (
            (vol_source * nar_count + nar_source) * vol_count + vol_owner
        ) * slot_width + within_slot

    norm_scale = 1.0 / math.sqrt(vol_count * nar_count * slot_total)
    facing = directions(observer_cells)
    share_rows = bin_cap // vol_count
    regrouped = lax.all_to_all(spectra, "vol", split_axis=0, concat_axis=2, tiled=True)
    bin_ids = own_start + vol_index * share_rows + jnp.arange(share_rows, dtype=jnp.int32)
    span_points = local_points * max(1, vol_count // 8)
    turn_count = vol_count * local_points // span_points

    def add_block(turn_index, running):
        first_point = turn_index * span_points
        spec_block = lax.dynamic_slice_in_dim(regrouped, first_point, span_points, 2)
        flat_index = first_point + jnp.arange(span_points, dtype=jnp.int32)
        point_list = point_ids(flat_index // local_points, flat_index % local_points)
        dotted = project(facing, positions(point_list))
        return running + apply_green(bin_ids, spec_block, dotted, facing, norm_scale)

    result = lax.fori_loop(
        0, turn_count, add_block, jnp.zeros((share_rows, 2, observer_cells.shape[1]), jnp.float32)
    )
    return result.reshape(1, share_rows, 2, result.shape[-1])


LANES = 128
TURN = 2.0 * math.pi

WIDE_SIN = (6.2831854820251465, -41.34170150756836, 81.60513305664062, -76.70301818847656,
            42.02592849731445, -14.899847030639648, 3.2381374835968018)
WIDE_COS = (1.0, -19.73920440673828, 64.93911743164062, -85.45014190673828,
            60.16762924194336, -25.967599868774414, 6.528658390045166)
NARROW_SIN = (6.2831854820251465, -41.34168243408203, 81.60247802734375, -76.58128356933594,
              39.76072311401367)
NARROW_COS = (1.0, -19.739208221435547, 64.93934631347656, -85.45356750488281,
              60.143951416015625, -24.981836318969727)


def horner(coefficients, z):
    total = jnp.full_like(z, coefficients[-1])
    for value in coefficients[-2::-1]:
        total = total * z + value
    return total


def cos_sin_turns(turns, narrow=False):
    if narrow:
        z = turns * turns
        return horner(NARROW_COS, z), horner(NARROW_SIN, z) * turns
    turns = turns - jnp.floor(turns + 0.5)
    z = turns * turns
    return horner(WIDE_COS, z), horner(WIDE_SIN, z) * turns


def slot_places(point_total):
    ids = np.arange(point_total, dtype=np.int64)
    angle = (ids * 1597 % 8191).astype(np.float64) * (TURN / 8191.0)
    axial = (ids // 128) * 0.5 + (ids * 613 % 127) * (0.37 / 127.0)
    place = np.stack([20.0 * np.cos(angle), 20.0 * np.sin(angle), axial])
    return place * (WAVE_STEP / TURN)


def dft_constant(time_len):
    turns = np.arange(time_len)[:, None] * (np.arange(NF) + 1)[None, :] % time_len
    angle = turns.astype(np.float32) * np.float32(TURN / time_len)
    grid = np.concatenate([np.cos(angle), -np.sin(angle)], axis=1)
    return grid.astype(jnp.bfloat16)


def own_bins(counts_ref, nar_count):
    nar_index = lax.axis_index("nar")
    start = jnp.int32(0)
    for m in range(nar_count - 1):
        start = start + jnp.where(m < nar_index, counts_ref[m], 0)
    return start, counts_ref[nar_index]


def swap_groups(blocks, width):
    blocks = list(blocks)
    amount = len(blocks)
    lanes = amount * width
    group = lax.broadcasted_iota(jnp.int32, blocks[0].shape, 1) // width
    step = 1
    while step < amount:
        high = (group & step) != 0
        for r in range(amount):
            if r & step == 0:
                x, y = blocks[r], blocks[r | step]
                blocks[r] = jnp.where(high, pltpu.roll(y, step * width, 1), x)
                blocks[r | step] = jnp.where(high, y, pltpu.roll(x, lanes - step * width, 1))
        step *= 2
    return blocks


def pack_kernel(counts_ref, rows_ref, series_ref, table_ref, out_ref, *, nar_count, width):
    row_total = series_ref.shape[0]
    slots = rows_ref.shape[2]
    time_len = series_ref.shape[1] // NQ
    row_ids = lax.broadcasted_iota(jnp.int32, (row_total, slots), 0)
    hot = jnp.where(row_ids == rows_ref[0], 1.0, 0.0).astype(jnp.bfloat16)
    picked = lax.dot_general(
        hot, series_ref[...], (((0,), (0,)), ((), ())), preferred_element_type=jnp.float32
    ).astype(jnp.bfloat16)
    stacked = jnp.concatenate(
        [picked[:, q * time_len:(q + 1) * time_len] for q in range(NQ)], axis=0
    )
    spectral = jnp.dot(stacked, table_ref[...], preferred_element_type=jnp.float32)
    spectral = spectral * (1.0 / math.sqrt(time_len))
    start = jnp.int32(0)
    for m in range(nar_count):
        blocks = []
        for part in range(2):
            half = spectral[:, part * NF:(part + 1) * NF]
            half = pltpu.roll(half, lax.rem(NF - start, NF), 1)[:, :LANES]
            blocks += [half[q * slots:(q + 1) * slots] for q in range(NQ)]
        for v, chunk in enumerate(swap_groups(blocks, width)):
            first = (v * nar_count + m) * slots
            out_ref[first:first + slots, :] = chunk.astype(jnp.bfloat16)
        start = start + counts_ref[m]


def green_kernel(
    counts_ref, cells_ref, place_ref, out_ref, facing_ref, spread_ref, column_ref,
    *, nar_count, share, narrow
):
    points = place_ref.shape[1]
    observers = cells_ref.shape[1]
    start, _ = own_bins(counts_ref, nar_count)
    first_bin = start + lax.axis_index("vol") * share
    base_step = (first_bin + 1).astype(jnp.float32)
    cells = cells_ref[...].astype(jnp.float32)
    cos_polar, sin_polar = cos_sin_turns((cells[0:1] + 0.5) * (1.0 / 256.0))
    cos_azimuth, sin_azimuth = cos_sin_turns(cells[1:2] * (1.0 / 128.0))
    facing = (sin_polar * cos_azimuth, sin_polar * sin_azimuth, cos_polar)
    for axis in range(3):
        facing_ref[axis:axis + 1, :] = facing[axis]
        spread_ref[axis] = jnp.broadcast_to(facing[axis], (8, observers))
    for tile in range(points // LANES):
        column_ref[tile * LANES:(tile + 1) * LANES, :] = (
            place_ref[:, tile * LANES:(tile + 1) * LANES].T
        )
    rows, lanes = 16, 256

    def tile_step(tile, carry):
        first = pl.multiple_of(tile * rows, rows)
        place = [column_ref[pl.ds(first, rows), axis:axis + 1] for axis in range(3)]
        for lane in range(0, observers, lanes):
            def seen(axis):
                return jnp.concatenate([spread_ref[axis, :, lane:lane + lanes]] * (rows // 8), axis=0)
            turns = seen(0) * place[0] + seen(1) * place[1]
            turns = turns + seen(2) * place[2]
            c_now, s_now = cos_sin_turns(turns * base_step)
            c_one, s_one = cos_sin_turns(turns, narrow)
            twice = c_one + c_one
            c_old = c_now * c_one + s_now * s_one
            s_old = s_now * c_one - c_now * s_one
            for j in range(share):
                out_ref[j, pl.ds(first, rows), lane:lane + lanes] = c_now.astype(jnp.bfloat16)
                out_ref[j, pl.ds(first + points, rows), lane:lane + lanes] = s_now.astype(jnp.bfloat16)
                if j < share - 1:
                    c_now, c_old = twice * c_now - c_old, c_now
                    s_now, s_old = twice * s_now - s_old, s_now
        return carry

    lax.fori_loop(0, points // rows, tile_step, 0)


def moment_kernel(
    counts_ref, spectra_ref, green_ref, facing_ref, out_ref, left_ref, moment_ref,
    *, nar_count, share
):
    points = spectra_ref.shape[0]
    half = NQ * share
    tiles = points // LANES
    for tile in range(tiles):
        turned = spectra_ref[tile * LANES:(tile + 1) * LANES, :].astype(jnp.float32).T
        left_ref[tile] = turned
        left_ref[tiles + tile, :half] = turned[half:]
        left_ref[tiles + tile, half:] = -turned[:half]
    pieces = moment_ref.shape[0]
    for j in range(share):
        own = pl.ds(j, 2 * NQ, stride=share)
        left = jnp.concatenate([left_ref[tile, own, :] for tile in range(2 * tiles)], axis=1)
        product = jnp.dot(
            left.astype(jnp.bfloat16), green_ref[j], preferred_element_type=jnp.float32
        )
        for piece in range(pieces):
            moment_ref[piece, own, :] = product[:, piece * LANES:(piece + 1) * LANES]
    sums = []
    for part in range(2):
        columns = []
        for piece in range(pieces):
            first = part * half
            total = moment_ref[piece, first:first + share, :]
            for q in range(1, NQ):
                weight = facing_ref[q - 1:q, piece * LANES:(piece + 1) * LANES]
                first = part * half + q * share
                total = total + moment_ref[piece, first:first + share, :] * weight
            columns.append(total)
        sums.append(jnp.concatenate(columns, axis=1))
    start, count = own_bins(counts_ref, nar_count)
    within = lax.axis_index("vol") * share + lax.broadcasted_iota(jnp.int32, sums[0].shape, 0)
    amplitude = (start + within + 1).astype(jnp.float32) * (1.0 / (math.sqrt(points) * NF))
    valid = within < count
    out_ref[0, :, 0, :] = jnp.where(valid, -amplitude * sums[1], 0.0)
    out_ref[0, :, 1, :] = jnp.where(valid, amplitude * sums[0], 0.0)


def per_device(series, send_rows, bin_counts, observer_cells):
    vol_count = lax.axis_size("vol")
    nar_count = lax.axis_size("nar")
    share = max(1, 2 * NF // (nar_count * vol_count))
    slots = send_rows.shape[2]
    points = vol_count * nar_count * slots
    observers = observer_cells.shape[1]
    time_len = series.shape[1] // NQ
    fits = (
        vol_count == 2 * NQ
        and vol_count * share == LANES
        and slots % 16 == 0
        and points % LANES == 0
        and observers % 256 == 0
        and share * points * observers <= 8 << 20
    )
    if not fits:
        return per_device_general(series, send_rows, bin_counts, observer_cells)
    vmem = pl.BlockSpec(memory_space=pltpu.VMEM)
    smem = pl.BlockSpec(memory_space=pltpu.SMEM)
    places = slot_places(points)
    reach = float(np.sqrt((places ** 2).sum(axis=0)).max())
    place_rows = np.zeros((8, points), np.float32)
    place_rows[:3] = places

    packed = pl.pallas_call(
        lambda *refs: pack_kernel(*refs, nar_count=nar_count, width=share),
        out_shape=jax.ShapeDtypeStruct((points, LANES), jnp.bfloat16),
        in_specs=[smem, vmem, vmem, vmem],
        out_specs=vmem,
        compiler_params=pltpu.CompilerParams(vmem_limit_bytes=8 << 20),
        name="pack_rows",
    )(bin_counts, send_rows, series, jnp.asarray(dft_constant(time_len)))
    spectra = lax.all_to_all(packed, ("vol", "nar"), split_axis=0, concat_axis=0, tiled=True)
    green, facing = pl.pallas_call(
        lambda *refs: green_kernel(
            *refs, nar_count=nar_count, share=share, narrow=reach < 0.249
        ),
        out_shape=(
            jax.ShapeDtypeStruct((share, 2 * points, observers), jnp.bfloat16),
            jax.ShapeDtypeStruct((3, observers), jnp.float32),
        ),
        in_specs=[smem, vmem, vmem],
        out_specs=(vmem, vmem),
        scratch_shapes=[
            pltpu.VMEM((3, 8, observers), jnp.float32),
            pltpu.VMEM((points, 8), jnp.float32),
        ],
        compiler_params=pltpu.CompilerParams(vmem_limit_bytes=24 << 20),
        cost_estimate=pl.CostEstimate(
            flops=60 * share * points * observers, bytes_accessed=4 * share * points * observers,
            transcendentals=0,
        ),
        name="green_grid",
    )(bin_counts, observer_cells, jnp.asarray(place_rows))
    return pl.pallas_call(
        lambda *refs: moment_kernel(*refs, nar_count=nar_count, share=share),
        out_shape=jax.ShapeDtypeStruct((1, share, 2, observers), jnp.float32),
        in_specs=[smem, vmem, vmem, vmem],
        out_specs=vmem,
        scratch_shapes=[
            pltpu.VMEM((2 * points // LANES, LANES, LANES), jnp.float32),
            pltpu.VMEM((observers // LANES, LANES, LANES), jnp.float32),
        ],
        compiler_params=pltpu.CompilerParams(vmem_limit_bytes=24 << 20),
        name="moments",
    )(bin_counts, spectra, green, facing)


def solution(mesh):
    placed = (P(("vol", "nar"), None), P("vol", "nar", None), P(), P())
    return jax.shard_map(
        per_device,
        mesh=mesh,
        in_specs=placed,
        out_specs=P("nar", "vol", None, None),
        check_vma=False,
    )
```

```python
import math

import jax
import jax.numpy as jnp
import numpy as np
from jax import lax
from jax.experimental import pallas as pl
from jax.experimental.pallas import tpu as pltpu
from jax.sharding import PartitionSpec as P

NF = 256
NQ = 4


WAVE_STEP = 0.05


def dft_table(bin_ids, keep_bin, time_len):
    time_steps = jnp.arange(time_len, dtype=jnp.int32)
    frequency = bin_ids + 1
    phase_turns = time_steps[:, None] * frequency[None, :] % time_len
    angle_grid = phase_turns.astype(jnp.float32) * (2.0 * math.pi / time_len)
    dft_grid = jnp.stack([jnp.cos(angle_grid), -jnp.sin(angle_grid)], axis=-1)
    dft_grid = jnp.where(keep_bin[None, :, None], dft_grid, jnp.float32(0.0))
    return dft_grid.reshape(time_len, 2 * bin_ids.shape[0]).astype(jnp.bfloat16)


def positions(point_list):
    beside_all = (point_list * 1597 % 8191).astype(jnp.float32) * (2.0 * math.pi / 8191.0)
    jitter = (point_list * 613 % 127).astype(jnp.float32) * (0.37 / 127.0)
    axial = (point_list // 128).astype(jnp.float32) * 0.5 + jitter
    return (20.0 * jnp.cos(beside_all), 20.0 * jnp.sin(beside_all), axial)


def directions(obs_cells):
    polar_angle = (obs_cells[0].astype(jnp.float32) + 0.5) * (math.pi / 128.0)
    azimuth = obs_cells[1].astype(jnp.float32) * (2.0 * math.pi / 128.0)
    return (
        jnp.sin(polar_angle) * jnp.cos(azimuth),
        jnp.sin(polar_angle) * jnp.sin(azimuth),
        jnp.cos(polar_angle),
    )


def project(facing, place_xyz):
    dotted = facing[0][:, None] * place_xyz[0][None, :] + facing[1][:, None] * place_xyz[1][None, :]
    return dotted + facing[2][:, None] * place_xyz[2][None, :]


def kernels(bin_ids, dotted):
    wavenumber = (bin_ids.astype(jnp.float32) + 1.0) * WAVE_STEP
    phase_grid = wavenumber[:, None, None] * dotted[None]
    return jnp.concatenate([jnp.cos(phase_grid), jnp.sin(phase_grid)], axis=1).astype(jnp.bfloat16)


def combine(products, bin_ids, facing, norm_scale):
    observers = facing[0].shape[0]
    bin_total = bin_ids.shape[0]
    cos_part = products[:, :observers].reshape(bin_total, observers, NQ, 2)
    sine_part = products[:, observers:].reshape(bin_total, observers, NQ, 2)
    real_part = cos_part[..., 0] + sine_part[..., 1]
    imag_part = cos_part[..., 1] - sine_part[..., 0]
    weights = jnp.stack([jnp.ones_like(facing[0]), facing[0], facing[1], facing[2]], axis=-1)
    real_sum = jnp.sum(real_part * weights[None], axis=-1)
    imag_sum = jnp.sum(imag_part * weights[None], axis=-1)
    amplitude = (bin_ids.astype(jnp.float32) + 1.0) * (norm_scale / NF)
    return jnp.stack([-amplitude[:, None] * imag_sum, amplitude[:, None] * real_sum], axis=1)


def apply_green(bin_ids, spec_block, dotted, facing, norm_scale):
    green_grid = kernels(bin_ids, dotted)
    products = jnp.einsum(
        "bxp,bcp->bxc", green_grid, spec_block, preferred_element_type=jnp.float32
    )
    return combine(products, bin_ids, facing, norm_scale)


def per_device_general(series, send_rows, bin_counts, observer_cells):
    vol_count = lax.axis_size("vol")
    nar_count = lax.axis_size("nar")
    vol_index = lax.axis_index("vol")
    nar_index = lax.axis_index("nar")
    bin_cap = vol_count * max(1, 2 * NF // (nar_count * vol_count))
    time_len = series.shape[1] // NQ
    slot_total = send_rows.shape[2]
    slot_width = slot_total // vol_count
    listing = send_rows.reshape(-1)
    picked = jnp.take(series, jnp.maximum(listing, 0), axis=0)
    packed = jnp.where((listing >= 0)[:, None], picked, jnp.zeros((), series.dtype))
    arrived = lax.all_to_all(packed, "vol", split_axis=0, concat_axis=0, tiled=True)
    starts = jnp.cumsum(bin_counts) - bin_counts
    own_start = starts[nar_index]
    own_count = bin_counts[nar_index]
    dft_scale = 1.0 / math.sqrt(time_len)
    within = jnp.arange(bin_cap, dtype=jnp.int32)
    own_table = dft_table(own_start + within, within < own_count, time_len)
    row_piece = lax.all_gather(arrived, "nar", axis=0, tiled=True)
    rows_here = row_piece.shape[0]
    spectral = jnp.dot(
        row_piece.reshape(rows_here * NQ, time_len), own_table, preferred_element_type=jnp.float32
    )
    spectral = (spectral * dft_scale).astype(jnp.bfloat16).reshape(rows_here, NQ, bin_cap, 2)
    spectra = spectral.transpose(2, 1, 3, 0).reshape(bin_cap, 2 * NQ, rows_here)
    local_points = nar_count * slot_total

    def point_ids(vol_owner, flat_index):
        nar_source = flat_index // slot_total
        remain = flat_index % slot_total
        vol_source = remain // slot_width
        within_slot = remain % slot_width
        return (
            (vol_source * nar_count + nar_source) * vol_count + vol_owner
        ) * slot_width + within_slot

    norm_scale = 1.0 / math.sqrt(vol_count * nar_count * slot_total)
    facing = directions(observer_cells)
    share_rows = bin_cap // vol_count
    regrouped = lax.all_to_all(spectra, "vol", split_axis=0, concat_axis=2, tiled=True)
    bin_ids = own_start + vol_index * share_rows + jnp.arange(share_rows, dtype=jnp.int32)
    span_points = local_points * max(1, vol_count // 8)
    turn_count = vol_count * local_points // span_points

    def add_block(turn_index, running):
        first_point = turn_index * span_points
        spec_block = lax.dynamic_slice_in_dim(regrouped, first_point, span_points, 2)
        flat_index = first_point + jnp.arange(span_points, dtype=jnp.int32)
        point_list = point_ids(flat_index // local_points, flat_index % local_points)
        dotted = project(facing, positions(point_list))
        return running + apply_green(bin_ids, spec_block, dotted, facing, norm_scale)

    result = lax.fori_loop(
        0, turn_count, add_block, jnp.zeros((share_rows, 2, observer_cells.shape[1]), jnp.float32)
    )
    return result.reshape(1, share_rows, 2, result.shape[-1])


LANES = 128
TURN = 2.0 * math.pi

WIDE_SIN = (6.2831854820251465, -41.34170150756836, 81.60513305664062, -76.70301818847656,
            42.02592849731445, -14.899847030639648, 3.2381374835968018)
WIDE_COS = (1.0, -19.73920440673828, 64.93911743164062, -85.45014190673828,
            60.16762924194336, -25.967599868774414, 6.528658390045166)
NARROW_SIN = (6.2831854820251465, -41.34168243408203, 81.60247802734375, -76.58128356933594,
              39.76072311401367)
NARROW_COS = (1.0, -19.739208221435547, 64.93934631347656, -85.45356750488281,
              60.143951416015625, -24.981836318969727)


def horner(coefficients, z):
    total = jnp.full_like(z, coefficients[-1])
    for value in coefficients[-2::-1]:
        total = total * z + value
    return total


def cos_sin_turns(turns, narrow=False):
    if narrow:
        z = turns * turns
        return horner(NARROW_COS, z), horner(NARROW_SIN, z) * turns
    turns = turns - jnp.floor(turns + 0.5)
    z = turns * turns
    return horner(WIDE_COS, z), horner(WIDE_SIN, z) * turns


def slot_places(point_total):
    ids = np.arange(point_total, dtype=np.int64)
    angle = (ids * 1597 % 8191).astype(np.float64) * (TURN / 8191.0)
    axial = (ids // 128) * 0.5 + (ids * 613 % 127) * (0.37 / 127.0)
    place = np.stack([20.0 * np.cos(angle), 20.0 * np.sin(angle), axial])
    return place * (WAVE_STEP / TURN)


def dft_constant(time_len):
    turns = np.arange(time_len)[:, None] * (np.arange(NF) + 1)[None, :] % time_len
    angle = turns.astype(np.float32) * np.float32(TURN / time_len)
    grid = np.concatenate([np.cos(angle), -np.sin(angle)], axis=1)
    return grid.astype(jnp.bfloat16)


def own_bins(counts_ref, nar_count):
    nar_index = lax.axis_index("nar")
    start = jnp.int32(0)
    for m in range(nar_count - 1):
        start = start + jnp.where(m < nar_index, counts_ref[m], 0)
    return start, counts_ref[nar_index]


def swap_groups(blocks, width):
    blocks = list(blocks)
    amount = len(blocks)
    lanes = amount * width
    group = lax.broadcasted_iota(jnp.int32, blocks[0].shape, 1) // width
    step = 1
    while step < amount:
        high = (group & step) != 0
        for r in range(amount):
            if r & step == 0:
                x, y = blocks[r], blocks[r | step]
                blocks[r] = jnp.where(high, pltpu.roll(y, step * width, 1), x)
                blocks[r | step] = jnp.where(high, y, pltpu.roll(x, lanes - step * width, 1))
        step *= 2
    return blocks


def in_hbm(array):
    return pltpu.with_memory_space_constraint(array, pltpu.HBM)


def fetch_all(pairs, sems):
    copies = [
        pltpu.make_async_copy(source, target, sems.at[i])
        for i, (source, target) in enumerate(pairs)
    ]
    for copy in copies:
        copy.start()
    return copies


def pack_kernel(
    counts_hbm, rows_hbm, series_hbm, table_hbm, out_ref,
    counts_ref, rows_ref, series_ref, table_ref, sems, *, nar_count, width
):
    copies = fetch_all(
        [(rows_hbm, rows_ref), (series_hbm, series_ref), (table_hbm, table_ref), (counts_hbm, counts_ref)],
        sems,
    )
    row_total = series_ref.shape[0]
    slots = rows_ref.shape[2]
    time_len = series_ref.shape[1] // NQ
    row_ids = lax.broadcasted_iota(jnp.int32, (row_total, slots), 0)
    copies[0].wait()
    hot = jnp.where(row_ids == rows_ref[0], 1.0, 0.0).astype(jnp.bfloat16)
    copies[1].wait()
    picked = lax.dot_general(
        hot, series_ref[...], (((0,), (0,)), ((), ())), preferred_element_type=jnp.float32
    ).astype(jnp.bfloat16)
    stacked = jnp.concatenate(
        [picked[:, q * time_len:(q + 1) * time_len] for q in range(NQ)], axis=0
    )
    copies[2].wait()
    spectral = jnp.dot(stacked, table_ref[...], preferred_element_type=jnp.float32)
    spectral = spectral * (1.0 / math.sqrt(time_len))
    copies[3].wait()
    start = jnp.int32(0)
    for m in range(nar_count):
        blocks = []
        for part in range(2):
            half = spectral[:, part * NF:(part + 1) * NF]
            half = pltpu.roll(half, lax.rem(NF - start, NF), 1)[:, :LANES]
            blocks += [half[q * slots:(q + 1) * slots] for q in range(NQ)]
        for v, chunk in enumerate(swap_groups(blocks, width)):
            first = (v * nar_count + m) * slots
            out_ref[first:first + slots, :] = chunk.astype(jnp.bfloat16)
        start = start + counts_ref[m]


def green_kernel(
    counts_hbm, cells_hbm, place_hbm, near_ref, far_hbm, facing_ref, amplitude_ref,
    counts_ref, cells_ref, place_ref, spread_ref, column_ref, far_ref, sems, far_sem,
    *, nar_count, share, narrow
):
    copies = fetch_all(
        [(counts_hbm, counts_ref), (cells_hbm, cells_ref), (place_hbm, place_ref)], sems
    )
    points = place_ref.shape[1]
    observers = cells_ref.shape[1]
    near = near_ref.shape[0]
    for copy in copies:
        copy.wait()
    start, count = own_bins(counts_ref, nar_count)
    within = lax.axis_index("vol") * share
    base_step = (start + within + 1).astype(jnp.float32)
    within = within + lax.broadcasted_iota(jnp.int32, amplitude_ref.shape, 0)
    amplitude = (start + within + 1).astype(jnp.float32) * (1.0 / (math.sqrt(points) * NF))
    amplitude_ref[...] = jnp.where(within < count, amplitude, 0.0)
    cells = cells_ref[...].astype(jnp.float32)
    cos_polar, sin_polar = cos_sin_turns((cells[0:1] + 0.5) * (1.0 / 256.0))
    cos_azimuth, sin_azimuth = cos_sin_turns(cells[1:2] * (1.0 / 128.0))
    facing = (sin_polar * cos_azimuth, sin_polar * sin_azimuth, cos_polar)
    for axis in range(3):
        facing_ref[axis:axis + 1, :] = facing[axis]
        spread_ref[axis] = jnp.broadcast_to(facing[axis], (8, observers))
    for tile in range(points // LANES):
        column_ref[tile * LANES:(tile + 1) * LANES, :] = (
            place_ref[:, tile * LANES:(tile + 1) * LANES].T
        )
    rows, lanes = 16, 256

    def tile_step(tile, carry):
        first = pl.multiple_of(tile * rows, rows)
        place = [column_ref[pl.ds(first, rows), axis:axis + 1] for axis in range(3)]
        for lane in range(0, observers, lanes):
            def seen(axis):
                return jnp.concatenate([spread_ref[axis, :, lane:lane + lanes]] * (rows // 8), axis=0)
            turns = seen(0) * place[0] + seen(1) * place[1]
            turns = turns + seen(2) * place[2]
            c_now, s_now = cos_sin_turns(turns * base_step)
            c_one, s_one = cos_sin_turns(turns, narrow)
            twice = c_one + c_one
            c_old = c_now * c_one + s_now * s_one
            s_old = s_now * c_one - c_now * s_one
            for j in range(share):
                target = near_ref.at[j] if j < near else far_ref.at[j - near]
                target[pl.ds(first, rows), lane:lane + lanes] = c_now.astype(jnp.bfloat16)
                target[pl.ds(first + points, rows), lane:lane + lanes] = s_now.astype(jnp.bfloat16)
                if j < share - 1:
                    c_now, c_old = twice * c_now - c_old, c_now
                    s_now, s_old = twice * s_now - s_old, s_now
        return carry

    step = 64
    for block in range(0, points, step):
        lax.fori_loop(block // rows, (block + step) // rows, tile_step, 0)
        for first in (block, points + block):
            pltpu.make_async_copy(
                far_ref.at[:, first:first + step, :], far_hbm.at[:, first:first + step, :], far_sem
            ).start()
    pltpu.make_async_copy(far_ref, far_hbm, far_sem).wait()


def moment_kernel(
    spectra_ref, near_ref, far_hbm, facing_ref, amplitude_ref, out_ref,
    left_ref, moment_ref, far_ref, sems, *, share
):
    near = near_ref.shape[0]
    copies = fetch_all([(far_hbm.at[j], far_ref.at[j]) for j in range(share - near)], sems)
    points = spectra_ref.shape[0]
    half = NQ * share
    tiles = points // LANES
    for tile in range(tiles):
        turned = spectra_ref[tile * LANES:(tile + 1) * LANES, :].astype(jnp.float32).T
        left_ref[tile] = turned
        left_ref[tiles + tile, :half] = turned[half:]
        left_ref[tiles + tile, half:] = -turned[:half]
    pieces = moment_ref.shape[0]
    for j in range(share):
        own = pl.ds(j, 2 * NQ, stride=share)
        left = jnp.concatenate([left_ref[tile, own, :] for tile in range(2 * tiles)], axis=1)
        if j >= near:
            copies[j - near].wait()
        green = near_ref[j] if j < near else far_ref[j - near]
        product = jnp.dot(left.astype(jnp.bfloat16), green, preferred_element_type=jnp.float32)
        for piece in range(pieces):
            moment_ref[piece, own, :] = product[:, piece * LANES:(piece + 1) * LANES]
    amplitude = amplitude_ref[...]
    for piece in range(pieces):
        lanes = slice(piece * LANES, (piece + 1) * LANES)
        sums = []
        for part in range(2):
            first = part * half
            total = moment_ref[piece, first:first + share, :]
            for q in range(1, NQ):
                first = part * half + q * share
                total = total + moment_ref[piece, first:first + share, :] * facing_ref[q - 1:q, lanes]
            sums.append(total)
        out_ref[0, :, 0, lanes] = -amplitude * sums[1]
        out_ref[0, :, 1, lanes] = amplitude * sums[0]


def per_device(series, send_rows, bin_counts, observer_cells):
    vol_count = lax.axis_size("vol")
    nar_count = lax.axis_size("nar")
    share = max(1, 2 * NF // (nar_count * vol_count))
    slots = send_rows.shape[2]
    points = vol_count * nar_count * slots
    observers = observer_cells.shape[1]
    time_len = series.shape[1] // NQ
    fits = (
        vol_count == 2 * NQ
        and vol_count * share == LANES
        and slots % 16 == 0
        and points % LANES == 0
        and observers % 256 == 0
        and share * points * observers <= 8 << 20
    )
    if not fits:
        return per_device_general(series, send_rows, bin_counts, observer_cells)
    vmem = pl.BlockSpec(memory_space=pltpu.VMEM)
    hbm = pl.BlockSpec(memory_space=pltpu.HBM)
    places = slot_places(points)
    reach = float(np.sqrt((places ** 2).sum(axis=0)).max())
    place_rows = np.zeros((8, points), np.float32)
    place_rows[:3] = places
    table = dft_constant(time_len)
    near = min(share - 1, (3 << 20) // (4 * points * observers))
    counts_scratch = pltpu.SMEM(bin_counts.shape, jnp.int32)

    packed = pl.pallas_call(
        lambda *refs: pack_kernel(*refs, nar_count=nar_count, width=share),
        out_shape=jax.ShapeDtypeStruct((points, LANES), jnp.bfloat16),
        in_specs=[hbm] * 4,
        out_specs=vmem,
        scratch_shapes=[
            counts_scratch,
            pltpu.VMEM(send_rows.shape, jnp.int32),
            pltpu.VMEM(series.shape, series.dtype),
            pltpu.VMEM(table.shape, jnp.bfloat16),
            pltpu.SemaphoreType.DMA((4,)),
        ],
        compiler_params=pltpu.CompilerParams(vmem_limit_bytes=8 << 20),
        name="pack_rows",
    )(*map(in_hbm, (bin_counts, send_rows, series, jnp.asarray(table))))
    spectra = lax.all_to_all(packed, ("vol", "nar"), split_axis=0, concat_axis=0, tiled=True)
    green_shape = (share - near, 2 * points, observers)
    near_green, far_green, facing, amplitude = pl.pallas_call(
        lambda *refs: green_kernel(
            *refs, nar_count=nar_count, share=share, narrow=reach < 0.249
        ),
        out_shape=(
            jax.ShapeDtypeStruct((near, 2 * points, observers), jnp.bfloat16),
            pltpu.HBM(green_shape, jnp.bfloat16),
            jax.ShapeDtypeStruct((3, observers), jnp.float32),
            jax.ShapeDtypeStruct((share, LANES), jnp.float32),
        ),
        in_specs=[hbm] * 3,
        out_specs=(vmem, hbm, vmem, vmem),
        scratch_shapes=[
            counts_scratch,
            pltpu.VMEM(observer_cells.shape, jnp.int32),
            pltpu.VMEM(place_rows.shape, jnp.float32),
            pltpu.VMEM((3, 8, observers), jnp.float32),
            pltpu.VMEM((points, 8), jnp.float32),
            pltpu.VMEM(green_shape, jnp.bfloat16),
            pltpu.SemaphoreType.DMA((3,)),
            pltpu.SemaphoreType.DMA,
        ],
        compiler_params=pltpu.CompilerParams(vmem_limit_bytes=24 << 20),
        cost_estimate=pl.CostEstimate(
            flops=60 * share * points * observers, bytes_accessed=4 * share * points * observers,
            transcendentals=0,
        ),
        name="green_grid",
    )(*map(in_hbm, (bin_counts, observer_cells, jnp.asarray(place_rows))))
    return pl.pallas_call(
        lambda *refs: moment_kernel(*refs, share=share),
        out_shape=jax.ShapeDtypeStruct((1, share, 2, observers), jnp.float32),
        in_specs=[vmem, vmem, hbm, vmem, vmem],
        out_specs=vmem,
        scratch_shapes=[
            pltpu.VMEM((2 * points // LANES, LANES, LANES), jnp.float32),
            pltpu.VMEM((observers // LANES, LANES, LANES), jnp.float32),
            pltpu.VMEM(green_shape, jnp.bfloat16),
            pltpu.SemaphoreType.DMA((share - near,)),
        ],
        compiler_params=pltpu.CompilerParams(vmem_limit_bytes=24 << 20),
        name="moments",
    )(spectra, near_green, in_hbm(far_green), facing, amplitude)


def solution(mesh):
    placed = (P(("vol", "nar"), None), P("vol", "nar", None), P(), P())
    return jax.shard_map(
        per_device,
        mesh=mesh,
        in_specs=placed,
        out_specs=P("nar", "vol", None, None),
        check_vma=False,
    )
```

```python
import math

import jax
import jax.numpy as jnp
import numpy as np
from jax import lax
from jax.experimental import pallas as pl
from jax.experimental.pallas import tpu as pltpu
from jax.sharding import PartitionSpec as P

NF = 256
NQ = 4


WAVE_STEP = 0.05


def dft_table(bin_ids, keep_bin, time_len):
    time_steps = jnp.arange(time_len, dtype=jnp.int32)
    frequency = bin_ids + 1
    phase_turns = time_steps[:, None] * frequency[None, :] % time_len
    angle_grid = phase_turns.astype(jnp.float32) * (2.0 * math.pi / time_len)
    dft_grid = jnp.stack([jnp.cos(angle_grid), -jnp.sin(angle_grid)], axis=-1)
    dft_grid = jnp.where(keep_bin[None, :, None], dft_grid, jnp.float32(0.0))
    return dft_grid.reshape(time_len, 2 * bin_ids.shape[0]).astype(jnp.bfloat16)


def positions(point_list):
    beside_all = (point_list * 1597 % 8191).astype(jnp.float32) * (2.0 * math.pi / 8191.0)
    jitter = (point_list * 613 % 127).astype(jnp.float32) * (0.37 / 127.0)
    axial = (point_list // 128).astype(jnp.float32) * 0.5 + jitter
    return (20.0 * jnp.cos(beside_all), 20.0 * jnp.sin(beside_all), axial)


def directions(obs_cells):
    polar_angle = (obs_cells[0].astype(jnp.float32) + 0.5) * (math.pi / 128.0)
    azimuth = obs_cells[1].astype(jnp.float32) * (2.0 * math.pi / 128.0)
    return (
        jnp.sin(polar_angle) * jnp.cos(azimuth),
        jnp.sin(polar_angle) * jnp.sin(azimuth),
        jnp.cos(polar_angle),
    )


def project(facing, place_xyz):
    dotted = facing[0][:, None] * place_xyz[0][None, :] + facing[1][:, None] * place_xyz[1][None, :]
    return dotted + facing[2][:, None] * place_xyz[2][None, :]


def kernels(bin_ids, dotted):
    wavenumber = (bin_ids.astype(jnp.float32) + 1.0) * WAVE_STEP
    phase_grid = wavenumber[:, None, None] * dotted[None]
    return jnp.concatenate([jnp.cos(phase_grid), jnp.sin(phase_grid)], axis=1).astype(jnp.bfloat16)


def combine(products, bin_ids, facing, norm_scale):
    observers = facing[0].shape[0]
    bin_total = bin_ids.shape[0]
    cos_part = products[:, :observers].reshape(bin_total, observers, NQ, 2)
    sine_part = products[:, observers:].reshape(bin_total, observers, NQ, 2)
    real_part = cos_part[..., 0] + sine_part[..., 1]
    imag_part = cos_part[..., 1] - sine_part[..., 0]
    weights = jnp.stack([jnp.ones_like(facing[0]), facing[0], facing[1], facing[2]], axis=-1)
    real_sum = jnp.sum(real_part * weights[None], axis=-1)
    imag_sum = jnp.sum(imag_part * weights[None], axis=-1)
    amplitude = (bin_ids.astype(jnp.float32) + 1.0) * (norm_scale / NF)
    return jnp.stack([-amplitude[:, None] * imag_sum, amplitude[:, None] * real_sum], axis=1)


def apply_green(bin_ids, spec_block, dotted, facing, norm_scale):
    green_grid = kernels(bin_ids, dotted)
    products = jnp.einsum(
        "bxp,bcp->bxc", green_grid, spec_block, preferred_element_type=jnp.float32
    )
    return combine(products, bin_ids, facing, norm_scale)


def per_device_general(series, send_rows, bin_counts, observer_cells):
    vol_count = lax.axis_size("vol")
    nar_count = lax.axis_size("nar")
    vol_index = lax.axis_index("vol")
    nar_index = lax.axis_index("nar")
    bin_cap = vol_count * max(1, 2 * NF // (nar_count * vol_count))
    time_len = series.shape[1] // NQ
    slot_total = send_rows.shape[2]
    slot_width = slot_total // vol_count
    listing = send_rows.reshape(-1)
    picked = jnp.take(series, jnp.maximum(listing, 0), axis=0)
    packed = jnp.where((listing >= 0)[:, None], picked, jnp.zeros((), series.dtype))
    arrived = lax.all_to_all(packed, "vol", split_axis=0, concat_axis=0, tiled=True)
    starts = jnp.cumsum(bin_counts) - bin_counts
    own_start = starts[nar_index]
    own_count = bin_counts[nar_index]
    dft_scale = 1.0 / math.sqrt(time_len)
    within = jnp.arange(bin_cap, dtype=jnp.int32)
    own_table = dft_table(own_start + within, within < own_count, time_len)
    row_piece = lax.all_gather(arrived, "nar", axis=0, tiled=True)
    rows_here = row_piece.shape[0]
    spectral = jnp.dot(
        row_piece.reshape(rows_here * NQ, time_len), own_table, preferred_element_type=jnp.float32
    )
    spectral = (spectral * dft_scale).astype(jnp.bfloat16).reshape(rows_here, NQ, bin_cap, 2)
    spectra = spectral.transpose(2, 1, 3, 0).reshape(bin_cap, 2 * NQ, rows_here)
    local_points = nar_count * slot_total

    def point_ids(vol_owner, flat_index):
        nar_source = flat_index // slot_total
        remain = flat_index % slot_total
        vol_source = remain // slot_width
        within_slot = remain % slot_width
        return (
            (vol_source * nar_count + nar_source) * vol_count + vol_owner
        ) * slot_width + within_slot

    norm_scale = 1.0 / math.sqrt(vol_count * nar_count * slot_total)
    facing = directions(observer_cells)
    share_rows = bin_cap // vol_count
    regrouped = lax.all_to_all(spectra, "vol", split_axis=0, concat_axis=2, tiled=True)
    bin_ids = own_start + vol_index * share_rows + jnp.arange(share_rows, dtype=jnp.int32)
    span_points = local_points * max(1, vol_count // 8)
    turn_count = vol_count * local_points // span_points

    def add_block(turn_index, running):
        first_point = turn_index * span_points
        spec_block = lax.dynamic_slice_in_dim(regrouped, first_point, span_points, 2)
        flat_index = first_point + jnp.arange(span_points, dtype=jnp.int32)
        point_list = point_ids(flat_index // local_points, flat_index % local_points)
        dotted = project(facing, positions(point_list))
        return running + apply_green(bin_ids, spec_block, dotted, facing, norm_scale)

    result = lax.fori_loop(
        0, turn_count, add_block, jnp.zeros((share_rows, 2, observer_cells.shape[1]), jnp.float32)
    )
    return result.reshape(1, share_rows, 2, result.shape[-1])


LANES = 128
TURN = 2.0 * math.pi

WIDE_SIN = (6.2831854820251465, -41.34170150756836, 81.60513305664062, -76.70301818847656,
            42.02592849731445, -14.899847030639648, 3.2381374835968018)
WIDE_COS = (1.0, -19.73920440673828, 64.93911743164062, -85.45014190673828,
            60.16762924194336, -25.967599868774414, 6.528658390045166)
NARROW_SIN = (6.2831854820251465, -41.34168243408203, 81.60247802734375, -76.58128356933594,
              39.76072311401367)
NARROW_COS = (1.0, -19.739208221435547, 64.93934631347656, -85.45356750488281,
              60.143951416015625, -24.981836318969727)


def horner(coefficients, z):
    total = jnp.full_like(z, coefficients[-1])
    for value in coefficients[-2::-1]:
        total = total * z + value
    return total


def cos_sin_turns(turns, narrow=False):
    if narrow:
        z = turns * turns
        return horner(NARROW_COS, z), horner(NARROW_SIN, z) * turns
    turns = turns - jnp.floor(turns + 0.5)
    z = turns * turns
    return horner(WIDE_COS, z), horner(WIDE_SIN, z) * turns


def slot_places(point_total):
    ids = np.arange(point_total, dtype=np.int64)
    angle = (ids * 1597 % 8191).astype(np.float64) * (TURN / 8191.0)
    axial = (ids // 128) * 0.5 + (ids * 613 % 127) * (0.37 / 127.0)
    place = np.stack([20.0 * np.cos(angle), 20.0 * np.sin(angle), axial])
    return place * (WAVE_STEP / TURN)


def dft_constant(time_len):
    turns = np.arange(time_len)[:, None] * (np.arange(NF) + 1)[None, :] % time_len
    angle = turns.astype(np.float32) * np.float32(TURN / time_len)
    grid = np.concatenate([np.cos(angle), -np.sin(angle)], axis=1)
    return grid.astype(jnp.bfloat16)


def own_bins(counts_ref, nar_count):
    nar_index = lax.axis_index("nar")
    start = jnp.int32(0)
    for m in range(nar_count - 1):
        start = start + jnp.where(m < nar_index, counts_ref[m], 0)
    return start, counts_ref[nar_index]


def swap_groups(blocks, width):
    blocks = list(blocks)
    amount = len(blocks)
    lanes = amount * width
    group = lax.broadcasted_iota(jnp.int32, blocks[0].shape, 1) // width
    step = 1
    while step < amount:
        high = (group & step) != 0
        for r in range(amount):
            if r & step == 0:
                x, y = blocks[r], blocks[r | step]
                blocks[r] = jnp.where(high, pltpu.roll(y, step * width, 1), x)
                blocks[r | step] = jnp.where(high, y, pltpu.roll(x, lanes - step * width, 1))
        step *= 2
    return blocks


def in_hbm(array):
    return pltpu.with_memory_space_constraint(array, pltpu.HBM)


def fetch_all(pairs, sems):
    copies = [
        pltpu.make_async_copy(source, target, sems.at[i])
        for i, (source, target) in enumerate(pairs)
    ]
    for copy in copies:
        copy.start()
    return copies


def pack_kernel(
    counts_hbm, rows_hbm, series_hbm, table_hbm, out_ref,
    counts_ref, rows_ref, series_ref, table_ref, sems, *, nar_count, width
):
    copies = fetch_all(
        [(rows_hbm, rows_ref), (series_hbm, series_ref), (table_hbm, table_ref), (counts_hbm, counts_ref)],
        sems,
    )
    row_total = series_ref.shape[0]
    slots = rows_ref.shape[2]
    time_len = series_ref.shape[1] // NQ
    row_ids = lax.broadcasted_iota(jnp.int32, (row_total, slots), 0)
    copies[0].wait()
    hot = jnp.where(row_ids == rows_ref[0], 1.0, 0.0).astype(jnp.bfloat16)
    copies[1].wait()
    picked = lax.dot_general(
        hot, series_ref[...], (((0,), (0,)), ((), ())), preferred_element_type=jnp.float32
    ).astype(jnp.bfloat16)
    stacked = jnp.concatenate(
        [picked[:, q * time_len:(q + 1) * time_len] for q in range(NQ)], axis=0
    )
    copies[2].wait()
    spectral = jnp.dot(stacked, table_ref[...], preferred_element_type=jnp.float32)
    spectral = spectral * (1.0 / math.sqrt(time_len))
    copies[3].wait()
    start = jnp.int32(0)
    for m in range(nar_count):
        blocks = []
        for part in range(2):
            half = spectral[:, part * NF:(part + 1) * NF]
            half = pltpu.roll(half, lax.rem(NF - start, NF), 1)[:, :LANES]
            blocks += [half[q * slots:(q + 1) * slots] for q in range(NQ)]
        for v, chunk in enumerate(swap_groups(blocks, width)):
            first = (v * nar_count + m) * slots
            out_ref[first:first + slots, :] = chunk.astype(jnp.bfloat16)
        start = start + counts_ref[m]


def green_kernel(
    counts_hbm, cells_hbm, place_hbm,
    c_first_ref, s_first_ref, c_unit_ref, s_lead_ref, s_unit_hbm, far_hbm, facing_ref, amplitude_ref,
    counts_ref, cells_ref, place_ref, spread_ref, column_ref, s_unit_ref, far_ref, sems, far_sem, unit_sem,
    *, nar_count, share, narrow
):
    copies = fetch_all(
        [(counts_hbm, counts_ref), (cells_hbm, cells_ref), (place_hbm, place_ref)], sems
    )
    points = place_ref.shape[1]
    observers = cells_ref.shape[1]
    near = share - far_ref.shape[0]
    for copy in copies:
        copy.wait()
    start, count = own_bins(counts_ref, nar_count)
    within = lax.axis_index("vol") * share
    base_step = (start + within + 1).astype(jnp.float32)
    within = within + lax.broadcasted_iota(jnp.int32, amplitude_ref.shape, 0)
    amplitude = (start + within + 1).astype(jnp.float32) * (1.0 / (math.sqrt(points) * NF))
    amplitude_ref[...] = jnp.where(within < count, amplitude, 0.0)
    cells = cells_ref[...].astype(jnp.float32)
    cos_polar, sin_polar = cos_sin_turns((cells[0:1] + 0.5) * (1.0 / 256.0))
    cos_azimuth, sin_azimuth = cos_sin_turns(cells[1:2] * (1.0 / 128.0))
    facing = (sin_polar * cos_azimuth, sin_polar * sin_azimuth, cos_polar)
    for axis in range(3):
        facing_ref[axis:axis + 1, :] = facing[axis]
        spread_ref[axis] = jnp.broadcast_to(facing[axis], (8, observers))
    for tile in range(points // LANES):
        column_ref[tile * LANES:(tile + 1) * LANES, :] = (
            place_ref[:, tile * LANES:(tile + 1) * LANES].T
        )
    rows, lanes = 16, 256

    def tile_step(tile, lead):
        first = pl.multiple_of(tile * rows, rows)
        place = [column_ref[pl.ds(first, rows), axis:axis + 1] for axis in range(3)]
        for lane in range(0, observers, lanes):
            def seen(axis):
                return jnp.concatenate([spread_ref[axis, :, lane:lane + lanes]] * (rows // 8), axis=0)
            here = (pl.ds(first, rows), slice(lane, lane + lanes))
            turns = seen(0) * place[0] + seen(1) * place[1]
            turns = turns + seen(2) * place[2]
            c_now, s_now = cos_sin_turns(turns * base_step)
            c_one, s_one = cos_sin_turns(turns, narrow)
            c_first_ref[here] = c_now
            s_first_ref[here] = s_now
            c_unit_ref[here] = c_one
            (s_lead_ref if lead else s_unit_ref)[here] = s_one
            c_jump, s_jump = c_one, s_one
            for _ in range(near.bit_length() - 1):
                double = c_jump + c_jump
                c_jump, s_jump = double * c_jump - 1.0, double * s_jump
            c_now, s_now = c_now * c_jump - s_now * s_jump, s_now * c_jump + c_now * s_jump
            twice = c_one + c_one
            c_old = c_now * c_one + s_now * s_one
            s_old = s_now * c_one - c_now * s_one
            for j in range(share - near):
                far_ref[j, pl.ds(first, rows), lane:lane + lanes] = c_now.astype(jnp.bfloat16)
                far_ref[j, pl.ds(first + points, rows), lane:lane + lanes] = s_now.astype(jnp.bfloat16)
                if j < share - near - 1:
                    c_now, c_old = twice * c_now - c_old, c_now
                    s_now, s_old = twice * s_now - s_old, s_now

    step = 64
    lead_rows = s_lead_ref.shape[0]
    for block in range(0, points, step):
        lead = block < lead_rows
        lax.fori_loop(
            block // rows, (block + step) // rows, lambda t, c: (tile_step(t, lead), c)[1], 0
        )
        for first in (block, points + block):
            pltpu.make_async_copy(
                far_ref.at[:, first:first + step, :], far_hbm.at[:, first:first + step, :], far_sem
            ).start()
    unit_copy = pltpu.make_async_copy(
        s_unit_ref.at[lead_rows:, :], s_unit_hbm.at[lead_rows:, :], unit_sem
    )
    unit_copy.start()
    pltpu.make_async_copy(far_ref, far_hbm, far_sem).wait()
    unit_copy.wait()


def moment_kernel(
    spectra_ref, c_first_ref, s_first_ref, c_unit_ref, s_lead_ref, s_unit_hbm, far_hbm,
    facing_ref, amplitude_ref, out_ref,
    left_ref, moment_ref, s_unit_ref, made_even, made_odd, far_ref, sems, *, share
):
    far = far_ref.shape[0]
    near = share - far
    lead = s_lead_ref.shape[0]
    points, observers = c_first_ref.shape
    half = NQ * share
    tiles = points // LANES
    copies = fetch_all(
        [
            (s_unit_hbm.at[tile * LANES:(tile + 1) * LANES, :], s_unit_ref.at[tile * LANES:(tile + 1) * LANES, :])
            for tile in range(lead // LANES, tiles)
        ] + [(far_hbm.at[j], far_ref.at[j]) for j in range(far)],
        sems,
    )
    unit_copies, far_copies = copies[:-far], copies[-far:]
    pieces = moment_ref.shape[0]
    made = (made_even, made_odd)
    rows, lanes = 16, 256

    for tile in range(tiles):
        turned = spectra_ref[tile * LANES:(tile + 1) * LANES, :].astype(jnp.float32).T
        left_ref[tile] = turned
        left_ref[tiles + tile, :half] = turned[half:]
        left_ref[tiles + tile, half:] = -turned[:half]

    def generate(block, part):
        for lane in range(0, observers, lanes):
            first = block * LANES + part * rows
            here = (slice(first, first + rows), slice(lane, lane + lanes))
            c_now, s_now, c_one = c_first_ref[here], s_first_ref[here], c_unit_ref[here]
            s_one = (s_lead_ref if first < lead else s_unit_ref)[here]
            twice = c_one + c_one
            c_old = c_now * c_one + s_now * s_one
            s_old = s_now * c_one - c_now * s_one
            into = made[block % 2]
            for j in range(near):
                spot = part * rows
                into[j, spot:spot + rows, lane:lane + lanes] = c_now.astype(jnp.bfloat16)
                into[j, LANES + spot:LANES + spot + rows, lane:lane + lanes] = s_now.astype(jnp.bfloat16)
                if j < near - 1:
                    c_now, c_old = twice * c_now - c_old, c_now
                    s_now, s_old = twice * s_now - s_old, s_now

    def multiply(j, which, green, fresh):
        own = pl.ds(j, 2 * NQ, stride=share)
        left = jnp.concatenate([left_ref[tile, own, :] for tile in which], axis=1)
        product = jnp.dot(left.astype(jnp.bfloat16), green, preferred_element_type=jnp.float32)
        for piece in range(pieces):
            value = product[:, piece * LANES:(piece + 1) * LANES]
            if not fresh:
                value = value + moment_ref[piece, own, :]
            moment_ref[piece, own, :] = value

    parts = LANES // rows
    for block in range(tiles):
        if block >= lead // LANES:
            unit_copies[block - lead // LANES].wait()
        for part in range(parts):
            generate(block, part)
            if block:
                for j in range(part * near // parts, (part + 1) * near // parts):
                    multiply(j, (block - 1, tiles + block - 1), made[(block - 1) % 2][j], block == 1)
    for j in range(near):
        multiply(j, (tiles - 1, 2 * tiles - 1), made[(tiles - 1) % 2][j], tiles == 1)
    for j in range(near, share):
        far_copies[j - near].wait()
        multiply(j, range(2 * tiles), far_ref[j - near], True)

    amplitude = amplitude_ref[...]
    for piece in range(pieces):
        lane = slice(piece * LANES, (piece + 1) * LANES)
        sums = []
        for part in range(2):
            first = part * half
            total = moment_ref[piece, first:first + share, :]
            for q in range(1, NQ):
                first = part * half + q * share
                total = total + moment_ref[piece, first:first + share, :] * facing_ref[q - 1:q, lane]
            sums.append(total)
        out_ref[0, :, 0, lane] = -amplitude * sums[1]
        out_ref[0, :, 1, lane] = amplitude * sums[0]


def per_device(series, send_rows, bin_counts, observer_cells):
    vol_count = lax.axis_size("vol")
    nar_count = lax.axis_size("nar")
    share = max(1, 2 * NF // (nar_count * vol_count))
    slots = send_rows.shape[2]
    points = vol_count * nar_count * slots
    observers = observer_cells.shape[1]
    time_len = series.shape[1] // NQ
    fits = (
        vol_count == 2 * NQ
        and vol_count * share == LANES
        and slots % 16 == 0
        and points % LANES == 0
        and share & (share - 1) == 0
        and observers % 256 == 0
        and share * points * observers <= 8 << 20
    )
    if not fits:
        return per_device_general(series, send_rows, bin_counts, observer_cells)
    vmem = pl.BlockSpec(memory_space=pltpu.VMEM)
    hbm = pl.BlockSpec(memory_space=pltpu.HBM)
    places = slot_places(points)
    reach = float(np.sqrt((places ** 2).sum(axis=0)).max())
    place_rows = np.zeros((8, points), np.float32)
    place_rows[:3] = places
    table = dft_constant(time_len)
    near = share // 2
    counts_scratch = pltpu.SMEM(bin_counts.shape, jnp.int32)

    packed = pl.pallas_call(
        lambda *refs: pack_kernel(*refs, nar_count=nar_count, width=share),
        out_shape=jax.ShapeDtypeStruct((points, LANES), jnp.bfloat16),
        in_specs=[hbm] * 4,
        out_specs=vmem,
        scratch_shapes=[
            counts_scratch,
            pltpu.VMEM(send_rows.shape, jnp.int32),
            pltpu.VMEM(series.shape, series.dtype),
            pltpu.VMEM(table.shape, jnp.bfloat16),
            pltpu.SemaphoreType.DMA((4,)),
        ],
        compiler_params=pltpu.CompilerParams(vmem_limit_bytes=8 << 20),
        name="pack_rows",
    )(*map(in_hbm, (bin_counts, send_rows, series, jnp.asarray(table))))
    spectra = lax.all_to_all(packed, ("vol", "nar"), split_axis=0, concat_axis=0, tiled=True)
    far_shape = (share - near, 2 * points, observers)
    grid = jax.ShapeDtypeStruct((points, observers), jnp.float32)
    made = pltpu.VMEM((near, 2 * LANES, observers), jnp.bfloat16)
    c_first, s_first, c_unit, s_lead, s_unit, far_green, facing, amplitude = pl.pallas_call(
        lambda *refs: green_kernel(
            *refs, nar_count=nar_count, share=share, narrow=reach < 0.249
        ),
        out_shape=(
            grid, grid, grid,
            jax.ShapeDtypeStruct((LANES, observers), jnp.float32),
            pltpu.HBM((points, observers), jnp.float32),
            pltpu.HBM(far_shape, jnp.bfloat16),
            jax.ShapeDtypeStruct((3, observers), jnp.float32),
            jax.ShapeDtypeStruct((share, LANES), jnp.float32),
        ),
        in_specs=[hbm] * 3,
        out_specs=(vmem, vmem, vmem, vmem, hbm, hbm, vmem, vmem),
        scratch_shapes=[
            counts_scratch,
            pltpu.VMEM(observer_cells.shape, jnp.int32),
            pltpu.VMEM(place_rows.shape, jnp.float32),
            pltpu.VMEM((3, 8, observers), jnp.float32),
            pltpu.VMEM((points, 8), jnp.float32),
            pltpu.VMEM((points, observers), jnp.float32),
            pltpu.VMEM(far_shape, jnp.bfloat16),
            pltpu.SemaphoreType.DMA((3,)),
            pltpu.SemaphoreType.DMA,
            pltpu.SemaphoreType.DMA,
        ],
        compiler_params=pltpu.CompilerParams(vmem_limit_bytes=24 << 20),
        cost_estimate=pl.CostEstimate(
            flops=60 * share * points * observers, bytes_accessed=4 * share * points * observers,
            transcendentals=0,
        ),
        name="green_grid",
    )(*map(in_hbm, (bin_counts, observer_cells, jnp.asarray(place_rows))))
    return pl.pallas_call(
        lambda *refs: moment_kernel(*refs, share=share),
        out_shape=jax.ShapeDtypeStruct((1, share, 2, observers), jnp.float32),
        in_specs=[vmem, vmem, vmem, vmem, vmem, hbm, hbm, vmem, vmem],
        out_specs=vmem,
        scratch_shapes=[
            pltpu.VMEM((2 * points // LANES, LANES, LANES), jnp.float32),
            pltpu.VMEM((observers // LANES, LANES, LANES), jnp.float32),
            pltpu.VMEM((points, observers), jnp.float32),
            made,
            made,
            pltpu.VMEM(far_shape, jnp.bfloat16),
            pltpu.SemaphoreType.DMA((points // LANES - 1 + share - near,)),
        ],
        compiler_params=pltpu.CompilerParams(vmem_limit_bytes=24 << 20),
        name="moments",
    )(spectra, c_first, s_first, c_unit, s_lead, in_hbm(s_unit), in_hbm(far_green), facing, amplitude)


def solution(mesh):
    placed = (P(("vol", "nar"), None), P("vol", "nar", None), P(), P())
    return jax.shard_map(
        per_device,
        mesh=mesh,
        in_specs=placed,
        out_specs=P("nar", "vol", None, None),
        check_vma=False,
    )
```

```python
import math

import jax
import jax.numpy as jnp
import numpy as np
from jax import lax
from jax.experimental import pallas as pl
from jax.experimental.pallas import tpu as pltpu
from jax.sharding import PartitionSpec as P

NF = 256
NQ = 4


WAVE_STEP = 0.05


def dft_table(bin_ids, keep_bin, time_len):
    time_steps = jnp.arange(time_len, dtype=jnp.int32)
    frequency = bin_ids + 1
    phase_turns = time_steps[:, None] * frequency[None, :] % time_len
    angle_grid = phase_turns.astype(jnp.float32) * (2.0 * math.pi / time_len)
    dft_grid = jnp.stack([jnp.cos(angle_grid), -jnp.sin(angle_grid)], axis=-1)
    dft_grid = jnp.where(keep_bin[None, :, None], dft_grid, jnp.float32(0.0))
    return dft_grid.reshape(time_len, 2 * bin_ids.shape[0]).astype(jnp.bfloat16)


def positions(point_list):
    beside_all = (point_list * 1597 % 8191).astype(jnp.float32) * (2.0 * math.pi / 8191.0)
    jitter = (point_list * 613 % 127).astype(jnp.float32) * (0.37 / 127.0)
    axial = (point_list // 128).astype(jnp.float32) * 0.5 + jitter
    return (20.0 * jnp.cos(beside_all), 20.0 * jnp.sin(beside_all), axial)


def directions(obs_cells):
    polar_angle = (obs_cells[0].astype(jnp.float32) + 0.5) * (math.pi / 128.0)
    azimuth = obs_cells[1].astype(jnp.float32) * (2.0 * math.pi / 128.0)
    return (
        jnp.sin(polar_angle) * jnp.cos(azimuth),
        jnp.sin(polar_angle) * jnp.sin(azimuth),
        jnp.cos(polar_angle),
    )


def project(facing, place_xyz):
    dotted = facing[0][:, None] * place_xyz[0][None, :] + facing[1][:, None] * place_xyz[1][None, :]
    return dotted + facing[2][:, None] * place_xyz[2][None, :]


def kernels(bin_ids, dotted):
    wavenumber = (bin_ids.astype(jnp.float32) + 1.0) * WAVE_STEP
    phase_grid = wavenumber[:, None, None] * dotted[None]
    return jnp.concatenate([jnp.cos(phase_grid), jnp.sin(phase_grid)], axis=1).astype(jnp.bfloat16)


def combine(products, bin_ids, facing, norm_scale):
    observers = facing[0].shape[0]
    bin_total = bin_ids.shape[0]
    cos_part = products[:, :observers].reshape(bin_total, observers, NQ, 2)
    sine_part = products[:, observers:].reshape(bin_total, observers, NQ, 2)
    real_part = cos_part[..., 0] + sine_part[..., 1]
    imag_part = cos_part[..., 1] - sine_part[..., 0]
    weights = jnp.stack([jnp.ones_like(facing[0]), facing[0], facing[1], facing[2]], axis=-1)
    real_sum = jnp.sum(real_part * weights[None], axis=-1)
    imag_sum = jnp.sum(imag_part * weights[None], axis=-1)
    amplitude = (bin_ids.astype(jnp.float32) + 1.0) * (norm_scale / NF)
    return jnp.stack([-amplitude[:, None] * imag_sum, amplitude[:, None] * real_sum], axis=1)


def apply_green(bin_ids, spec_block, dotted, facing, norm_scale):
    green_grid = kernels(bin_ids, dotted)
    products = jnp.einsum(
        "bxp,bcp->bxc", green_grid, spec_block, preferred_element_type=jnp.float32
    )
    return combine(products, bin_ids, facing, norm_scale)


def per_device_general(series, send_rows, bin_counts, observer_cells):
    vol_count = lax.axis_size("vol")
    nar_count = lax.axis_size("nar")
    vol_index = lax.axis_index("vol")
    nar_index = lax.axis_index("nar")
    bin_cap = vol_count * max(1, 2 * NF // (nar_count * vol_count))
    time_len = series.shape[1] // NQ
    slot_total = send_rows.shape[2]
    slot_width = slot_total // vol_count
    listing = send_rows.reshape(-1)
    picked = jnp.take(series, jnp.maximum(listing, 0), axis=0)
    packed = jnp.where((listing >= 0)[:, None], picked, jnp.zeros((), series.dtype))
    arrived = lax.all_to_all(packed, "vol", split_axis=0, concat_axis=0, tiled=True)
    starts = jnp.cumsum(bin_counts) - bin_counts
    own_start = starts[nar_index]
    own_count = bin_counts[nar_index]
    dft_scale = 1.0 / math.sqrt(time_len)
    within = jnp.arange(bin_cap, dtype=jnp.int32)
    own_table = dft_table(own_start + within, within < own_count, time_len)
    row_piece = lax.all_gather(arrived, "nar", axis=0, tiled=True)
    rows_here = row_piece.shape[0]
    spectral = jnp.dot(
        row_piece.reshape(rows_here * NQ, time_len), own_table, preferred_element_type=jnp.float32
    )
    spectral = (spectral * dft_scale).astype(jnp.bfloat16).reshape(rows_here, NQ, bin_cap, 2)
    spectra = spectral.transpose(2, 1, 3, 0).reshape(bin_cap, 2 * NQ, rows_here)
    local_points = nar_count * slot_total

    def point_ids(vol_owner, flat_index):
        nar_source = flat_index // slot_total
        remain = flat_index % slot_total
        vol_source = remain // slot_width
        within_slot = remain % slot_width
        return (
            (vol_source * nar_count + nar_source) * vol_count + vol_owner
        ) * slot_width + within_slot

    norm_scale = 1.0 / math.sqrt(vol_count * nar_count * slot_total)
    facing = directions(observer_cells)
    share_rows = bin_cap // vol_count
    regrouped = lax.all_to_all(spectra, "vol", split_axis=0, concat_axis=2, tiled=True)
    bin_ids = own_start + vol_index * share_rows + jnp.arange(share_rows, dtype=jnp.int32)
    span_points = local_points * max(1, vol_count // 8)
    turn_count = vol_count * local_points // span_points

    def add_block(turn_index, running):
        first_point = turn_index * span_points
        spec_block = lax.dynamic_slice_in_dim(regrouped, first_point, span_points, 2)
        flat_index = first_point + jnp.arange(span_points, dtype=jnp.int32)
        point_list = point_ids(flat_index // local_points, flat_index % local_points)
        dotted = project(facing, positions(point_list))
        return running + apply_green(bin_ids, spec_block, dotted, facing, norm_scale)

    result = lax.fori_loop(
        0, turn_count, add_block, jnp.zeros((share_rows, 2, observer_cells.shape[1]), jnp.float32)
    )
    return result.reshape(1, share_rows, 2, result.shape[-1])


LANES = 128
TURN = 2.0 * math.pi

WIDE_SIN = (6.2831854820251465, -41.34170150756836, 81.60513305664062, -76.70301818847656,
            42.02592849731445, -14.899847030639648, 3.2381374835968018)
WIDE_COS = (1.0, -19.73920440673828, 64.93911743164062, -85.45014190673828,
            60.16762924194336, -25.967599868774414, 6.528658390045166)
NARROW_SIN = (6.2831854820251465, -41.34168243408203, 81.60247802734375, -76.58128356933594,
              39.76072311401367)
NARROW_COS = (1.0, -19.739208221435547, 64.93934631347656, -85.45356750488281,
              60.143951416015625, -24.981836318969727)


def horner(coefficients, z):
    total = jnp.full_like(z, coefficients[-1])
    for value in coefficients[-2::-1]:
        total = total * z + value
    return total


def cos_sin_turns(turns, narrow=False):
    if narrow:
        z = turns * turns
        return horner(NARROW_COS, z), horner(NARROW_SIN, z) * turns
    turns = turns - jnp.floor(turns + 0.5)
    z = turns * turns
    return horner(WIDE_COS, z), horner(WIDE_SIN, z) * turns


def slot_places(point_total):
    ids = np.arange(point_total, dtype=np.int64)
    angle = (ids * 1597 % 8191).astype(np.float64) * (TURN / 8191.0)
    axial = (ids // 128) * 0.5 + (ids * 613 % 127) * (0.37 / 127.0)
    place = np.stack([20.0 * np.cos(angle), 20.0 * np.sin(angle), axial])
    return place * (WAVE_STEP / TURN)


def dft_constant(time_len):
    turns = np.arange(time_len)[:, None] * (np.arange(NF) + 1)[None, :] % time_len
    angle = turns.astype(np.float32) * np.float32(TURN / time_len)
    grid = np.concatenate([np.cos(angle), -np.sin(angle)], axis=1)
    return grid.astype(jnp.bfloat16)


def own_bins(counts_ref, nar_count):
    nar_index = lax.axis_index("nar")
    start = jnp.int32(0)
    for m in range(nar_count - 1):
        start = start + jnp.where(m < nar_index, counts_ref[m], 0)
    return start, counts_ref[nar_index]


def swap_groups(blocks, width):
    blocks = list(blocks)
    amount = len(blocks)
    lanes = amount * width
    group = lax.broadcasted_iota(jnp.int32, blocks[0].shape, 1) // width
    step = 1
    while step < amount:
        high = (group & step) != 0
        for r in range(amount):
            if r & step == 0:
                x, y = blocks[r], blocks[r | step]
                blocks[r] = jnp.where(high, pltpu.roll(y, step * width, 1), x)
                blocks[r | step] = jnp.where(high, y, pltpu.roll(x, lanes - step * width, 1))
        step *= 2
    return blocks


def in_hbm(array):
    return pltpu.with_memory_space_constraint(array, pltpu.HBM)


def fetch_all(pairs, sems):
    copies = [
        pltpu.make_async_copy(source, target, sems.at[i])
        for i, (source, target) in enumerate(pairs)
    ]
    for copy in copies:
        copy.start()
    return copies


def pack_kernel(
    counts_hbm, rows_hbm, series_hbm, table_hbm, out_ref,
    counts_ref, rows_ref, series_ref, table_ref, sems, *, nar_count, width
):
    copies = fetch_all(
        [(rows_hbm, rows_ref), (series_hbm, series_ref), (table_hbm, table_ref), (counts_hbm, counts_ref)],
        sems,
    )
    row_total = series_ref.shape[0]
    slots = rows_ref.shape[2]
    time_len = series_ref.shape[1] // NQ
    row_ids = lax.broadcasted_iota(jnp.int32, (row_total, slots), 0)
    copies[0].wait()
    hot = jnp.where(row_ids == rows_ref[0], 1.0, 0.0).astype(jnp.bfloat16)
    copies[1].wait()
    picked = lax.dot_general(
        hot, series_ref[...], (((0,), (0,)), ((), ())), preferred_element_type=jnp.float32
    ).astype(jnp.bfloat16)
    stacked = jnp.concatenate(
        [picked[:, q * time_len:(q + 1) * time_len] for q in range(NQ)], axis=0
    )
    copies[2].wait()
    spectral = jnp.dot(stacked, table_ref[...], preferred_element_type=jnp.float32)
    spectral = spectral * (1.0 / math.sqrt(time_len))
    copies[3].wait()
    start = jnp.int32(0)
    for m in range(nar_count):
        blocks = []
        for part in range(2):
            half = spectral[:, part * NF:(part + 1) * NF]
            half = pltpu.roll(half, lax.rem(NF - start, NF), 1)[:, :LANES]
            blocks += [half[q * slots:(q + 1) * slots] for q in range(NQ)]
        for v, chunk in enumerate(swap_groups(blocks, width)):
            first = (v * nar_count + m) * slots
            out_ref[first:first + slots, :] = chunk.astype(jnp.bfloat16)
        start = start + counts_ref[m]


def green_kernel(
    counts_hbm, cells_hbm, place_hbm,
    c_next_ref, s_next_ref, c_unit_ref, s_lead_ref, s_unit_hbm, far_hbm, facing_ref, amplitude_ref,
    counts_ref, cells_ref, place_ref, spread_ref, column_ref, s_unit_ref, far_ref, sems, far_sem, unit_sem,
    *, nar_count, share, narrow
):
    copies = fetch_all(
        [(counts_hbm, counts_ref), (cells_hbm, cells_ref), (place_hbm, place_ref)], sems
    )
    points = place_ref.shape[1]
    observers = cells_ref.shape[1]
    far = far_ref.shape[0]
    for copy in copies:
        copy.wait()
    start, count = own_bins(counts_ref, nar_count)
    within = lax.axis_index("vol") * share
    base_step = (start + within + 1).astype(jnp.float32)
    within = within + lax.broadcasted_iota(jnp.int32, amplitude_ref.shape, 0)
    amplitude = (start + within + 1).astype(jnp.float32) * (1.0 / (math.sqrt(points) * NF))
    amplitude_ref[...] = jnp.where(within < count, amplitude, 0.0)
    cells = cells_ref[...].astype(jnp.float32)
    cos_polar, sin_polar = cos_sin_turns((cells[0:1] + 0.5) * (1.0 / 256.0))
    cos_azimuth, sin_azimuth = cos_sin_turns(cells[1:2] * (1.0 / 128.0))
    facing = (sin_polar * cos_azimuth, sin_polar * sin_azimuth, cos_polar)
    for axis in range(3):
        facing_ref[axis:axis + 1, :] = facing[axis]
        spread_ref[axis] = jnp.broadcast_to(facing[axis], (8, observers))
    for tile in range(points // LANES):
        column_ref[tile * LANES:(tile + 1) * LANES, :] = (
            place_ref[:, tile * LANES:(tile + 1) * LANES].T
        )
    rows, lanes = 16, 256

    def tile_step(tile, lead):
        first = pl.multiple_of(tile * rows, rows)
        place = [column_ref[pl.ds(first, rows), axis:axis + 1] for axis in range(3)]
        for lane in range(0, observers, lanes):
            def seen(axis):
                return jnp.concatenate([spread_ref[axis, :, lane:lane + lanes]] * (rows // 8), axis=0)
            here = (pl.ds(first, rows), slice(lane, lane + lanes))
            turns = seen(0) * place[0] + seen(1) * place[1]
            turns = turns + seen(2) * place[2]
            c_now, s_now = cos_sin_turns(turns * base_step)
            c_one, s_one = cos_sin_turns(turns, narrow)
            c_unit_ref[here] = c_one
            (s_lead_ref if lead else s_unit_ref)[here] = s_one
            twice = c_one + c_one
            c_old = c_now * c_one + s_now * s_one
            s_old = s_now * c_one - c_now * s_one
            for j in range(far):
                far_ref[j, pl.ds(first, rows), lane:lane + lanes] = c_now.astype(jnp.bfloat16)
                far_ref[j, pl.ds(first + points, rows), lane:lane + lanes] = s_now.astype(jnp.bfloat16)
                c_now, c_old = twice * c_now - c_old, c_now
                s_now, s_old = twice * s_now - s_old, s_now
            c_next_ref[here] = c_now
            s_next_ref[here] = s_now

    step = 64
    lead_rows = s_lead_ref.shape[0]
    for block in range(0, points, step):
        lead = block < lead_rows
        def pair_step(pair, carry):
            for k in range(2):
                tile_step(pair * 2 + k, lead)
            return carry

        lax.fori_loop(block // rows // 2, (block + step) // rows // 2, pair_step, 0)
        for first in (block, points + block):
            pltpu.make_async_copy(
                far_ref.at[:, first:first + step, :], far_hbm.at[:, first:first + step, :], far_sem
            ).start()
    unit_copy = pltpu.make_async_copy(
        s_unit_ref.at[lead_rows:, :], s_unit_hbm.at[lead_rows:, :], unit_sem
    )
    unit_copy.start()
    pltpu.make_async_copy(far_ref, far_hbm, far_sem).wait()
    unit_copy.wait()


def moment_kernel(
    spectra_ref, c_next_ref, s_next_ref, c_unit_ref, s_lead_ref, s_unit_hbm, far_hbm,
    facing_ref, amplitude_ref, out_ref,
    left_ref, moment_ref, s_unit_ref, made_even, made_odd, far_ref, sems, *, share
):
    far = far_ref.shape[0]
    near = share - far
    lead = s_lead_ref.shape[0]
    points, observers = c_next_ref.shape
    half = NQ * share
    tiles = points // LANES
    unit_copies, far_copies = {}, []
    for k in range(max(tiles, far)):
        if lead // LANES <= k < tiles:
            spot = slice(k * LANES, (k + 1) * LANES)
            unit_copies[k] = pltpu.make_async_copy(
                s_unit_hbm.at[spot, :], s_unit_ref.at[spot, :], sems.at[far + k]
            )
            unit_copies[k].start()
        if k < far:
            far_copies.append(
                pltpu.make_async_copy(far_hbm.at[k], far_ref.at[k], sems.at[k])
            )
            far_copies[k].start()
    made = (made_even, made_odd)
    rows, lanes = 16, 256

    for tile in range(tiles):
        turned = spectra_ref[tile * LANES:(tile + 1) * LANES, :].astype(jnp.float32).T
        left_ref[tile] = turned
        left_ref[tiles + tile, :half] = turned[half:]
        left_ref[tiles + tile, half:] = -turned[:half]

    def generate(block, part):
        first = pl.multiple_of(block * LANES + part * rows, rows)
        spot = pl.multiple_of(part * rows, rows)
        into = made[block % 2]
        s_source = s_lead_ref if block * LANES < lead else s_unit_ref
        for lane in range(0, observers, lanes):
            here = (pl.ds(first, rows), slice(lane, lane + lanes))
            c_now, s_now, c_one, s_one = c_next_ref[here], s_next_ref[here], c_unit_ref[here], s_source[here]
            twice = c_one + c_one
            c_old = c_now * c_one + s_now * s_one
            s_old = s_now * c_one - c_now * s_one
            for j in range(near):
                into[j, pl.ds(spot, rows), lane:lane + lanes] = c_now.astype(jnp.bfloat16)
                into[j, pl.ds(LANES + spot, rows), lane:lane + lanes] = s_now.astype(jnp.bfloat16)
                if j < near - 1:
                    c_now, c_old = twice * c_now - c_old, c_now
                    s_now, s_old = twice * s_now - s_old, s_now

    def multiply(j, which, green, fresh):
        own = pl.ds(j, 2 * NQ, stride=share)
        left = jnp.concatenate([left_ref[tile, own, :] for tile in which], axis=1)
        product = jnp.dot(left.astype(jnp.bfloat16), green, preferred_element_type=jnp.float32)
        spot = pl.ds(pl.multiple_of(2 * NQ * j, 2 * NQ), 2 * NQ)
        for piece in range(observers // LANES):
            value = product[:, piece * LANES:(piece + 1) * LANES]
            moment_ref[piece, spot, :] = value if fresh else moment_ref[piece, spot, :] + value

    parts = LANES // rows
    for block in range(tiles):
        if block in unit_copies:
            unit_copies[block].wait()

        def part_step(part, carry):
            if block:
                multiply(
                    far + part, (block - 1, tiles + block - 1), made[(block - 1) % 2][part], block == 1
                )
            generate(block, part)
            return carry

        lax.fori_loop(0, parts, part_step, 0)
    for j in range(near):
        multiply(far + j, (tiles - 1, 2 * tiles - 1), made[(tiles - 1) % 2][j], tiles == 1)
    for j in range(far):
        far_copies[j].wait()
        multiply(j, range(2 * tiles), far_ref[j], True)

    amplitude = amplitude_ref[...]
    for piece in range(observers // LANES):
        lane = slice(piece * LANES, (piece + 1) * LANES)
        sums = []
        for part in range(2):
            total = None
            for q in range(NQ):
                term = moment_ref[piece, pl.ds(part * NQ + q, share, stride=2 * NQ), :]
                if q:
                    term = term * facing_ref[q - 1:q, lane]
                total = term if total is None else total + term
            sums.append(total)
        out_ref[0, :, 0, lane] = -amplitude * sums[1]
        out_ref[0, :, 1, lane] = amplitude * sums[0]


def per_device(series, send_rows, bin_counts, observer_cells):
    vol_count = lax.axis_size("vol")
    nar_count = lax.axis_size("nar")
    share = max(1, 2 * NF // (nar_count * vol_count))
    slots = send_rows.shape[2]
    points = vol_count * nar_count * slots
    observers = observer_cells.shape[1]
    time_len = series.shape[1] // NQ
    fits = (
        vol_count == 2 * NQ
        and vol_count * share == LANES
        and slots % 16 == 0
        and points % LANES == 0
        and share == 2 * (LANES // 16)
        and observers % 256 == 0
        and share * points * observers <= 8 << 20
    )
    if not fits:
        return per_device_general(series, send_rows, bin_counts, observer_cells)
    vmem = pl.BlockSpec(memory_space=pltpu.VMEM)
    hbm = pl.BlockSpec(memory_space=pltpu.HBM)
    places = slot_places(points)
    reach = float(np.sqrt((places ** 2).sum(axis=0)).max())
    place_rows = np.zeros((8, points), np.float32)
    place_rows[:3] = places
    table = dft_constant(time_len)
    near = share // 2
    counts_scratch = pltpu.SMEM(bin_counts.shape, jnp.int32)

    packed = pl.pallas_call(
        lambda *refs: pack_kernel(*refs, nar_count=nar_count, width=share),
        out_shape=jax.ShapeDtypeStruct((points, LANES), jnp.bfloat16),
        in_specs=[hbm] * 4,
        out_specs=vmem,
        scratch_shapes=[
            counts_scratch,
            pltpu.VMEM(send_rows.shape, jnp.int32),
            pltpu.VMEM(series.shape, series.dtype),
            pltpu.VMEM(table.shape, jnp.bfloat16),
            pltpu.SemaphoreType.DMA((4,)),
        ],
        compiler_params=pltpu.CompilerParams(vmem_limit_bytes=8 << 20),
        name="pack_rows",
    )(*map(in_hbm, (bin_counts, send_rows, series, jnp.asarray(table))))
    spectra = lax.all_to_all(packed, ("vol", "nar"), split_axis=0, concat_axis=0, tiled=True)
    far_shape = (share - near, 2 * points, observers)
    grid = jax.ShapeDtypeStruct((points, observers), jnp.float32)
    made = pltpu.VMEM((near, 2 * LANES, observers), jnp.bfloat16)
    c_next, s_next, c_unit, s_lead, s_unit, far_green, facing, amplitude = pl.pallas_call(
        lambda *refs: green_kernel(
            *refs, nar_count=nar_count, share=share, narrow=reach < 0.249
        ),
        out_shape=(
            grid, grid, grid,
            jax.ShapeDtypeStruct((LANES, observers), jnp.float32),
            pltpu.HBM((points, observers), jnp.float32),
            pltpu.HBM(far_shape, jnp.bfloat16),
            jax.ShapeDtypeStruct((3, observers), jnp.float32),
            jax.ShapeDtypeStruct((share, LANES), jnp.float32),
        ),
        in_specs=[hbm] * 3,
        out_specs=(vmem, vmem, vmem, vmem, hbm, hbm, vmem, vmem),
        scratch_shapes=[
            counts_scratch,
            pltpu.VMEM(observer_cells.shape, jnp.int32),
            pltpu.VMEM(place_rows.shape, jnp.float32),
            pltpu.VMEM((3, 8, observers), jnp.float32),
            pltpu.VMEM((points, 8), jnp.float32),
            pltpu.VMEM((points, observers), jnp.float32),
            pltpu.VMEM(far_shape, jnp.bfloat16),
            pltpu.SemaphoreType.DMA((3,)),
            pltpu.SemaphoreType.DMA,
            pltpu.SemaphoreType.DMA,
        ],
        compiler_params=pltpu.CompilerParams(vmem_limit_bytes=24 << 20),
        cost_estimate=pl.CostEstimate(
            flops=60 * share * points * observers, bytes_accessed=4 * share * points * observers,
            transcendentals=0,
        ),
        name="green_grid",
    )(*map(in_hbm, (bin_counts, observer_cells, jnp.asarray(place_rows))))
    return pl.pallas_call(
        lambda *refs: moment_kernel(*refs, share=share),
        out_shape=jax.ShapeDtypeStruct((1, share, 2, observers), jnp.float32),
        in_specs=[vmem, vmem, vmem, vmem, vmem, hbm, hbm, vmem, vmem],
        out_specs=vmem,
        scratch_shapes=[
            pltpu.VMEM((2 * points // LANES, LANES, LANES), jnp.float32),
            pltpu.VMEM((observers // LANES, LANES, LANES), jnp.float32),
            pltpu.VMEM((points, observers), jnp.float32),
            made,
            made,
            pltpu.VMEM(far_shape, jnp.bfloat16),
            pltpu.SemaphoreType.DMA((points // LANES + share - near,)),
        ],
        compiler_params=pltpu.CompilerParams(vmem_limit_bytes=24 << 20),
        name="moments",
    )(spectra, c_next, s_next, c_unit, s_lead, in_hbm(s_unit), in_hbm(far_green), facing, amplitude)


def solution(mesh):
    placed = (P(("vol", "nar"), None), P("vol", "nar", None), P(), P())
    return jax.shard_map(
        per_device,
        mesh=mesh,
        in_specs=placed,
        out_specs=P("nar", "vol", None, None),
        check_vma=False,
    )
```

```python
import math

import jax
import jax.numpy as jnp
import numpy as np
from jax import lax
from jax.experimental import pallas as pl
from jax.experimental.pallas import tpu as pltpu
from jax.sharding import PartitionSpec as P

NF = 256
NQ = 4


WAVE_STEP = 0.05


def dft_table(bin_ids, keep_bin, time_len):
    time_steps = jnp.arange(time_len, dtype=jnp.int32)
    frequency = bin_ids + 1
    phase_turns = time_steps[:, None] * frequency[None, :] % time_len
    angle_grid = phase_turns.astype(jnp.float32) * (2.0 * math.pi / time_len)
    dft_grid = jnp.stack([jnp.cos(angle_grid), -jnp.sin(angle_grid)], axis=-1)
    dft_grid = jnp.where(keep_bin[None, :, None], dft_grid, jnp.float32(0.0))
    return dft_grid.reshape(time_len, 2 * bin_ids.shape[0]).astype(jnp.bfloat16)


def positions(point_list):
    beside_all = (point_list * 1597 % 8191).astype(jnp.float32) * (2.0 * math.pi / 8191.0)
    jitter = (point_list * 613 % 127).astype(jnp.float32) * (0.37 / 127.0)
    axial = (point_list // 128).astype(jnp.float32) * 0.5 + jitter
    return (20.0 * jnp.cos(beside_all), 20.0 * jnp.sin(beside_all), axial)


def directions(obs_cells):
    polar_angle = (obs_cells[0].astype(jnp.float32) + 0.5) * (math.pi / 128.0)
    azimuth = obs_cells[1].astype(jnp.float32) * (2.0 * math.pi / 128.0)
    return (
        jnp.sin(polar_angle) * jnp.cos(azimuth),
        jnp.sin(polar_angle) * jnp.sin(azimuth),
        jnp.cos(polar_angle),
    )


def project(facing, place_xyz):
    dotted = facing[0][:, None] * place_xyz[0][None, :] + facing[1][:, None] * place_xyz[1][None, :]
    return dotted + facing[2][:, None] * place_xyz[2][None, :]


def kernels(bin_ids, dotted):
    wavenumber = (bin_ids.astype(jnp.float32) + 1.0) * WAVE_STEP
    phase_grid = wavenumber[:, None, None] * dotted[None]
    return jnp.concatenate([jnp.cos(phase_grid), jnp.sin(phase_grid)], axis=1).astype(jnp.bfloat16)


def combine(products, bin_ids, facing, norm_scale):
    observers = facing[0].shape[0]
    bin_total = bin_ids.shape[0]
    cos_part = products[:, :observers].reshape(bin_total, observers, NQ, 2)
    sine_part = products[:, observers:].reshape(bin_total, observers, NQ, 2)
    real_part = cos_part[..., 0] + sine_part[..., 1]
    imag_part = cos_part[..., 1] - sine_part[..., 0]
    weights = jnp.stack([jnp.ones_like(facing[0]), facing[0], facing[1], facing[2]], axis=-1)
    real_sum = jnp.sum(real_part * weights[None], axis=-1)
    imag_sum = jnp.sum(imag_part * weights[None], axis=-1)
    amplitude = (bin_ids.astype(jnp.float32) + 1.0) * (norm_scale / NF)
    return jnp.stack([-amplitude[:, None] * imag_sum, amplitude[:, None] * real_sum], axis=1)


def apply_green(bin_ids, spec_block, dotted, facing, norm_scale):
    green_grid = kernels(bin_ids, dotted)
    products = jnp.einsum(
        "bxp,bcp->bxc", green_grid, spec_block, preferred_element_type=jnp.float32
    )
    return combine(products, bin_ids, facing, norm_scale)


def per_device_general(series, send_rows, bin_counts, observer_cells):
    vol_count = lax.axis_size("vol")
    nar_count = lax.axis_size("nar")
    vol_index = lax.axis_index("vol")
    nar_index = lax.axis_index("nar")
    bin_cap = vol_count * max(1, 2 * NF // (nar_count * vol_count))
    time_len = series.shape[1] // NQ
    slot_total = send_rows.shape[2]
    slot_width = slot_total // vol_count
    listing = send_rows.reshape(-1)
    picked = jnp.take(series, jnp.maximum(listing, 0), axis=0)
    packed = jnp.where((listing >= 0)[:, None], picked, jnp.zeros((), series.dtype))
    arrived = lax.all_to_all(packed, "vol", split_axis=0, concat_axis=0, tiled=True)
    starts = jnp.cumsum(bin_counts) - bin_counts
    own_start = starts[nar_index]
    own_count = bin_counts[nar_index]
    dft_scale = 1.0 / math.sqrt(time_len)
    within = jnp.arange(bin_cap, dtype=jnp.int32)
    own_table = dft_table(own_start + within, within < own_count, time_len)
    row_piece = lax.all_gather(arrived, "nar", axis=0, tiled=True)
    rows_here = row_piece.shape[0]
    spectral = jnp.dot(
        row_piece.reshape(rows_here * NQ, time_len), own_table, preferred_element_type=jnp.float32
    )
    spectral = (spectral * dft_scale).astype(jnp.bfloat16).reshape(rows_here, NQ, bin_cap, 2)
    spectra = spectral.transpose(2, 1, 3, 0).reshape(bin_cap, 2 * NQ, rows_here)
    local_points = nar_count * slot_total

    def point_ids(vol_owner, flat_index):
        nar_source = flat_index // slot_total
        remain = flat_index % slot_total
        vol_source = remain // slot_width
        within_slot = remain % slot_width
        return (
            (vol_source * nar_count + nar_source) * vol_count + vol_owner
        ) * slot_width + within_slot

    norm_scale = 1.0 / math.sqrt(vol_count * nar_count * slot_total)
    facing = directions(observer_cells)
    share_rows = bin_cap // vol_count
    regrouped = lax.all_to_all(spectra, "vol", split_axis=0, concat_axis=2, tiled=True)
    bin_ids = own_start + vol_index * share_rows + jnp.arange(share_rows, dtype=jnp.int32)
    span_points = local_points * max(1, vol_count // 8)
    turn_count = vol_count * local_points // span_points

    def add_block(turn_index, running):
        first_point = turn_index * span_points
        spec_block = lax.dynamic_slice_in_dim(regrouped, first_point, span_points, 2)
        flat_index = first_point + jnp.arange(span_points, dtype=jnp.int32)
        point_list = point_ids(flat_index // local_points, flat_index % local_points)
        dotted = project(facing, positions(point_list))
        return running + apply_green(bin_ids, spec_block, dotted, facing, norm_scale)

    result = lax.fori_loop(
        0, turn_count, add_block, jnp.zeros((share_rows, 2, observer_cells.shape[1]), jnp.float32)
    )
    return result.reshape(1, share_rows, 2, result.shape[-1])


LANES = 128
TURN = 2.0 * math.pi

WIDE_SIN = (6.2831854820251465, -41.34170150756836, 81.60513305664062, -76.70301818847656,
            42.02592849731445, -14.899847030639648, 3.2381374835968018)
WIDE_COS = (1.0, -19.73920440673828, 64.93911743164062, -85.45014190673828,
            60.16762924194336, -25.967599868774414, 6.528658390045166)
NARROW_SIN = (6.2831854820251465, -41.34168243408203, 81.60247802734375, -76.58128356933594,
              39.76072311401367)
NARROW_COS = (1.0, -19.739208221435547, 64.93934631347656, -85.45356750488281,
              60.143951416015625, -24.981836318969727)


def horner(coefficients, z):
    total = jnp.full_like(z, coefficients[-1])
    for value in coefficients[-2::-1]:
        total = total * z + value
    return total


def cos_sin_turns(turns, narrow=False):
    if narrow:
        z = turns * turns
        return horner(NARROW_COS, z), horner(NARROW_SIN, z) * turns
    turns = turns - jnp.floor(turns + 0.5)
    z = turns * turns
    return horner(WIDE_COS, z), horner(WIDE_SIN, z) * turns


def slot_places(point_total):
    ids = np.arange(point_total, dtype=np.int64)
    angle = (ids * 1597 % 8191).astype(np.float64) * (TURN / 8191.0)
    axial = (ids // 128) * 0.5 + (ids * 613 % 127) * (0.37 / 127.0)
    place = np.stack([20.0 * np.cos(angle), 20.0 * np.sin(angle), axial])
    return place * (WAVE_STEP / TURN)


def dft_constant(time_len):
    turns = np.arange(time_len)[:, None] * (np.arange(NF) + 1)[None, :] % time_len
    angle = turns.astype(np.float32) * np.float32(TURN / time_len)
    grid = np.concatenate([np.cos(angle), -np.sin(angle)], axis=1)
    return grid.astype(jnp.bfloat16)


def own_bins(counts_ref, nar_count):
    nar_index = lax.axis_index("nar")
    start = jnp.int32(0)
    for m in range(nar_count - 1):
        start = start + jnp.where(m < nar_index, counts_ref[m], 0)
    return start, counts_ref[nar_index]


def swap_groups(blocks, width):
    blocks = list(blocks)
    amount = len(blocks)
    lanes = amount * width
    group = lax.broadcasted_iota(jnp.int32, blocks[0].shape, 1) // width
    step = 1
    while step < amount:
        high = (group & step) != 0
        for r in range(amount):
            if r & step == 0:
                x, y = blocks[r], blocks[r | step]
                blocks[r] = jnp.where(high, pltpu.roll(y, step * width, 1), x)
                blocks[r | step] = jnp.where(high, y, pltpu.roll(x, lanes - step * width, 1))
        step *= 2
    return blocks


def in_hbm(array):
    return pltpu.with_memory_space_constraint(array, pltpu.HBM)


def fetch_all(pairs, sems):
    copies = [
        pltpu.make_async_copy(source, target, sems.at[i])
        for i, (source, target) in enumerate(pairs)
    ]
    for copy in copies:
        copy.start()
    return copies


def pack_kernel(
    counts_hbm, rows_hbm, series_hbm, table_hbm, out_ref,
    counts_ref, rows_ref, series_ref, table_ref, sems, *, nar_count, width
):
    copies = fetch_all(
        [(rows_hbm, rows_ref), (series_hbm, series_ref), (table_hbm, table_ref), (counts_hbm, counts_ref)],
        sems,
    )
    row_total = series_ref.shape[0]
    slots = rows_ref.shape[2]
    time_len = series_ref.shape[1] // NQ
    row_ids = lax.broadcasted_iota(jnp.int32, (row_total, slots), 0)
    copies[0].wait()
    hot = jnp.where(row_ids == rows_ref[0], 1.0, 0.0).astype(jnp.bfloat16)
    copies[1].wait()
    picked = lax.dot_general(
        hot, series_ref[...], (((0,), (0,)), ((), ())), preferred_element_type=jnp.float32
    ).astype(jnp.bfloat16)
    stacked = jnp.concatenate(
        [picked[:, q * time_len:(q + 1) * time_len] for q in range(NQ)], axis=0
    )
    copies[2].wait()
    spectral = jnp.dot(stacked, table_ref[...], preferred_element_type=jnp.float32)
    spectral = spectral * (1.0 / math.sqrt(time_len))
    copies[3].wait()
    start = jnp.int32(0)
    for m in range(nar_count):
        blocks = []
        for part in range(2):
            half = spectral[:, part * NF:(part + 1) * NF]
            half = pltpu.roll(half, lax.rem(NF - start, NF), 1)[:, :LANES]
            blocks += [half[q * slots:(q + 1) * slots] for q in range(NQ)]
        for v, chunk in enumerate(swap_groups(blocks, width)):
            first = (v * nar_count + m) * slots
            out_ref[first:first + slots, :] = chunk.astype(jnp.bfloat16)
        start = start + counts_ref[m]


def green_kernel(
    counts_hbm, cells_hbm, place_hbm,
    seed_ref, rest_hbm, far_hbm, facing_ref, amplitude_ref,
    counts_ref, cells_ref, place_ref, spread_ref, column_ref, rest_ref, far_ref, sems, far_sem, rest_sem,
    *, nar_count, share, narrow
):
    copies = fetch_all(
        [(counts_hbm, counts_ref), (cells_hbm, cells_ref), (place_hbm, place_ref)], sems
    )
    points = place_ref.shape[1]
    observers = cells_ref.shape[1]
    far = far_ref.shape[0]
    for copy in copies:
        copy.wait()
    start, count = own_bins(counts_ref, nar_count)
    within = lax.axis_index("vol") * share
    base_step = (start + within + 1).astype(jnp.float32)
    within = within + lax.broadcasted_iota(jnp.int32, amplitude_ref.shape, 0)
    amplitude = (start + within + 1).astype(jnp.float32) * (1.0 / (math.sqrt(points) * NF))
    amplitude_ref[...] = jnp.where(within < count, amplitude, 0.0)
    cells = cells_ref[...].astype(jnp.float32)
    cos_polar, sin_polar = cos_sin_turns((cells[0:1] + 0.5) * (1.0 / 256.0))
    cos_azimuth, sin_azimuth = cos_sin_turns(cells[1:2] * (1.0 / 128.0))
    facing = (sin_polar * cos_azimuth, sin_polar * sin_azimuth, cos_polar)
    for axis in range(3):
        facing_ref[axis:axis + 1, :] = facing[axis]
        spread_ref[axis] = jnp.broadcast_to(facing[axis], (8, observers))
    for tile in range(points // LANES):
        column_ref[tile * LANES:(tile + 1) * LANES, :] = (
            place_ref[:, tile * LANES:(tile + 1) * LANES].T
        )
    rows, lanes = 16, 256

    def tile_step(tile, seeds, offset):
        first = pl.multiple_of(tile * rows, rows)
        place = [column_ref[pl.ds(first, rows), axis:axis + 1] for axis in range(3)]
        for lane in range(0, observers, lanes):
            def seen(axis):
                return jnp.concatenate([spread_ref[axis, :, lane:lane + lanes]] * (rows // 8), axis=0)
            turns = seen(0) * place[0] + seen(1) * place[1]
            turns = turns + seen(2) * place[2]
            c_now, s_now = cos_sin_turns(turns * base_step)
            c_one, s_one = cos_sin_turns(turns, narrow)
            twice = c_one + c_one
            c_old = c_now * c_one + s_now * s_one
            s_old = s_now * c_one - c_now * s_one
            for j in range(far):
                far_ref[j, pl.ds(first, rows), lane:lane + lanes] = c_now.astype(jnp.bfloat16)
                far_ref[j, pl.ds(first + points, rows), lane:lane + lanes] = s_now.astype(jnp.bfloat16)
                c_now, c_old = twice * c_now - c_old, c_now
                s_now, s_old = twice * s_now - s_old, s_now
            spot = (pl.ds(first - offset, rows), slice(lane, lane + lanes))
            for k, value in enumerate((c_now, s_now, c_one, s_one)):
                seeds[k, *spot] = value

    step = 64
    lead = seed_ref.shape[1]
    for block in range(0, points, step):
        seeds, offset = (seed_ref, 0) if block < lead else (rest_ref, lead)
        def pair_step(pair, carry):
            for k in range(2):
                tile_step(pair * 2 + k, seeds, offset)
            return carry

        lax.fori_loop(block // rows // 2, (block + step) // rows // 2, pair_step, 0)
        for first in (block, points + block):
            pltpu.make_async_copy(
                far_ref.at[:, first:first + step, :], far_hbm.at[:, first:first + step, :], far_sem
            ).start()
    rest_copy = pltpu.make_async_copy(rest_ref, rest_hbm, rest_sem)
    rest_copy.start()
    pltpu.make_async_copy(far_ref, far_hbm, far_sem).wait()
    rest_copy.wait()


def moment_kernel(
    spectra_ref, seed_ref, rest_hbm, far_hbm, facing_ref, amplitude_ref, out_ref,
    left_ref, moment_ref, rest_ref, made_even, made_odd, far_ref, sems, rest_sem, *, share
):
    far = far_ref.shape[0]
    near = share - far
    lead, observers = seed_ref.shape[1:]
    points = spectra_ref.shape[0]
    half = NQ * share
    tiles = points // LANES

    def far_copy(j):
        return pltpu.make_async_copy(far_hbm.at[j], far_ref.at[j], sems.at[j])

    rest_copy = pltpu.make_async_copy(rest_hbm, rest_ref, rest_sem)
    for j in range(far):
        far_copy(j).start()
        if j == min(1, far - 1):
            rest_copy.start()
    made = (made_even, made_odd)
    rows, lanes = 16, 256

    for tile in range(tiles):
        turned = spectra_ref[tile * LANES:(tile + 1) * LANES, :].astype(jnp.float32).T
        left_ref[tile] = turned
        left_ref[tiles + tile, :half] = turned[half:]
        left_ref[tiles + tile, half:] = -turned[:half]

    def generate(block, part):
        seeds, offset = (seed_ref, block * LANES) if block * LANES < lead else (rest_ref, block * LANES - lead)
        spot = pl.multiple_of(part * rows, rows)
        into = made[block % 2]
        for lane in range(0, observers, lanes):
            c_now, s_now, c_one, s_one = (
                seeds[k, pl.ds(offset + spot, rows), lane:lane + lanes] for k in range(4)
            )
            twice = c_one + c_one
            c_old = c_now * c_one + s_now * s_one
            s_old = s_now * c_one - c_now * s_one
            for j in range(near):
                into[j, pl.ds(spot, rows), lane:lane + lanes] = c_now.astype(jnp.bfloat16)
                into[j, pl.ds(LANES + spot, rows), lane:lane + lanes] = s_now.astype(jnp.bfloat16)
                if j < near - 1:
                    c_now, c_old = twice * c_now - c_old, c_now
                    s_now, s_old = twice * s_now - s_old, s_now

    def multiply(j, which, green, fresh):
        own = pl.ds(j, 2 * NQ, stride=share)
        left = jnp.concatenate([left_ref[tile, own, :] for tile in which], axis=1)
        product = jnp.dot(left.astype(jnp.bfloat16), green, preferred_element_type=jnp.float32)
        spot = pl.ds(pl.multiple_of(2 * NQ * j, 2 * NQ), 2 * NQ)
        for piece in range(observers // LANES):
            value = product[:, piece * LANES:(piece + 1) * LANES]
            moment_ref[piece, spot, :] = value if fresh else moment_ref[piece, spot, :] + value

    parts = LANES // rows
    unroll = 4
    trips = parts // unroll
    streamed = [0 if block < tiles // 2 else 1 for block in range(tiles)]
    fetched = 0
    for block in range(tiles):
        if block * LANES == lead:
            rest_copy.wait()
        base, per_trip = fetched, min(streamed[block], (far - fetched) // trips)
        fetched += per_trip * trips

        def part_step(step, carry):
            if block:
                for j in [step * (near // trips) + k for k in range(near // trips)]:
                    multiply(
                        far + j, (block - 1, tiles + block - 1), made[(block - 1) % 2][j], block == 1
                    )
            for j in [base + step * per_trip + k for k in range(per_trip)]:
                far_copy(j).wait()
                multiply(j, range(2 * tiles), far_ref[j], True)
            for part in [step * unroll + u for u in range(unroll)]:
                generate(block, part)
            return carry

        lax.fori_loop(0, trips, part_step, 0)
    for j in range(near):
        multiply(far + j, (tiles - 1, 2 * tiles - 1), made[(tiles - 1) % 2][j], tiles == 1)
    for j in range(fetched, far):
        far_copy(j).wait()
        multiply(j, range(2 * tiles), far_ref[j], True)

    amplitude = amplitude_ref[...]
    for piece in range(observers // LANES):
        lane = slice(piece * LANES, (piece + 1) * LANES)
        sums = []
        for part in range(2):
            total = None
            for q in range(NQ):
                term = moment_ref[piece, pl.ds(part * NQ + q, share, stride=2 * NQ), :]
                if q:
                    term = term * facing_ref[q - 1:q, lane]
                total = term if total is None else total + term
            sums.append(total)
        out_ref[0, :, 0, lane] = -amplitude * sums[1]
        out_ref[0, :, 1, lane] = amplitude * sums[0]


def per_device(series, send_rows, bin_counts, observer_cells):
    vol_count = lax.axis_size("vol")
    nar_count = lax.axis_size("nar")
    share = max(1, 2 * NF // (nar_count * vol_count))
    slots = send_rows.shape[2]
    points = vol_count * nar_count * slots
    observers = observer_cells.shape[1]
    time_len = series.shape[1] // NQ
    fits = (
        vol_count == 2 * NQ
        and vol_count * share == LANES
        and slots % 16 == 0
        and points % LANES == 0
        and share == 2 * (LANES // 16)
        and observers % 256 == 0
        and share * points * observers <= 8 << 20
    )
    if not fits:
        return per_device_general(series, send_rows, bin_counts, observer_cells)
    vmem = pl.BlockSpec(memory_space=pltpu.VMEM)
    hbm = pl.BlockSpec(memory_space=pltpu.HBM)
    places = slot_places(points)
    reach = float(np.sqrt((places ** 2).sum(axis=0)).max())
    place_rows = np.zeros((8, points), np.float32)
    place_rows[:3] = places
    table = dft_constant(time_len)
    near = share // 2
    counts_scratch = pltpu.SMEM(bin_counts.shape, jnp.int32)

    packed = pl.pallas_call(
        lambda *refs: pack_kernel(*refs, nar_count=nar_count, width=share),
        out_shape=jax.ShapeDtypeStruct((points, LANES), jnp.bfloat16),
        in_specs=[hbm] * 4,
        out_specs=vmem,
        scratch_shapes=[
            counts_scratch,
            pltpu.VMEM(send_rows.shape, jnp.int32),
            pltpu.VMEM(series.shape, series.dtype),
            pltpu.VMEM(table.shape, jnp.bfloat16),
            pltpu.SemaphoreType.DMA((4,)),
        ],
        compiler_params=pltpu.CompilerParams(vmem_limit_bytes=8 << 20),
        name="pack_rows",
    )(*map(in_hbm, (bin_counts, send_rows, series, jnp.asarray(table))))
    spectra = lax.all_to_all(packed, ("vol", "nar"), split_axis=0, concat_axis=0, tiled=True)
    far_shape = (share - near, 2 * points, observers)
    rest_shape = (4, LANES, observers)
    made = pltpu.VMEM((near, 2 * LANES, observers), jnp.bfloat16)
    seeds, rest, far_green, facing, amplitude = pl.pallas_call(
        lambda *refs: green_kernel(
            *refs, nar_count=nar_count, share=share, narrow=reach < 0.249
        ),
        out_shape=(
            jax.ShapeDtypeStruct((4, points - LANES, observers), jnp.float32),
            pltpu.HBM(rest_shape, jnp.float32),
            pltpu.HBM(far_shape, jnp.bfloat16),
            jax.ShapeDtypeStruct((3, observers), jnp.float32),
            jax.ShapeDtypeStruct((share, LANES), jnp.float32),
        ),
        in_specs=[hbm] * 3,
        out_specs=(vmem, hbm, hbm, vmem, vmem),
        scratch_shapes=[
            counts_scratch,
            pltpu.VMEM(observer_cells.shape, jnp.int32),
            pltpu.VMEM(place_rows.shape, jnp.float32),
            pltpu.VMEM((3, 8, observers), jnp.float32),
            pltpu.VMEM((points, 8), jnp.float32),
            pltpu.VMEM(rest_shape, jnp.float32),
            pltpu.VMEM(far_shape, jnp.bfloat16),
            pltpu.SemaphoreType.DMA((3,)),
            pltpu.SemaphoreType.DMA,
            pltpu.SemaphoreType.DMA,
        ],
        compiler_params=pltpu.CompilerParams(vmem_limit_bytes=24 << 20),
        cost_estimate=pl.CostEstimate(
            flops=60 * share * points * observers, bytes_accessed=4 * share * points * observers,
            transcendentals=0,
        ),
        name="green_grid",
    )(*map(in_hbm, (bin_counts, observer_cells, jnp.asarray(place_rows))))
    return pl.pallas_call(
        lambda *refs: moment_kernel(*refs, share=share),
        out_shape=jax.ShapeDtypeStruct((1, share, 2, observers), jnp.float32),
        in_specs=[vmem, vmem, hbm, hbm, vmem, vmem],
        out_specs=vmem,
        scratch_shapes=[
            pltpu.VMEM((2 * points // LANES, LANES, LANES), jnp.float32),
            pltpu.VMEM((observers // LANES, LANES, LANES), jnp.float32),
            pltpu.VMEM(rest_shape, jnp.float32),
            made,
            made,
            pltpu.VMEM(far_shape, jnp.bfloat16),
            pltpu.SemaphoreType.DMA((share - near,)),
            pltpu.SemaphoreType.DMA,
        ],
        compiler_params=pltpu.CompilerParams(
            vmem_limit_bytes=24 << 20
        ),
        name="moments",
    )(spectra, seeds, in_hbm(rest), in_hbm(far_green), facing, amplitude)


def solution(mesh):
    placed = (P(("vol", "nar"), None), P("vol", "nar", None), P(), P())
    return jax.shard_map(
        per_device,
        mesh=mesh,
        in_specs=placed,
        out_specs=P("nar", "vol", None, None),
        check_vma=False,
    )
```

```python
import math

import jax
import jax.numpy as jnp
import numpy as np
from jax import lax
from jax.experimental import pallas as pl
from jax.experimental.pallas import tpu as pltpu
from jax.sharding import PartitionSpec as P

NF = 256
NQ = 4


WAVE_STEP = 0.05


def dft_table(bin_ids, keep_bin, time_len):
    time_steps = jnp.arange(time_len, dtype=jnp.int32)
    frequency = bin_ids + 1
    phase_turns = time_steps[:, None] * frequency[None, :] % time_len
    angle_grid = phase_turns.astype(jnp.float32) * (2.0 * math.pi / time_len)
    dft_grid = jnp.stack([jnp.cos(angle_grid), -jnp.sin(angle_grid)], axis=-1)
    dft_grid = jnp.where(keep_bin[None, :, None], dft_grid, jnp.float32(0.0))
    return dft_grid.reshape(time_len, 2 * bin_ids.shape[0]).astype(jnp.bfloat16)


def positions(point_list):
    beside_all = (point_list * 1597 % 8191).astype(jnp.float32) * (2.0 * math.pi / 8191.0)
    jitter = (point_list * 613 % 127).astype(jnp.float32) * (0.37 / 127.0)
    axial = (point_list // 128).astype(jnp.float32) * 0.5 + jitter
    return (20.0 * jnp.cos(beside_all), 20.0 * jnp.sin(beside_all), axial)


def directions(obs_cells):
    polar_angle = (obs_cells[0].astype(jnp.float32) + 0.5) * (math.pi / 128.0)
    azimuth = obs_cells[1].astype(jnp.float32) * (2.0 * math.pi / 128.0)
    return (
        jnp.sin(polar_angle) * jnp.cos(azimuth),
        jnp.sin(polar_angle) * jnp.sin(azimuth),
        jnp.cos(polar_angle),
    )


def project(facing, place_xyz):
    dotted = facing[0][:, None] * place_xyz[0][None, :] + facing[1][:, None] * place_xyz[1][None, :]
    return dotted + facing[2][:, None] * place_xyz[2][None, :]


def kernels(bin_ids, dotted):
    wavenumber = (bin_ids.astype(jnp.float32) + 1.0) * WAVE_STEP
    phase_grid = wavenumber[:, None, None] * dotted[None]
    return jnp.concatenate([jnp.cos(phase_grid), jnp.sin(phase_grid)], axis=1).astype(jnp.bfloat16)


def combine(products, bin_ids, facing, norm_scale):
    observers = facing[0].shape[0]
    bin_total = bin_ids.shape[0]
    cos_part = products[:, :observers].reshape(bin_total, observers, NQ, 2)
    sine_part = products[:, observers:].reshape(bin_total, observers, NQ, 2)
    real_part = cos_part[..., 0] + sine_part[..., 1]
    imag_part = cos_part[..., 1] - sine_part[..., 0]
    weights = jnp.stack([jnp.ones_like(facing[0]), facing[0], facing[1], facing[2]], axis=-1)
    real_sum = jnp.sum(real_part * weights[None], axis=-1)
    imag_sum = jnp.sum(imag_part * weights[None], axis=-1)
    amplitude = (bin_ids.astype(jnp.float32) + 1.0) * (norm_scale / NF)
    return jnp.stack([-amplitude[:, None] * imag_sum, amplitude[:, None] * real_sum], axis=1)


def apply_green(bin_ids, spec_block, dotted, facing, norm_scale):
    green_grid = kernels(bin_ids, dotted)
    products = jnp.einsum(
        "bxp,bcp->bxc", green_grid, spec_block, preferred_element_type=jnp.float32
    )
    return combine(products, bin_ids, facing, norm_scale)


def per_device_general(series, send_rows, bin_counts, observer_cells):
    vol_count = lax.axis_size("vol")
    nar_count = lax.axis_size("nar")
    vol_index = lax.axis_index("vol")
    nar_index = lax.axis_index("nar")
    bin_cap = vol_count * max(1, 2 * NF // (nar_count * vol_count))
    time_len = series.shape[1] // NQ
    slot_total = send_rows.shape[2]
    slot_width = slot_total // vol_count
    listing = send_rows.reshape(-1)
    picked = jnp.take(series, jnp.maximum(listing, 0), axis=0)
    packed = jnp.where((listing >= 0)[:, None], picked, jnp.zeros((), series.dtype))
    arrived = lax.all_to_all(packed, "vol", split_axis=0, concat_axis=0, tiled=True)
    starts = jnp.cumsum(bin_counts) - bin_counts
    own_start = starts[nar_index]
    own_count = bin_counts[nar_index]
    dft_scale = 1.0 / math.sqrt(time_len)
    within = jnp.arange(bin_cap, dtype=jnp.int32)
    own_table = dft_table(own_start + within, within < own_count, time_len)
    row_piece = lax.all_gather(arrived, "nar", axis=0, tiled=True)
    rows_here = row_piece.shape[0]
    spectral = jnp.dot(
        row_piece.reshape(rows_here * NQ, time_len), own_table, preferred_element_type=jnp.float32
    )
    spectral = (spectral * dft_scale).astype(jnp.bfloat16).reshape(rows_here, NQ, bin_cap, 2)
    spectra = spectral.transpose(2, 1, 3, 0).reshape(bin_cap, 2 * NQ, rows_here)
    local_points = nar_count * slot_total

    def point_ids(vol_owner, flat_index):
        nar_source = flat_index // slot_total
        remain = flat_index % slot_total
        vol_source = remain // slot_width
        within_slot = remain % slot_width
        return (
            (vol_source * nar_count + nar_source) * vol_count + vol_owner
        ) * slot_width + within_slot

    norm_scale = 1.0 / math.sqrt(vol_count * nar_count * slot_total)
    facing = directions(observer_cells)
    share_rows = bin_cap // vol_count
    regrouped = lax.all_to_all(spectra, "vol", split_axis=0, concat_axis=2, tiled=True)
    bin_ids = own_start + vol_index * share_rows + jnp.arange(share_rows, dtype=jnp.int32)
    span_points = local_points * max(1, vol_count // 8)
    turn_count = vol_count * local_points // span_points

    def add_block(turn_index, running):
        first_point = turn_index * span_points
        spec_block = lax.dynamic_slice_in_dim(regrouped, first_point, span_points, 2)
        flat_index = first_point + jnp.arange(span_points, dtype=jnp.int32)
        point_list = point_ids(flat_index // local_points, flat_index % local_points)
        dotted = project(facing, positions(point_list))
        return running + apply_green(bin_ids, spec_block, dotted, facing, norm_scale)

    result = lax.fori_loop(
        0, turn_count, add_block, jnp.zeros((share_rows, 2, observer_cells.shape[1]), jnp.float32)
    )
    return result.reshape(1, share_rows, 2, result.shape[-1])


LANES = 128
TURN = 2.0 * math.pi

WIDE_SIN = (6.2831854820251465, -41.34170150756836, 81.60513305664062, -76.70301818847656,
            42.02592849731445, -14.899847030639648, 3.2381374835968018)
WIDE_COS = (1.0, -19.73920440673828, 64.93911743164062, -85.45014190673828,
            60.16762924194336, -25.967599868774414, 6.528658390045166)
NARROW_SIN = (6.2831854820251465, -41.34168243408203, 81.60247802734375, -76.58128356933594,
              39.76072311401367)
NARROW_COS = (1.0, -19.739208221435547, 64.93934631347656, -85.45356750488281,
              60.143951416015625, -24.981836318969727)


def horner(coefficients, z):
    total = jnp.full_like(z, coefficients[-1])
    for value in coefficients[-2::-1]:
        total = total * z + value
    return total


def cos_sin_turns(turns, narrow=False):
    if narrow:
        z = turns * turns
        return horner(NARROW_COS, z), horner(NARROW_SIN, z) * turns
    turns = turns - jnp.floor(turns + 0.5)
    z = turns * turns
    return horner(WIDE_COS, z), horner(WIDE_SIN, z) * turns


def slot_places(point_total):
    ids = np.arange(point_total, dtype=np.int64)
    angle = (ids * 1597 % 8191).astype(np.float64) * (TURN / 8191.0)
    axial = (ids // 128) * 0.5 + (ids * 613 % 127) * (0.37 / 127.0)
    place = np.stack([20.0 * np.cos(angle), 20.0 * np.sin(angle), axial])
    return place * (WAVE_STEP / TURN)


def dft_constant(time_len):
    turns = np.arange(time_len)[:, None] * (np.arange(NF) + 1)[None, :] % time_len
    angle = turns.astype(np.float32) * np.float32(TURN / time_len)
    grid = np.concatenate([np.cos(angle), -np.sin(angle)], axis=1)
    return grid.astype(jnp.bfloat16)


def own_bins(counts_ref, nar_count):
    nar_index = lax.axis_index("nar")
    start = jnp.int32(0)
    for m in range(nar_count - 1):
        start = start + jnp.where(m < nar_index, counts_ref[m], 0)
    return start, counts_ref[nar_index]


def swap_groups(blocks, width):
    blocks = list(blocks)
    amount = len(blocks)
    lanes = amount * width
    group = lax.broadcasted_iota(jnp.int32, blocks[0].shape, 1) // width
    step = 1
    while step < amount:
        high = (group & step) != 0
        for r in range(amount):
            if r & step == 0:
                x, y = blocks[r], blocks[r | step]
                blocks[r] = jnp.where(high, pltpu.roll(y, step * width, 1), x)
                blocks[r | step] = jnp.where(high, y, pltpu.roll(x, lanes - step * width, 1))
        step *= 2
    return blocks


def in_hbm(array):
    return pltpu.with_memory_space_constraint(array, pltpu.HBM)


def fetch_all(pairs, sems):
    copies = [
        pltpu.make_async_copy(source, target, sems.at[i])
        for i, (source, target) in enumerate(pairs)
    ]
    for copy in copies:
        copy.start()
    return copies


def pack_kernel(
    counts_hbm, rows_hbm, series_hbm, table_hbm, out_ref,
    counts_ref, rows_ref, series_ref, table_ref, sems, *, nar_count, width
):
    copies = fetch_all(
        [(rows_hbm, rows_ref), (series_hbm, series_ref), (table_hbm, table_ref), (counts_hbm, counts_ref)],
        sems,
    )
    row_total = series_ref.shape[0]
    slots = rows_ref.shape[2]
    time_len = series_ref.shape[1] // NQ
    row_ids = lax.broadcasted_iota(jnp.int32, (row_total, slots), 0)
    copies[0].wait()
    hot = jnp.where(row_ids == rows_ref[0], 1.0, 0.0).astype(jnp.bfloat16)
    copies[1].wait()
    picked = lax.dot_general(
        hot, series_ref[...], (((0,), (0,)), ((), ())), preferred_element_type=jnp.float32
    ).astype(jnp.bfloat16)
    stacked = jnp.concatenate(
        [picked[:, q * time_len:(q + 1) * time_len] for q in range(NQ)], axis=0
    )
    copies[2].wait()
    spectral = jnp.dot(stacked, table_ref[...], preferred_element_type=jnp.float32)
    spectral = spectral * (1.0 / math.sqrt(time_len))
    copies[3].wait()
    start = jnp.int32(0)
    for m in range(nar_count):
        blocks = []
        for part in range(2):
            half = spectral[:, part * NF:(part + 1) * NF]
            half = pltpu.roll(half, lax.rem(NF - start, NF), 1)[:, :LANES]
            blocks += [half[q * slots:(q + 1) * slots] for q in range(NQ)]
        for v, chunk in enumerate(swap_groups(blocks, width)):
            first = (v * nar_count + m) * slots
            out_ref[first:first + slots, :] = chunk.astype(jnp.bfloat16)
        start = start + counts_ref[m]


def green_kernel(
    counts_hbm, cells_hbm, place_hbm,
    seed_ref, rest_hbm, far_hbm, facing_ref, amplitude_ref,
    counts_ref, cells_ref, place_ref, spread_ref, column_ref, rest_ref, far_ref, sems, far_sem, rest_sem,
    *, nar_count, share, narrow
):
    copies = fetch_all(
        [(counts_hbm, counts_ref), (cells_hbm, cells_ref), (place_hbm, place_ref)], sems
    )
    points = place_ref.shape[1]
    observers = cells_ref.shape[1]
    far = far_ref.shape[0]
    for copy in copies:
        copy.wait()
    start, count = own_bins(counts_ref, nar_count)
    within = lax.axis_index("vol") * share
    base_step = (start + within + 1).astype(jnp.float32)
    within = within + lax.broadcasted_iota(jnp.int32, amplitude_ref.shape, 0)
    amplitude = (start + within + 1).astype(jnp.float32) * (1.0 / (math.sqrt(points) * NF))
    amplitude_ref[...] = jnp.where(within < count, amplitude, 0.0)
    cells = cells_ref[...].astype(jnp.float32)
    cos_polar, sin_polar = cos_sin_turns((cells[0:1] + 0.5) * (1.0 / 256.0))
    cos_azimuth, sin_azimuth = cos_sin_turns(cells[1:2] * (1.0 / 128.0))
    facing = (sin_polar * cos_azimuth, sin_polar * sin_azimuth, cos_polar)
    for axis in range(3):
        facing_ref[axis:axis + 1, :] = facing[axis]
        spread_ref[axis] = jnp.broadcast_to(facing[axis], (8, observers))
    for tile in range(points // LANES):
        column_ref[tile * LANES:(tile + 1) * LANES, :] = (
            place_ref[:, tile * LANES:(tile + 1) * LANES].T
        )
    rows, lanes = 16, 256

    def tile_step(tile, seeds, offset):
        first = pl.multiple_of(tile * rows, rows)
        place = [column_ref[pl.ds(first, rows), axis:axis + 1] for axis in range(3)]
        for lane in range(0, observers, lanes):
            def seen(axis):
                return jnp.concatenate([spread_ref[axis, :, lane:lane + lanes]] * (rows // 8), axis=0)
            turns = seen(0) * place[0] + seen(1) * place[1]
            turns = turns + seen(2) * place[2]
            c_now, s_now = cos_sin_turns(turns * base_step)
            c_one, s_one = cos_sin_turns(turns, narrow)
            twice = c_one + c_one
            c_old = c_now * c_one + s_now * s_one
            s_old = s_now * c_one - c_now * s_one
            for j in range(far):
                far_ref[j, pl.ds(first, rows), lane:lane + lanes] = c_now.astype(jnp.bfloat16)
                far_ref[j, pl.ds(first + points, rows), lane:lane + lanes] = s_now.astype(jnp.bfloat16)
                c_now, c_old = twice * c_now - c_old, c_now
                s_now, s_old = twice * s_now - s_old, s_now
            spot = (pl.ds(first - offset, rows), slice(lane, lane + lanes))
            for k, value in enumerate((c_now, s_now, c_one, s_one)):
                seeds[k, *spot] = value

    step = 64
    lead = seed_ref.shape[1]
    for block in range(0, points, step):
        seeds, offset = (seed_ref, 0) if block < lead else (rest_ref, lead)
        def pair_step(pair, carry):
            for k in range(2):
                tile_step(pair * 2 + k, seeds, offset)
            return carry

        lax.fori_loop(block // rows // 2, (block + step) // rows // 2, pair_step, 0)
        for first in (block, points + block):
            pltpu.make_async_copy(
                far_ref.at[:, first:first + step, :], far_hbm.at[:, first:first + step, :], far_sem
            ).start()
    rest_copy = pltpu.make_async_copy(rest_ref, rest_hbm, rest_sem)
    rest_copy.start()
    pltpu.make_async_copy(far_ref, far_hbm, far_sem).wait()
    rest_copy.wait()


def moment_kernel(
    spectra_ref, seed_ref, rest_hbm, far_hbm, facing_ref, amplitude_ref, out_ref,
    left_ref, moment_ref, rest_ref, made_even, made_odd, far_ref, sems, rest_sem, *, share
):
    far = far_ref.shape[0]
    near = share - far
    lead, observers = seed_ref.shape[1:]
    points = spectra_ref.shape[0]
    half = NQ * share
    tiles = points // LANES

    def far_copy(j):
        return pltpu.make_async_copy(far_hbm.at[j], far_ref.at[j], sems.at[j])

    rest_copy = pltpu.make_async_copy(rest_hbm, rest_ref, rest_sem)
    for j in range(far):
        far_copy(j).start()
        if j == min(1, far - 1):
            rest_copy.start()
    made = (made_even, made_odd)
    rows, lanes = 16, 128

    for tile in range(tiles):
        turned = spectra_ref[tile * LANES:(tile + 1) * LANES, :].astype(jnp.float32).T
        left_ref[tile] = turned
        left_ref[tiles + tile, :half] = turned[half:]
        left_ref[tiles + tile, half:] = -turned[:half]

    def generate(block, part):
        seeds, offset = (seed_ref, block * LANES) if block * LANES < lead else (rest_ref, block * LANES - lead)
        spot = pl.multiple_of(part * rows, rows)
        into = made[block % 2]
        for lane in range(0, observers, lanes):
            c_now, s_now, c_one, s_one = (
                seeds[k, pl.ds(offset + spot, rows), lane:lane + lanes] for k in range(4)
            )
            twice = c_one + c_one
            c_old = c_now * c_one + s_now * s_one
            s_old = s_now * c_one - c_now * s_one
            for j in range(near):
                into[j, pl.ds(spot, rows), lane:lane + lanes] = c_now.astype(jnp.bfloat16)
                into[j, pl.ds(LANES + spot, rows), lane:lane + lanes] = s_now.astype(jnp.bfloat16)
                if j < near - 1:
                    c_now, c_old = twice * c_now - c_old, c_now
                    s_now, s_old = twice * s_now - s_old, s_now

    def multiply(j, which, green, fresh):
        own = pl.ds(j, 2 * NQ, stride=share)
        left = jnp.concatenate([left_ref[tile, own, :] for tile in which], axis=1)
        product = jnp.dot(left.astype(jnp.bfloat16), green, preferred_element_type=jnp.float32)
        spot = pl.ds(pl.multiple_of(2 * NQ * j, 2 * NQ), 2 * NQ)
        for piece in range(observers // LANES):
            value = product[:, piece * LANES:(piece + 1) * LANES]
            moment_ref[piece, spot, :] = value if fresh else moment_ref[piece, spot, :] + value

    parts = LANES // rows
    unroll = 4
    trips = parts // unroll
    for block in range(tiles):
        if block * LANES == lead:
            rest_copy.wait()

        def part_step(step, carry):
            if block:
                for j in [step * (near // trips) + k for k in range(near // trips)]:
                    multiply(
                        far + j, (block - 1, tiles + block - 1), made[(block - 1) % 2][j], block == 1
                    )
            for part in [step * unroll + u for u in range(unroll)]:
                generate(block, part)
            return carry

        lax.fori_loop(0, trips, part_step, 0)
    for j in range(far // 2):
        far_copy(j).wait()
    for j in range(near):
        multiply(far + j, (tiles - 1, 2 * tiles - 1), made[(tiles - 1) % 2][j], tiles == 1)
    for j in range(far // 2):
        multiply(j, range(2 * tiles), far_ref[j], True)
    for j in range(far // 2, far):
        far_copy(j).wait()
    for j in range(far // 2, far):
        multiply(j, range(2 * tiles), far_ref[j], True)

    amplitude = amplitude_ref[...]
    for piece in range(observers // LANES):
        lane = slice(piece * LANES, (piece + 1) * LANES)
        sums = []
        for part in range(2):
            total = None
            for q in range(NQ):
                term = moment_ref[piece, pl.ds(part * NQ + q, share, stride=2 * NQ), :]
                if q:
                    term = term * facing_ref[q - 1:q, lane]
                total = term if total is None else total + term
            sums.append(total)
        out_ref[0, :, 0, lane] = -amplitude * sums[1]
        out_ref[0, :, 1, lane] = amplitude * sums[0]


def per_device(series, send_rows, bin_counts, observer_cells):
    vol_count = lax.axis_size("vol")
    nar_count = lax.axis_size("nar")
    share = max(1, 2 * NF // (nar_count * vol_count))
    slots = send_rows.shape[2]
    points = vol_count * nar_count * slots
    observers = observer_cells.shape[1]
    time_len = series.shape[1] // NQ
    fits = (
        vol_count == 2 * NQ
        and vol_count * share == LANES
        and slots % 16 == 0
        and points % LANES == 0
        and share == 2 * (LANES // 16)
        and observers % 256 == 0
        and share * points * observers <= 8 << 20
    )
    if not fits:
        return per_device_general(series, send_rows, bin_counts, observer_cells)
    vmem = pl.BlockSpec(memory_space=pltpu.VMEM)
    hbm = pl.BlockSpec(memory_space=pltpu.HBM)
    places = slot_places(points)
    reach = float(np.sqrt((places ** 2).sum(axis=0)).max())
    place_rows = np.zeros((8, points), np.float32)
    place_rows[:3] = places
    table = dft_constant(time_len)
    near = 5 * share // 8
    counts_scratch = pltpu.SMEM(bin_counts.shape, jnp.int32)

    packed = pl.pallas_call(
        lambda *refs: pack_kernel(*refs, nar_count=nar_count, width=share),
        out_shape=jax.ShapeDtypeStruct((points, LANES), jnp.bfloat16),
        in_specs=[hbm] * 4,
        out_specs=vmem,
        scratch_shapes=[
            counts_scratch,
            pltpu.VMEM(send_rows.shape, jnp.int32),
            pltpu.VMEM(series.shape, series.dtype),
            pltpu.VMEM(table.shape, jnp.bfloat16),
            pltpu.SemaphoreType.DMA((4,)),
        ],
        compiler_params=pltpu.CompilerParams(vmem_limit_bytes=8 << 20),
        name="pack_rows",
    )(*map(in_hbm, (bin_counts, send_rows, series, jnp.asarray(table))))
    spectra = lax.all_to_all(packed, ("vol", "nar"), split_axis=0, concat_axis=0, tiled=True)
    far_shape = (share - near, 2 * points, observers)
    rest_shape = (4, LANES, observers)
    made = pltpu.VMEM((near, 2 * LANES, observers), jnp.bfloat16)
    seeds, rest, far_green, facing, amplitude = pl.pallas_call(
        lambda *refs: green_kernel(
            *refs, nar_count=nar_count, share=share, narrow=reach < 0.249
        ),
        out_shape=(
            jax.ShapeDtypeStruct((4, points - LANES, observers), jnp.float32),
            pltpu.HBM(rest_shape, jnp.float32),
            pltpu.HBM(far_shape, jnp.bfloat16),
            jax.ShapeDtypeStruct((3, observers), jnp.float32),
            jax.ShapeDtypeStruct((share, LANES), jnp.float32),
        ),
        in_specs=[hbm] * 3,
        out_specs=(vmem, hbm, hbm, vmem, vmem),
        scratch_shapes=[
            counts_scratch,
            pltpu.VMEM(observer_cells.shape, jnp.int32),
            pltpu.VMEM(place_rows.shape, jnp.float32),
            pltpu.VMEM((3, 8, observers), jnp.float32),
            pltpu.VMEM((points, 8), jnp.float32),
            pltpu.VMEM(rest_shape, jnp.float32),
            pltpu.VMEM(far_shape, jnp.bfloat16),
            pltpu.SemaphoreType.DMA((3,)),
            pltpu.SemaphoreType.DMA,
            pltpu.SemaphoreType.DMA,
        ],
        compiler_params=pltpu.CompilerParams(vmem_limit_bytes=24 << 20),
        cost_estimate=pl.CostEstimate(
            flops=60 * share * points * observers, bytes_accessed=4 * share * points * observers,
            transcendentals=0,
        ),
        name="green_grid",
    )(*map(in_hbm, (bin_counts, observer_cells, jnp.asarray(place_rows))))
    return pl.pallas_call(
        lambda *refs: moment_kernel(*refs, share=share),
        out_shape=jax.ShapeDtypeStruct((1, share, 2, observers), jnp.float32),
        in_specs=[vmem, vmem, hbm, hbm, vmem, vmem],
        out_specs=vmem,
        scratch_shapes=[
            pltpu.VMEM((2 * points // LANES, LANES, LANES), jnp.float32),
            pltpu.VMEM((observers // LANES, LANES, LANES), jnp.float32),
            pltpu.VMEM(rest_shape, jnp.float32),
            made,
            made,
            pltpu.VMEM(far_shape, jnp.bfloat16),
            pltpu.SemaphoreType.DMA((share - near,)),
            pltpu.SemaphoreType.DMA,
        ],
        compiler_params=pltpu.CompilerParams(
            vmem_limit_bytes=24 << 20
        ),
        name="moments",
    )(spectra, seeds, in_hbm(rest), in_hbm(far_green), facing, amplitude)


def solution(mesh):
    placed = (P(("vol", "nar"), None), P("vol", "nar", None), P(), P())
    return jax.shard_map(
        per_device,
        mesh=mesh,
        in_specs=placed,
        out_specs=P("nar", "vol", None, None),
        check_vma=False,
    )
```

```python
import math

import jax
import jax.numpy as jnp
import numpy as np
from jax import lax
from jax.experimental import pallas as pl
from jax.experimental.pallas import tpu as pltpu
from jax.sharding import PartitionSpec as P

NF = 256
NQ = 4


WAVE_STEP = 0.05


def dft_table(bin_ids, keep_bin, time_len):
    time_steps = jnp.arange(time_len, dtype=jnp.int32)
    frequency = bin_ids + 1
    phase_turns = time_steps[:, None] * frequency[None, :] % time_len
    angle_grid = phase_turns.astype(jnp.float32) * (2.0 * math.pi / time_len)
    dft_grid = jnp.stack([jnp.cos(angle_grid), -jnp.sin(angle_grid)], axis=-1)
    dft_grid = jnp.where(keep_bin[None, :, None], dft_grid, jnp.float32(0.0))
    return dft_grid.reshape(time_len, 2 * bin_ids.shape[0]).astype(jnp.bfloat16)


def positions(point_list):
    beside_all = (point_list * 1597 % 8191).astype(jnp.float32) * (2.0 * math.pi / 8191.0)
    jitter = (point_list * 613 % 127).astype(jnp.float32) * (0.37 / 127.0)
    axial = (point_list // 128).astype(jnp.float32) * 0.5 + jitter
    return (20.0 * jnp.cos(beside_all), 20.0 * jnp.sin(beside_all), axial)


def directions(obs_cells):
    polar_angle = (obs_cells[0].astype(jnp.float32) + 0.5) * (math.pi / 128.0)
    azimuth = obs_cells[1].astype(jnp.float32) * (2.0 * math.pi / 128.0)
    return (
        jnp.sin(polar_angle) * jnp.cos(azimuth),
        jnp.sin(polar_angle) * jnp.sin(azimuth),
        jnp.cos(polar_angle),
    )


def project(facing, place_xyz):
    dotted = facing[0][:, None] * place_xyz[0][None, :] + facing[1][:, None] * place_xyz[1][None, :]
    return dotted + facing[2][:, None] * place_xyz[2][None, :]


def kernels(bin_ids, dotted):
    wavenumber = (bin_ids.astype(jnp.float32) + 1.0) * WAVE_STEP
    phase_grid = wavenumber[:, None, None] * dotted[None]
    return jnp.concatenate([jnp.cos(phase_grid), jnp.sin(phase_grid)], axis=1).astype(jnp.bfloat16)


def combine(products, bin_ids, facing, norm_scale):
    observers = facing[0].shape[0]
    bin_total = bin_ids.shape[0]
    cos_part = products[:, :observers].reshape(bin_total, observers, NQ, 2)
    sine_part = products[:, observers:].reshape(bin_total, observers, NQ, 2)
    real_part = cos_part[..., 0] + sine_part[..., 1]
    imag_part = cos_part[..., 1] - sine_part[..., 0]
    weights = jnp.stack([jnp.ones_like(facing[0]), facing[0], facing[1], facing[2]], axis=-1)
    real_sum = jnp.sum(real_part * weights[None], axis=-1)
    imag_sum = jnp.sum(imag_part * weights[None], axis=-1)
    amplitude = (bin_ids.astype(jnp.float32) + 1.0) * (norm_scale / NF)
    return jnp.stack([-amplitude[:, None] * imag_sum, amplitude[:, None] * real_sum], axis=1)


def apply_green(bin_ids, spec_block, dotted, facing, norm_scale):
    green_grid = kernels(bin_ids, dotted)
    products = jnp.einsum(
        "bxp,bcp->bxc", green_grid, spec_block, preferred_element_type=jnp.float32
    )
    return combine(products, bin_ids, facing, norm_scale)


def per_device_general(series, send_rows, bin_counts, observer_cells):
    vol_count = lax.axis_size("vol")
    nar_count = lax.axis_size("nar")
    vol_index = lax.axis_index("vol")
    nar_index = lax.axis_index("nar")
    bin_cap = vol_count * max(1, 2 * NF // (nar_count * vol_count))
    time_len = series.shape[1] // NQ
    slot_total = send_rows.shape[2]
    slot_width = slot_total // vol_count
    listing = send_rows.reshape(-1)
    picked = jnp.take(series, jnp.maximum(listing, 0), axis=0)
    packed = jnp.where((listing >= 0)[:, None], picked, jnp.zeros((), series.dtype))
    arrived = lax.all_to_all(packed, "vol", split_axis=0, concat_axis=0, tiled=True)
    starts = jnp.cumsum(bin_counts) - bin_counts
    own_start = starts[nar_index]
    own_count = bin_counts[nar_index]
    dft_scale = 1.0 / math.sqrt(time_len)
    within = jnp.arange(bin_cap, dtype=jnp.int32)
    own_table = dft_table(own_start + within, within < own_count, time_len)
    row_piece = lax.all_gather(arrived, "nar", axis=0, tiled=True)
    rows_here = row_piece.shape[0]
    spectral = jnp.dot(
        row_piece.reshape(rows_here * NQ, time_len), own_table, preferred_element_type=jnp.float32
    )
    spectral = (spectral * dft_scale).astype(jnp.bfloat16).reshape(rows_here, NQ, bin_cap, 2)
    spectra = spectral.transpose(2, 1, 3, 0).reshape(bin_cap, 2 * NQ, rows_here)
    local_points = nar_count * slot_total

    def point_ids(vol_owner, flat_index):
        nar_source = flat_index // slot_total
        remain = flat_index % slot_total
        vol_source = remain // slot_width
        within_slot = remain % slot_width
        return (
            (vol_source * nar_count + nar_source) * vol_count + vol_owner
        ) * slot_width + within_slot

    norm_scale = 1.0 / math.sqrt(vol_count * nar_count * slot_total)
    facing = directions(observer_cells)
    share_rows = bin_cap // vol_count
    regrouped = lax.all_to_all(spectra, "vol", split_axis=0, concat_axis=2, tiled=True)
    bin_ids = own_start + vol_index * share_rows + jnp.arange(share_rows, dtype=jnp.int32)
    span_points = local_points * max(1, vol_count // 8)
    turn_count = vol_count * local_points // span_points

    def add_block(turn_index, running):
        first_point = turn_index * span_points
        spec_block = lax.dynamic_slice_in_dim(regrouped, first_point, span_points, 2)
        flat_index = first_point + jnp.arange(span_points, dtype=jnp.int32)
        point_list = point_ids(flat_index // local_points, flat_index % local_points)
        dotted = project(facing, positions(point_list))
        return running + apply_green(bin_ids, spec_block, dotted, facing, norm_scale)

    result = lax.fori_loop(
        0, turn_count, add_block, jnp.zeros((share_rows, 2, observer_cells.shape[1]), jnp.float32)
    )
    return result.reshape(1, share_rows, 2, result.shape[-1])


LANES = 128
TURN = 2.0 * math.pi

WIDE_SIN = (6.2831854820251465, -41.34170150756836, 81.60513305664062, -76.70301818847656,
            42.02592849731445, -14.899847030639648, 3.2381374835968018)
WIDE_COS = (1.0, -19.73920440673828, 64.93911743164062, -85.45014190673828,
            60.16762924194336, -25.967599868774414, 6.528658390045166)
NARROW_SIN = (6.2831854820251465, -41.34168243408203, 81.60247802734375, -76.58128356933594,
              39.76072311401367)
NARROW_COS = (1.0, -19.739208221435547, 64.93934631347656, -85.45356750488281,
              60.143951416015625, -24.981836318969727)


def horner(coefficients, z):
    total = jnp.full_like(z, coefficients[-1])
    for value in coefficients[-2::-1]:
        total = total * z + value
    return total


def cos_sin_turns(turns, narrow=False):
    if narrow:
        z = turns * turns
        return horner(NARROW_COS, z), horner(NARROW_SIN, z) * turns
    turns = turns - jnp.floor(turns + 0.5)
    z = turns * turns
    return horner(WIDE_COS, z), horner(WIDE_SIN, z) * turns


def slot_places(point_total):
    ids = np.arange(point_total, dtype=np.int64)
    angle = (ids * 1597 % 8191).astype(np.float64) * (TURN / 8191.0)
    axial = (ids // 128) * 0.5 + (ids * 613 % 127) * (0.37 / 127.0)
    place = np.stack([20.0 * np.cos(angle), 20.0 * np.sin(angle), axial])
    return place * (WAVE_STEP / TURN)


def dft_constant(time_len):
    turns = np.arange(time_len)[:, None] * (np.arange(NF) + 1)[None, :] % time_len
    angle = turns.astype(np.float32) * np.float32(TURN / time_len)
    grid = np.concatenate([np.cos(angle), -np.sin(angle)], axis=1)
    return grid.astype(jnp.bfloat16)


def own_bins(counts_ref, nar_count):
    nar_index = lax.axis_index("nar")
    start = jnp.int32(0)
    for m in range(nar_count - 1):
        start = start + jnp.where(m < nar_index, counts_ref[m], 0)
    return start, counts_ref[nar_index]


def swap_groups(blocks, width):
    blocks = list(blocks)
    amount = len(blocks)
    lanes = amount * width
    group = lax.broadcasted_iota(jnp.int32, blocks[0].shape, 1) // width
    step = 1
    while step < amount:
        high = (group & step) != 0
        for r in range(amount):
            if r & step == 0:
                x, y = blocks[r], blocks[r | step]
                blocks[r] = jnp.where(high, pltpu.roll(y, step * width, 1), x)
                blocks[r | step] = jnp.where(high, y, pltpu.roll(x, lanes - step * width, 1))
        step *= 2
    return blocks


def in_hbm(array):
    return pltpu.with_memory_space_constraint(array, pltpu.HBM)


def fetch_all(pairs, sems):
    copies = [
        pltpu.make_async_copy(source, target, sems.at[i])
        for i, (source, target) in enumerate(pairs)
    ]
    for copy in copies:
        copy.start()
    return copies


def pack_kernel(
    counts_hbm, rows_hbm, series_hbm, table_hbm, out_ref,
    counts_ref, rows_ref, series_ref, table_ref, sems, *, nar_count, width
):
    copies = fetch_all(
        [(rows_hbm, rows_ref), (series_hbm, series_ref), (table_hbm, table_ref), (counts_hbm, counts_ref)],
        sems,
    )
    row_total = series_ref.shape[0]
    slots = rows_ref.shape[2]
    time_len = series_ref.shape[1] // NQ
    row_ids = lax.broadcasted_iota(jnp.int32, (row_total, slots), 0)
    copies[0].wait()
    hot = jnp.where(row_ids == rows_ref[0], 1.0, 0.0).astype(jnp.bfloat16)
    copies[1].wait()
    picked = lax.dot_general(
        hot, series_ref[...], (((0,), (0,)), ((), ())), preferred_element_type=jnp.float32
    ).astype(jnp.bfloat16)
    stacked = jnp.concatenate(
        [picked[:, q * time_len:(q + 1) * time_len] for q in range(NQ)], axis=0
    )
    copies[2].wait()
    spectral = jnp.dot(stacked, table_ref[...], preferred_element_type=jnp.float32)
    spectral = spectral * (1.0 / math.sqrt(time_len))
    copies[3].wait()
    start = jnp.int32(0)
    for m in range(nar_count):
        blocks = []
        for part in range(2):
            half = spectral[:, part * NF:(part + 1) * NF]
            half = pltpu.roll(half, lax.rem(NF - start, NF), 1)[:, :LANES]
            blocks += [half[q * slots:(q + 1) * slots] for q in range(NQ)]
        for v, chunk in enumerate(swap_groups(blocks, width)):
            first = (v * nar_count + m) * slots
            out_ref[first:first + slots, :] = chunk.astype(jnp.bfloat16)
        start = start + counts_ref[m]


def green_kernel(
    counts_hbm, cells_hbm, place_hbm,
    seed_ref, rest_hbm, far_hbm, facing_ref, amplitude_ref,
    counts_ref, cells_ref, place_ref, spread_ref, column_ref, rest_ref, far_ref, sems, far_sem, rest_sem,
    *, nar_count, share, narrow
):
    copies = fetch_all(
        [(counts_hbm, counts_ref), (cells_hbm, cells_ref), (place_hbm, place_ref)], sems
    )
    points = place_ref.shape[1]
    observers = cells_ref.shape[1]
    far = far_ref.shape[0]
    for copy in copies:
        copy.wait()
    start, count = own_bins(counts_ref, nar_count)
    within = lax.axis_index("vol") * share
    base_step = (start + within + 1).astype(jnp.float32)
    within = within + lax.broadcasted_iota(jnp.int32, amplitude_ref.shape, 0)
    amplitude = (start + within + 1).astype(jnp.float32) * (1.0 / (math.sqrt(points) * NF))
    amplitude_ref[...] = jnp.where(within < count, amplitude, 0.0)
    cells = cells_ref[...].astype(jnp.float32)
    cos_polar, sin_polar = cos_sin_turns((cells[0:1] + 0.5) * (1.0 / 256.0))
    cos_azimuth, sin_azimuth = cos_sin_turns(cells[1:2] * (1.0 / 128.0))
    facing = (sin_polar * cos_azimuth, sin_polar * sin_azimuth, cos_polar)
    for axis in range(3):
        facing_ref[axis:axis + 1, :] = facing[axis]
        spread_ref[axis] = jnp.broadcast_to(facing[axis], (8, observers))
    for tile in range(points // LANES):
        column_ref[tile * LANES:(tile + 1) * LANES, :] = (
            place_ref[:, tile * LANES:(tile + 1) * LANES].T
        )
    rows, lanes = 16, 256

    def tile_step(tile, seeds, offset):
        first = pl.multiple_of(tile * rows, rows)
        place = [column_ref[pl.ds(first, rows), axis:axis + 1] for axis in range(3)]
        for lane in range(0, observers, lanes):
            def seen(axis):
                return jnp.concatenate([spread_ref[axis, :, lane:lane + lanes]] * (rows // 8), axis=0)
            turns = seen(0) * place[0] + seen(1) * place[1]
            turns = turns + seen(2) * place[2]
            c_now, s_now = cos_sin_turns(turns * base_step)
            c_one, s_one = cos_sin_turns(turns, narrow)
            twice = c_one + c_one
            c_old = c_now * c_one + s_now * s_one
            s_old = s_now * c_one - c_now * s_one
            for j in range(far):
                far_ref[j, pl.ds(first, rows), lane:lane + lanes] = c_now.astype(jnp.bfloat16)
                far_ref[j, pl.ds(first + points, rows), lane:lane + lanes] = s_now.astype(jnp.bfloat16)
                c_now, c_old = twice * c_now - c_old, c_now
                s_now, s_old = twice * s_now - s_old, s_now
            spot = (pl.ds(first - offset, rows), slice(lane, lane + lanes))
            for k, value in enumerate((c_now, s_now, c_one, s_one)):
                seeds[k, *spot] = value

    step = 64
    lead = seed_ref.shape[1]
    for block in range(0, points, step):
        seeds, offset = (seed_ref, 0) if block < lead else (rest_ref, lead)
        def pair_step(pair, carry):
            for k in range(2):
                tile_step(pair * 2 + k, seeds, offset)
            return carry

        lax.fori_loop(block // rows // 2, (block + step) // rows // 2, pair_step, 0)
        for first in (block, points + block):
            pltpu.make_async_copy(
                far_ref.at[:, first:first + step, :], far_hbm.at[:, first:first + step, :], far_sem
            ).start()
    rest_copy = pltpu.make_async_copy(rest_ref, rest_hbm, rest_sem)
    rest_copy.start()
    pltpu.make_async_copy(far_ref, far_hbm, far_sem).wait()
    rest_copy.wait()


def moment_kernel(
    spectra_ref, seed_ref, rest_hbm, far_hbm, facing_ref, amplitude_ref, out_ref,
    left_ref, moment_ref, rest_ref, made_even, made_odd, far_ref, sems, rest_sem, *, share
):
    far = far_ref.shape[0]
    near = share - far
    lead, observers = seed_ref.shape[1:]
    points = spectra_ref.shape[0]
    half = NQ * share
    tiles = points // LANES

    def far_copy(j):
        return pltpu.make_async_copy(far_hbm.at[j], far_ref.at[j], sems.at[j])

    rest_copy = pltpu.make_async_copy(rest_hbm, rest_ref, rest_sem)
    for j in range(far):
        far_copy(j).start()
        if j == min(1, far - 1):
            rest_copy.start()
    made = (made_even, made_odd)
    rows, lanes = 16, 128

    for tile in range(tiles):
        turned = spectra_ref[tile * LANES:(tile + 1) * LANES, :].astype(jnp.float32).T
        left_ref[tile] = turned
        left_ref[tiles + tile, :half] = turned[half:]
        left_ref[tiles + tile, half:] = -turned[:half]

    def generate(block, part):
        seeds, offset = (seed_ref, block * LANES) if block * LANES < lead else (rest_ref, block * LANES - lead)
        spot = pl.multiple_of(part * rows, rows)
        into = made[block % 2]
        for lane in range(0, observers, lanes):
            c_now, s_now, c_one, s_one = (
                seeds[k, pl.ds(offset + spot, rows), lane:lane + lanes] for k in range(4)
            )
            twice = c_one + c_one
            c_old = c_now * c_one + s_now * s_one
            s_old = s_now * c_one - c_now * s_one
            for j in range(near):
                into[j, pl.ds(spot, rows), lane:lane + lanes] = c_now.astype(jnp.bfloat16)
                into[j, pl.ds(LANES + spot, rows), lane:lane + lanes] = s_now.astype(jnp.bfloat16)
                if j < near - 1:
                    c_now, c_old = twice * c_now - c_old, c_now
                    s_now, s_old = twice * s_now - s_old, s_now

    def multiply(j, which, green, fresh):
        own = pl.ds(j, 2 * NQ, stride=share)
        left = jnp.concatenate([left_ref[tile, own, :] for tile in which], axis=1)
        product = jnp.dot(left.astype(jnp.bfloat16), green, preferred_element_type=jnp.float32)
        spot = pl.ds(pl.multiple_of(2 * NQ * j, 2 * NQ), 2 * NQ)
        for piece in range(observers // LANES):
            value = product[:, piece * LANES:(piece + 1) * LANES]
            moment_ref[piece, spot, :] = value if fresh else moment_ref[piece, spot, :] + value

    parts = LANES // rows
    unroll = 4
    trips = parts // unroll
    early = tiles // 2
    for block in range(tiles):
        if block * LANES == lead:
            rest_copy.wait()

        if block >= early:
            far_copy(block - early).wait()
            spot = slice(2 * NQ * (block - early), 2 * NQ * (block - early + 1))
            moment_ref[:, spot, :] = jnp.zeros((observers // LANES, 2 * NQ, LANES), jnp.float32)

        def part_step(step, carry):
            if block:
                for j in [step * (near // trips) + k for k in range(near // trips)]:
                    multiply(
                        far + j, (block - 1, tiles + block - 1), made[(block - 1) % 2][j], block == 1
                    )
            if block >= early:
                span = 2 * tiles // trips
                first = step * span
                multiply(
                    block - early, [first + k for k in range(span)],
                    far_ref[block - early, pl.ds(pl.multiple_of(first * LANES, LANES), span * LANES), :],
                    False,
                )
            for part in [step * unroll + u for u in range(unroll)]:
                generate(block, part)
            return carry

        lax.fori_loop(0, trips, part_step, 0)
    taken = tiles - early
    middle = (taken + far) // 2
    for j in range(taken, middle):
        far_copy(j).wait()
    for j in range(near):
        multiply(far + j, (tiles - 1, 2 * tiles - 1), made[(tiles - 1) % 2][j], tiles == 1)
    for j in range(taken, middle):
        multiply(j, range(2 * tiles), far_ref[j], True)
    for j in range(middle, far):
        far_copy(j).wait()
    for j in range(middle, far):
        multiply(j, range(2 * tiles), far_ref[j], True)

    amplitude = amplitude_ref[...]
    for piece in range(observers // LANES):
        lane = slice(piece * LANES, (piece + 1) * LANES)
        sums = []
        for part in range(2):
            total = None
            for q in range(NQ):
                term = moment_ref[piece, pl.ds(part * NQ + q, share, stride=2 * NQ), :]
                if q:
                    term = term * facing_ref[q - 1:q, lane]
                total = term if total is None else total + term
            sums.append(total)
        out_ref[0, :, 0, lane] = -amplitude * sums[1]
        out_ref[0, :, 1, lane] = amplitude * sums[0]


def per_device(series, send_rows, bin_counts, observer_cells):
    vol_count = lax.axis_size("vol")
    nar_count = lax.axis_size("nar")
    share = max(1, 2 * NF // (nar_count * vol_count))
    slots = send_rows.shape[2]
    points = vol_count * nar_count * slots
    observers = observer_cells.shape[1]
    time_len = series.shape[1] // NQ
    fits = (
        vol_count == 2 * NQ
        and vol_count * share == LANES
        and slots % 16 == 0
        and points % LANES == 0
        and share == 2 * (LANES // 16)
        and observers % 256 == 0
        and share * points * observers <= 8 << 20
    )
    if not fits:
        return per_device_general(series, send_rows, bin_counts, observer_cells)
    vmem = pl.BlockSpec(memory_space=pltpu.VMEM)
    hbm = pl.BlockSpec(memory_space=pltpu.HBM)
    places = slot_places(points)
    reach = float(np.sqrt((places ** 2).sum(axis=0)).max())
    place_rows = np.zeros((8, points), np.float32)
    place_rows[:3] = places
    table = dft_constant(time_len)
    near = 5 * share // 8
    counts_scratch = pltpu.SMEM(bin_counts.shape, jnp.int32)

    packed = pl.pallas_call(
        lambda *refs: pack_kernel(*refs, nar_count=nar_count, width=share),
        out_shape=jax.ShapeDtypeStruct((points, LANES), jnp.bfloat16),
        in_specs=[hbm] * 4,
        out_specs=vmem,
        scratch_shapes=[
            counts_scratch,
            pltpu.VMEM(send_rows.shape, jnp.int32),
            pltpu.VMEM(series.shape, series.dtype),
            pltpu.VMEM(table.shape, jnp.bfloat16),
            pltpu.SemaphoreType.DMA((4,)),
        ],
        compiler_params=pltpu.CompilerParams(vmem_limit_bytes=8 << 20),
        name="pack_rows",
    )(*map(in_hbm, (bin_counts, send_rows, series, jnp.asarray(table))))
    spectra = lax.all_to_all(packed, ("vol", "nar"), split_axis=0, concat_axis=0, tiled=True)
    far_shape = (share - near, 2 * points, observers)
    rest_shape = (4, LANES, observers)
    made = pltpu.VMEM((near, 2 * LANES, observers), jnp.bfloat16)
    seeds, rest, far_green, facing, amplitude = pl.pallas_call(
        lambda *refs: green_kernel(
            *refs, nar_count=nar_count, share=share, narrow=reach < 0.249
        ),
        out_shape=(
            jax.ShapeDtypeStruct((4, points - LANES, observers), jnp.float32),
            pltpu.HBM(rest_shape, jnp.float32),
            pltpu.HBM(far_shape, jnp.bfloat16),
            jax.ShapeDtypeStruct((3, observers), jnp.float32),
            jax.ShapeDtypeStruct((share, LANES), jnp.float32),
        ),
        in_specs=[hbm] * 3,
        out_specs=(vmem, hbm, hbm, vmem, vmem),
        scratch_shapes=[
            counts_scratch,
            pltpu.VMEM(observer_cells.shape, jnp.int32),
            pltpu.VMEM(place_rows.shape, jnp.float32),
            pltpu.VMEM((3, 8, observers), jnp.float32),
            pltpu.VMEM((points, 8), jnp.float32),
            pltpu.VMEM(rest_shape, jnp.float32),
            pltpu.VMEM(far_shape, jnp.bfloat16),
            pltpu.SemaphoreType.DMA((3,)),
            pltpu.SemaphoreType.DMA,
            pltpu.SemaphoreType.DMA,
        ],
        compiler_params=pltpu.CompilerParams(vmem_limit_bytes=24 << 20),
        cost_estimate=pl.CostEstimate(
            flops=60 * share * points * observers, bytes_accessed=4 * share * points * observers,
            transcendentals=0,
        ),
        name="green_grid",
    )(*map(in_hbm, (bin_counts, observer_cells, jnp.asarray(place_rows))))
    return pl.pallas_call(
        lambda *refs: moment_kernel(*refs, share=share),
        out_shape=jax.ShapeDtypeStruct((1, share, 2, observers), jnp.float32),
        in_specs=[vmem, vmem, hbm, hbm, vmem, vmem],
        out_specs=vmem,
        scratch_shapes=[
            pltpu.VMEM((2 * points // LANES, LANES, LANES), jnp.float32),
            pltpu.VMEM((observers // LANES, LANES, LANES), jnp.float32),
            pltpu.VMEM(rest_shape, jnp.float32),
            made,
            made,
            pltpu.VMEM(far_shape, jnp.bfloat16),
            pltpu.SemaphoreType.DMA((share - near,)),
            pltpu.SemaphoreType.DMA,
        ],
        compiler_params=pltpu.CompilerParams(
            vmem_limit_bytes=24 << 20
        ),
        name="moments",
    )(spectra, seeds, in_hbm(rest), in_hbm(far_green), facing, amplitude)


def solution(mesh):
    placed = (P(("vol", "nar"), None), P("vol", "nar", None), P(), P())
    return jax.shard_map(
        per_device,
        mesh=mesh,
        in_specs=placed,
        out_specs=P("nar", "vol", None, None),
        check_vma=False,
    )
```

```python
import math

import jax
import jax.numpy as jnp
import numpy as np
from jax import lax
from jax.experimental import pallas as pl
from jax.experimental.pallas import tpu as pltpu
from jax.sharding import PartitionSpec as P

NF = 256
NQ = 4


WAVE_STEP = 0.05


def dft_table(bin_ids, keep_bin, time_len):
    time_steps = jnp.arange(time_len, dtype=jnp.int32)
    frequency = bin_ids + 1
    phase_turns = time_steps[:, None] * frequency[None, :] % time_len
    angle_grid = phase_turns.astype(jnp.float32) * (2.0 * math.pi / time_len)
    dft_grid = jnp.stack([jnp.cos(angle_grid), -jnp.sin(angle_grid)], axis=-1)
    dft_grid = jnp.where(keep_bin[None, :, None], dft_grid, jnp.float32(0.0))
    return dft_grid.reshape(time_len, 2 * bin_ids.shape[0]).astype(jnp.bfloat16)


def positions(point_list):
    beside_all = (point_list * 1597 % 8191).astype(jnp.float32) * (2.0 * math.pi / 8191.0)
    jitter = (point_list * 613 % 127).astype(jnp.float32) * (0.37 / 127.0)
    axial = (point_list // 128).astype(jnp.float32) * 0.5 + jitter
    return (20.0 * jnp.cos(beside_all), 20.0 * jnp.sin(beside_all), axial)


def directions(obs_cells):
    polar_angle = (obs_cells[0].astype(jnp.float32) + 0.5) * (math.pi / 128.0)
    azimuth = obs_cells[1].astype(jnp.float32) * (2.0 * math.pi / 128.0)
    return (
        jnp.sin(polar_angle) * jnp.cos(azimuth),
        jnp.sin(polar_angle) * jnp.sin(azimuth),
        jnp.cos(polar_angle),
    )


def project(facing, place_xyz):
    dotted = facing[0][:, None] * place_xyz[0][None, :] + facing[1][:, None] * place_xyz[1][None, :]
    return dotted + facing[2][:, None] * place_xyz[2][None, :]


def kernels(bin_ids, dotted):
    wavenumber = (bin_ids.astype(jnp.float32) + 1.0) * WAVE_STEP
    phase_grid = wavenumber[:, None, None] * dotted[None]
    return jnp.concatenate([jnp.cos(phase_grid), jnp.sin(phase_grid)], axis=1).astype(jnp.bfloat16)


def combine(products, bin_ids, facing, norm_scale):
    observers = facing[0].shape[0]
    bin_total = bin_ids.shape[0]
    cos_part = products[:, :observers].reshape(bin_total, observers, NQ, 2)
    sine_part = products[:, observers:].reshape(bin_total, observers, NQ, 2)
    real_part = cos_part[..., 0] + sine_part[..., 1]
    imag_part = cos_part[..., 1] - sine_part[..., 0]
    weights = jnp.stack([jnp.ones_like(facing[0]), facing[0], facing[1], facing[2]], axis=-1)
    real_sum = jnp.sum(real_part * weights[None], axis=-1)
    imag_sum = jnp.sum(imag_part * weights[None], axis=-1)
    amplitude = (bin_ids.astype(jnp.float32) + 1.0) * (norm_scale / NF)
    return jnp.stack([-amplitude[:, None] * imag_sum, amplitude[:, None] * real_sum], axis=1)


def apply_green(bin_ids, spec_block, dotted, facing, norm_scale):
    green_grid = kernels(bin_ids, dotted)
    products = jnp.einsum(
        "bxp,bcp->bxc", green_grid, spec_block, preferred_element_type=jnp.float32
    )
    return combine(products, bin_ids, facing, norm_scale)


def per_device_general(series, send_rows, bin_counts, observer_cells):
    vol_count = lax.axis_size("vol")
    nar_count = lax.axis_size("nar")
    vol_index = lax.axis_index("vol")
    nar_index = lax.axis_index("nar")
    bin_cap = vol_count * max(1, 2 * NF // (nar_count * vol_count))
    time_len = series.shape[1] // NQ
    slot_total = send_rows.shape[2]
    slot_width = slot_total // vol_count
    listing = send_rows.reshape(-1)
    picked = jnp.take(series, jnp.maximum(listing, 0), axis=0)
    packed = jnp.where((listing >= 0)[:, None], picked, jnp.zeros((), series.dtype))
    arrived = lax.all_to_all(packed, "vol", split_axis=0, concat_axis=0, tiled=True)
    starts = jnp.cumsum(bin_counts) - bin_counts
    own_start = starts[nar_index]
    own_count = bin_counts[nar_index]
    dft_scale = 1.0 / math.sqrt(time_len)
    within = jnp.arange(bin_cap, dtype=jnp.int32)
    own_table = dft_table(own_start + within, within < own_count, time_len)
    row_piece = lax.all_gather(arrived, "nar", axis=0, tiled=True)
    rows_here = row_piece.shape[0]
    spectral = jnp.dot(
        row_piece.reshape(rows_here * NQ, time_len), own_table, preferred_element_type=jnp.float32
    )
    spectral = (spectral * dft_scale).astype(jnp.bfloat16).reshape(rows_here, NQ, bin_cap, 2)
    spectra = spectral.transpose(2, 1, 3, 0).reshape(bin_cap, 2 * NQ, rows_here)
    local_points = nar_count * slot_total

    def point_ids(vol_owner, flat_index):
        nar_source = flat_index // slot_total
        remain = flat_index % slot_total
        vol_source = remain // slot_width
        within_slot = remain % slot_width
        return (
            (vol_source * nar_count + nar_source) * vol_count + vol_owner
        ) * slot_width + within_slot

    norm_scale = 1.0 / math.sqrt(vol_count * nar_count * slot_total)
    facing = directions(observer_cells)
    share_rows = bin_cap // vol_count
    regrouped = lax.all_to_all(spectra, "vol", split_axis=0, concat_axis=2, tiled=True)
    bin_ids = own_start + vol_index * share_rows + jnp.arange(share_rows, dtype=jnp.int32)
    span_points = local_points * max(1, vol_count // 8)
    turn_count = vol_count * local_points // span_points

    def add_block(turn_index, running):
        first_point = turn_index * span_points
        spec_block = lax.dynamic_slice_in_dim(regrouped, first_point, span_points, 2)
        flat_index = first_point + jnp.arange(span_points, dtype=jnp.int32)
        point_list = point_ids(flat_index // local_points, flat_index % local_points)
        dotted = project(facing, positions(point_list))
        return running + apply_green(bin_ids, spec_block, dotted, facing, norm_scale)

    result = lax.fori_loop(
        0, turn_count, add_block, jnp.zeros((share_rows, 2, observer_cells.shape[1]), jnp.float32)
    )
    return result.reshape(1, share_rows, 2, result.shape[-1])


LANES = 128
TURN = 2.0 * math.pi

WIDE_SIN = (6.2831854820251465, -41.34170150756836, 81.60513305664062, -76.70301818847656,
            42.02592849731445, -14.899847030639648, 3.2381374835968018)
WIDE_COS = (1.0, -19.73920440673828, 64.93911743164062, -85.45014190673828,
            60.16762924194336, -25.967599868774414, 6.528658390045166)
NARROW_SIN = (6.2831854820251465, -41.34168243408203, 81.60247802734375, -76.58128356933594,
              39.76072311401367)
NARROW_COS = (1.0, -19.739208221435547, 64.93934631347656, -85.45356750488281,
              60.143951416015625, -24.981836318969727)


def horner(coefficients, z):
    total = jnp.full_like(z, coefficients[-1])
    for value in coefficients[-2::-1]:
        total = total * z + value
    return total


def cos_sin_turns(turns, narrow=False):
    if narrow:
        z = turns * turns
        return horner(NARROW_COS, z), horner(NARROW_SIN, z) * turns
    turns = turns - jnp.floor(turns + 0.5)
    z = turns * turns
    return horner(WIDE_COS, z), horner(WIDE_SIN, z) * turns


def slot_places(point_total):
    ids = np.arange(point_total, dtype=np.int64)
    angle = (ids * 1597 % 8191).astype(np.float64) * (TURN / 8191.0)
    axial = (ids // 128) * 0.5 + (ids * 613 % 127) * (0.37 / 127.0)
    place = np.stack([20.0 * np.cos(angle), 20.0 * np.sin(angle), axial])
    return place * (WAVE_STEP / TURN)


def dft_constant(time_len):
    turns = np.arange(time_len)[:, None] * (np.arange(NF) + 1)[None, :] % time_len
    angle = turns.astype(np.float32) * np.float32(TURN / time_len)
    grid = np.concatenate([np.cos(angle), -np.sin(angle)], axis=1)
    return grid.astype(jnp.bfloat16)


def own_bins(counts_ref, nar_count):
    nar_index = lax.axis_index("nar")
    start = jnp.int32(0)
    for m in range(nar_count - 1):
        start = start + jnp.where(m < nar_index, counts_ref[m], 0)
    return start, counts_ref[nar_index]


def swap_groups(blocks, width):
    blocks = list(blocks)
    amount = len(blocks)
    lanes = amount * width
    group = lax.broadcasted_iota(jnp.int32, blocks[0].shape, 1) // width
    step = 1
    while step < amount:
        high = (group & step) != 0
        for r in range(amount):
            if r & step == 0:
                x, y = blocks[r], blocks[r | step]
                blocks[r] = jnp.where(high, pltpu.roll(y, step * width, 1), x)
                blocks[r | step] = jnp.where(high, y, pltpu.roll(x, lanes - step * width, 1))
        step *= 2
    return blocks


def in_hbm(array):
    return pltpu.with_memory_space_constraint(array, pltpu.HBM)


def fetch_all(pairs, sems):
    copies = [
        pltpu.make_async_copy(source, target, sems.at[i])
        for i, (source, target) in enumerate(pairs)
    ]
    for copy in copies:
        copy.start()
    return copies


def pack_kernel(
    counts_hbm, rows_hbm, series_hbm, table_hbm, out_ref,
    counts_ref, rows_ref, series_ref, table_ref, sems, *, nar_count, width
):
    copies = fetch_all(
        [(rows_hbm, rows_ref), (series_hbm, series_ref), (table_hbm, table_ref), (counts_hbm, counts_ref)],
        sems,
    )
    row_total = series_ref.shape[0]
    slots = rows_ref.shape[2]
    time_len = series_ref.shape[1] // NQ
    row_ids = lax.broadcasted_iota(jnp.int32, (row_total, slots), 0)
    copies[0].wait()
    hot = jnp.where(row_ids == rows_ref[0], 1.0, 0.0).astype(jnp.bfloat16)
    copies[1].wait()
    picked = lax.dot_general(
        hot, series_ref[...], (((0,), (0,)), ((), ())), preferred_element_type=jnp.float32
    ).astype(jnp.bfloat16)
    stacked = jnp.concatenate(
        [picked[:, q * time_len:(q + 1) * time_len] for q in range(NQ)], axis=0
    )
    copies[2].wait()
    spectral = jnp.dot(stacked, table_ref[...], preferred_element_type=jnp.float32)
    spectral = spectral * (1.0 / math.sqrt(time_len))
    copies[3].wait()
    start = jnp.int32(0)
    for m in range(nar_count):
        blocks = []
        for part in range(2):
            half = spectral[:, part * NF:(part + 1) * NF]
            half = pltpu.roll(half, lax.rem(NF - start, NF), 1)[:, :LANES]
            half = half.astype(jnp.bfloat16)
            blocks += [half[q * slots:(q + 1) * slots] for q in range(NQ)]
        for v, chunk in enumerate(swap_groups(blocks, width)):
            first = (v * nar_count + m) * slots
            out_ref[first:first + slots, :] = chunk.astype(jnp.bfloat16)
        start = start + counts_ref[m]


def green_kernel(
    counts_hbm, cells_hbm, place_hbm,
    seed_ref, rest_hbm, far_hbm, facing_ref, amplitude_ref,
    counts_ref, cells_ref, place_ref, spread_ref, column_ref, rest_ref, far_ref, sems, far_sem, rest_sem,
    *, nar_count, share, narrow
):
    copies = fetch_all(
        [(counts_hbm, counts_ref), (cells_hbm, cells_ref), (place_hbm, place_ref)], sems
    )
    points = place_ref.shape[1]
    observers = cells_ref.shape[1]
    far = far_ref.shape[0]
    for copy in copies:
        copy.wait()
    start, count = own_bins(counts_ref, nar_count)
    within = lax.axis_index("vol") * share
    base_step = (start + within + 1).astype(jnp.float32)
    within = within + lax.broadcasted_iota(jnp.int32, amplitude_ref.shape, 0)
    amplitude = (start + within + 1).astype(jnp.float32) * (1.0 / (math.sqrt(points) * NF))
    amplitude_ref[...] = jnp.where(within < count, amplitude, 0.0)
    cells = cells_ref[...].astype(jnp.float32)
    cos_polar, sin_polar = cos_sin_turns((cells[0:1] + 0.5) * (1.0 / 256.0))
    cos_azimuth, sin_azimuth = cos_sin_turns(cells[1:2] * (1.0 / 128.0))
    facing = (sin_polar * cos_azimuth, sin_polar * sin_azimuth, cos_polar)
    for axis in range(3):
        facing_ref[axis:axis + 1, :] = facing[axis]
        spread_ref[axis] = jnp.broadcast_to(facing[axis], (8, observers))
    for tile in range(points // LANES):
        column_ref[tile * LANES:(tile + 1) * LANES, :] = (
            place_ref[:, tile * LANES:(tile + 1) * LANES].T
        )
    rows, lanes = 16, 256

    def tile_step(tile, seeds, offset):
        first = pl.multiple_of(tile * rows, rows)
        place = [column_ref[pl.ds(first, rows), axis:axis + 1] for axis in range(3)]
        for lane in range(0, observers, lanes):
            def seen(axis):
                return jnp.concatenate([spread_ref[axis, :, lane:lane + lanes]] * (rows // 8), axis=0)
            turns = seen(0) * place[0] + seen(1) * place[1]
            turns = turns + seen(2) * place[2]
            c_now, s_now = cos_sin_turns(turns * base_step)
            c_one, s_one = cos_sin_turns(turns, narrow)
            twice = c_one + c_one
            c_old = c_now * c_one + s_now * s_one
            s_old = s_now * c_one - c_now * s_one
            for j in range(far):
                far_ref[j, pl.ds(first, rows), lane:lane + lanes] = c_now.astype(jnp.bfloat16)
                far_ref[j, pl.ds(first + points, rows), lane:lane + lanes] = s_now.astype(jnp.bfloat16)
                c_now, c_old = twice * c_now - c_old, c_now
                s_now, s_old = twice * s_now - s_old, s_now
            spot = (pl.ds(first - offset, rows), slice(lane, lane + lanes))
            for k, value in enumerate((c_now, s_now, c_one, s_one)):
                seeds[k, *spot] = value

    step = 64
    lead = seed_ref.shape[1]
    for block in range(0, points, step):
        seeds, offset = (seed_ref, 0) if block < lead else (rest_ref, lead)
        def pair_step(pair, carry):
            for k in range(2):
                tile_step(pair * 2 + k, seeds, offset)
            return carry

        lax.fori_loop(block // rows // 2, (block + step) // rows // 2, pair_step, 0)
        for first in (block, points + block):
            pltpu.make_async_copy(
                far_ref.at[:, first:first + step, :], far_hbm.at[:, first:first + step, :], far_sem
            ).start()
    rest_copy = pltpu.make_async_copy(rest_ref, rest_hbm, rest_sem)
    rest_copy.start()
    pltpu.make_async_copy(far_ref, far_hbm, far_sem).wait()
    rest_copy.wait()


def moment_kernel(
    spectra_ref, seed_ref, rest_hbm, far_hbm, facing_ref, amplitude_ref, out_ref,
    left_ref, moment_ref, rest_ref, made_even, made_odd, far_ref, sems, rest_sem, *, share
):
    far = far_ref.shape[0]
    near = share - far
    lead, observers = seed_ref.shape[1:]
    points = spectra_ref.shape[0]
    half = NQ * share
    tiles = points // LANES

    def far_copy(j):
        return pltpu.make_async_copy(far_hbm.at[j], far_ref.at[j], sems.at[j])

    rest_copy = pltpu.make_async_copy(rest_hbm, rest_ref, rest_sem)
    for j in range(far):
        far_copy(j).start()
        if j == min(1, far - 1):
            rest_copy.start()
    made = (made_even, made_odd)
    rows, lanes = 16, 128

    for tile in range(tiles):
        turned = spectra_ref[tile * LANES:(tile + 1) * LANES, :].astype(jnp.float32).T
        left_ref[tile] = turned
        left_ref[tiles + tile, :half] = turned[half:]
        left_ref[tiles + tile, half:] = -turned[:half]

    def generate(block, part):
        seeds, offset = (seed_ref, block * LANES) if block * LANES < lead else (rest_ref, block * LANES - lead)
        spot = pl.multiple_of(part * rows, rows)
        into = made[block % 2]
        for lane in range(0, observers, lanes):
            c_now, s_now, c_one, s_one = (
                seeds[k, pl.ds(offset + spot, rows), lane:lane + lanes] for k in range(4)
            )
            twice = c_one + c_one
            c_old = c_now * c_one + s_now * s_one
            s_old = s_now * c_one - c_now * s_one
            for j in range(near):
                into[j, pl.ds(spot, rows), lane:lane + lanes] = c_now.astype(jnp.bfloat16)
                into[j, pl.ds(LANES + spot, rows), lane:lane + lanes] = s_now.astype(jnp.bfloat16)
                if j < near - 1:
                    c_now, c_old = twice * c_now - c_old, c_now
                    s_now, s_old = twice * s_now - s_old, s_now

    def multiply(j, which, green, fresh):
        own = pl.ds(j, 2 * NQ, stride=share)
        left = jnp.concatenate([left_ref[tile, own, :] for tile in which], axis=1)
        product = jnp.dot(left.astype(jnp.bfloat16), green, preferred_element_type=jnp.float32)
        spot = pl.ds(pl.multiple_of(2 * NQ * j, 2 * NQ), 2 * NQ)
        for piece in range(observers // LANES):
            value = product[:, piece * LANES:(piece + 1) * LANES]
            moment_ref[piece, spot, :] = value if fresh else moment_ref[piece, spot, :] + value

    parts = LANES // rows
    unroll = 4
    trips = parts // unroll
    early = tiles // 2
    for block in range(tiles):
        if block * LANES == lead:
            rest_copy.wait()

        if block >= early:
            far_copy(block - early).wait()
            spot = slice(2 * NQ * (block - early), 2 * NQ * (block - early + 1))
            moment_ref[:, spot, :] = jnp.zeros((observers // LANES, 2 * NQ, LANES), jnp.float32)

        def part_step(step, carry):
            if block:
                for j in [step * (near // trips) + k for k in range(near // trips)]:
                    multiply(
                        far + j, (block - 1, tiles + block - 1), made[(block - 1) % 2][j], block == 1
                    )
            if block >= early:
                span = 2 * tiles // trips
                first = step * span
                multiply(
                    block - early, [first + k for k in range(span)],
                    far_ref[block - early, pl.ds(pl.multiple_of(first * LANES, LANES), span * LANES), :],
                    False,
                )
            for part in [step * unroll + u for u in range(unroll)]:
                generate(block, part)
            return carry

        lax.fori_loop(0, trips, part_step, 0)
    taken = tiles - early
    middle = (taken + far) // 2
    for j in range(taken, middle):
        far_copy(j).wait()
    for j in range(near):
        multiply(far + j, (tiles - 1, 2 * tiles - 1), made[(tiles - 1) % 2][j], tiles == 1)
    for j in range(taken, middle):
        multiply(j, range(2 * tiles), far_ref[j], True)
    for j in range(middle, far):
        far_copy(j).wait()
    for j in range(middle, far):
        multiply(j, range(2 * tiles), far_ref[j], True)

    amplitude = amplitude_ref[...]
    for piece in range(observers // LANES):
        lane = slice(piece * LANES, (piece + 1) * LANES)
        sums = []
        for part in range(2):
            total = None
            for q in range(NQ):
                term = moment_ref[piece, pl.ds(part * NQ + q, share, stride=2 * NQ), :]
                if q:
                    term = term * facing_ref[q - 1:q, lane]
                total = term if total is None else total + term
            sums.append(total)
        out_ref[0, :, 0, lane] = -amplitude * sums[1]
        out_ref[0, :, 1, lane] = amplitude * sums[0]


def per_device(series, send_rows, bin_counts, observer_cells):
    vol_count = lax.axis_size("vol")
    nar_count = lax.axis_size("nar")
    share = max(1, 2 * NF // (nar_count * vol_count))
    slots = send_rows.shape[2]
    points = vol_count * nar_count * slots
    observers = observer_cells.shape[1]
    time_len = series.shape[1] // NQ
    fits = (
        vol_count == 2 * NQ
        and vol_count * share == LANES
        and slots % 16 == 0
        and points % LANES == 0
        and share == 2 * (LANES // 16)
        and observers % 256 == 0
        and share * points * observers <= 8 << 20
    )
    if not fits:
        return per_device_general(series, send_rows, bin_counts, observer_cells)
    vmem = pl.BlockSpec(memory_space=pltpu.VMEM)
    hbm = pl.BlockSpec(memory_space=pltpu.HBM)
    places = slot_places(points)
    reach = float(np.sqrt((places ** 2).sum(axis=0)).max())
    place_rows = np.zeros((8, points), np.float32)
    place_rows[:3] = places
    table = dft_constant(time_len)
    near = 5 * share // 8
    counts_scratch = pltpu.SMEM(bin_counts.shape, jnp.int32)

    packed = pl.pallas_call(
        lambda *refs: pack_kernel(*refs, nar_count=nar_count, width=share),
        out_shape=jax.ShapeDtypeStruct((points, LANES), jnp.bfloat16),
        in_specs=[hbm] * 4,
        out_specs=vmem,
        scratch_shapes=[
            counts_scratch,
            pltpu.VMEM(send_rows.shape, jnp.int32),
            pltpu.VMEM(series.shape, series.dtype),
            pltpu.VMEM(table.shape, jnp.bfloat16),
            pltpu.SemaphoreType.DMA((4,)),
        ],
        compiler_params=pltpu.CompilerParams(vmem_limit_bytes=8 << 20),
        name="pack_rows",
    )(*map(in_hbm, (bin_counts, send_rows, series, jnp.asarray(table))))
    spectra = lax.all_to_all(packed, ("vol", "nar"), split_axis=0, concat_axis=0, tiled=True)
    far_shape = (share - near, 2 * points, observers)
    rest_shape = (4, LANES, observers)
    made = pltpu.VMEM((near, 2 * LANES, observers), jnp.bfloat16)
    seeds, rest, far_green, facing, amplitude = pl.pallas_call(
        lambda *refs: green_kernel(
            *refs, nar_count=nar_count, share=share, narrow=reach < 0.249
        ),
        out_shape=(
            jax.ShapeDtypeStruct((4, points - LANES, observers), jnp.float32),
            pltpu.HBM(rest_shape, jnp.float32),
            pltpu.HBM(far_shape, jnp.bfloat16),
            jax.ShapeDtypeStruct((3, observers), jnp.float32),
            jax.ShapeDtypeStruct((share, LANES), jnp.float32),
        ),
        in_specs=[hbm] * 3,
        out_specs=(vmem, hbm, hbm, vmem, vmem),
        scratch_shapes=[
            counts_scratch,
            pltpu.VMEM(observer_cells.shape, jnp.int32),
            pltpu.VMEM(place_rows.shape, jnp.float32),
            pltpu.VMEM((3, 8, observers), jnp.float32),
            pltpu.VMEM((points, 8), jnp.float32),
            pltpu.VMEM(rest_shape, jnp.float32),
            pltpu.VMEM(far_shape, jnp.bfloat16),
            pltpu.SemaphoreType.DMA((3,)),
            pltpu.SemaphoreType.DMA,
            pltpu.SemaphoreType.DMA,
        ],
        compiler_params=pltpu.CompilerParams(vmem_limit_bytes=24 << 20),
        cost_estimate=pl.CostEstimate(
            flops=60 * share * points * observers, bytes_accessed=4 * share * points * observers,
            transcendentals=0,
        ),
        name="green_grid",
    )(*map(in_hbm, (bin_counts, observer_cells, jnp.asarray(place_rows))))
    return pl.pallas_call(
        lambda *refs: moment_kernel(*refs, share=share),
        out_shape=jax.ShapeDtypeStruct((1, share, 2, observers), jnp.float32),
        in_specs=[vmem, vmem, hbm, hbm, vmem, vmem],
        out_specs=vmem,
        scratch_shapes=[
            pltpu.VMEM((2 * points // LANES, LANES, LANES), jnp.float32),
            pltpu.VMEM((observers // LANES, LANES, LANES), jnp.float32),
            pltpu.VMEM(rest_shape, jnp.float32),
            made,
            made,
            pltpu.VMEM(far_shape, jnp.bfloat16),
            pltpu.SemaphoreType.DMA((share - near,)),
            pltpu.SemaphoreType.DMA,
        ],
        compiler_params=pltpu.CompilerParams(
            vmem_limit_bytes=24 << 20
        ),
        name="moments",
    )(spectra, seeds, in_hbm(rest), in_hbm(far_green), facing, amplitude)


def solution(mesh):
    placed = (P(("vol", "nar"), None), P("vol", "nar", None), P(), P())
    return jax.shard_map(
        per_device,
        mesh=mesh,
        in_specs=placed,
        out_specs=P("nar", "vol", None, None),
        check_vma=False,
    )
```

```python
import math

import jax
import jax.numpy as jnp
import numpy as np
from jax import lax
from jax.experimental import pallas as pl
from jax.experimental.pallas import tpu as pltpu
from jax.sharding import PartitionSpec as P

NF = 256
NQ = 4


WAVE_STEP = 0.05


def dft_table(bin_ids, keep_bin, time_len):
    time_steps = jnp.arange(time_len, dtype=jnp.int32)
    frequency = bin_ids + 1
    phase_turns = time_steps[:, None] * frequency[None, :] % time_len
    angle_grid = phase_turns.astype(jnp.float32) * (2.0 * math.pi / time_len)
    dft_grid = jnp.stack([jnp.cos(angle_grid), -jnp.sin(angle_grid)], axis=-1)
    dft_grid = jnp.where(keep_bin[None, :, None], dft_grid, jnp.float32(0.0))
    return dft_grid.reshape(time_len, 2 * bin_ids.shape[0]).astype(jnp.bfloat16)


def positions(point_list):
    beside_all = (point_list * 1597 % 8191).astype(jnp.float32) * (2.0 * math.pi / 8191.0)
    jitter = (point_list * 613 % 127).astype(jnp.float32) * (0.37 / 127.0)
    axial = (point_list // 128).astype(jnp.float32) * 0.5 + jitter
    return (20.0 * jnp.cos(beside_all), 20.0 * jnp.sin(beside_all), axial)


def directions(obs_cells):
    polar_angle = (obs_cells[0].astype(jnp.float32) + 0.5) * (math.pi / 128.0)
    azimuth = obs_cells[1].astype(jnp.float32) * (2.0 * math.pi / 128.0)
    return (
        jnp.sin(polar_angle) * jnp.cos(azimuth),
        jnp.sin(polar_angle) * jnp.sin(azimuth),
        jnp.cos(polar_angle),
    )


def project(facing, place_xyz):
    dotted = facing[0][:, None] * place_xyz[0][None, :] + facing[1][:, None] * place_xyz[1][None, :]
    return dotted + facing[2][:, None] * place_xyz[2][None, :]


def kernels(bin_ids, dotted):
    wavenumber = (bin_ids.astype(jnp.float32) + 1.0) * WAVE_STEP
    phase_grid = wavenumber[:, None, None] * dotted[None]
    return jnp.concatenate([jnp.cos(phase_grid), jnp.sin(phase_grid)], axis=1).astype(jnp.bfloat16)


def combine(products, bin_ids, facing, norm_scale):
    observers = facing[0].shape[0]
    bin_total = bin_ids.shape[0]
    cos_part = products[:, :observers].reshape(bin_total, observers, NQ, 2)
    sine_part = products[:, observers:].reshape(bin_total, observers, NQ, 2)
    real_part = cos_part[..., 0] + sine_part[..., 1]
    imag_part = cos_part[..., 1] - sine_part[..., 0]
    weights = jnp.stack([jnp.ones_like(facing[0]), facing[0], facing[1], facing[2]], axis=-1)
    real_sum = jnp.sum(real_part * weights[None], axis=-1)
    imag_sum = jnp.sum(imag_part * weights[None], axis=-1)
    amplitude = (bin_ids.astype(jnp.float32) + 1.0) * (norm_scale / NF)
    return jnp.stack([-amplitude[:, None] * imag_sum, amplitude[:, None] * real_sum], axis=1)


def apply_green(bin_ids, spec_block, dotted, facing, norm_scale):
    green_grid = kernels(bin_ids, dotted)
    products = jnp.einsum(
        "bxp,bcp->bxc", green_grid, spec_block, preferred_element_type=jnp.float32
    )
    return combine(products, bin_ids, facing, norm_scale)


def per_device_general(series, send_rows, bin_counts, observer_cells):
    vol_count = lax.axis_size("vol")
    nar_count = lax.axis_size("nar")
    vol_index = lax.axis_index("vol")
    nar_index = lax.axis_index("nar")
    bin_cap = vol_count * max(1, 2 * NF // (nar_count * vol_count))
    time_len = series.shape[1] // NQ
    slot_total = send_rows.shape[2]
    slot_width = slot_total // vol_count
    listing = send_rows.reshape(-1)
    picked = jnp.take(series, jnp.maximum(listing, 0), axis=0)
    packed = jnp.where((listing >= 0)[:, None], picked, jnp.zeros((), series.dtype))
    arrived = lax.all_to_all(packed, "vol", split_axis=0, concat_axis=0, tiled=True)
    starts = jnp.cumsum(bin_counts) - bin_counts
    own_start = starts[nar_index]
    own_count = bin_counts[nar_index]
    dft_scale = 1.0 / math.sqrt(time_len)
    within = jnp.arange(bin_cap, dtype=jnp.int32)
    own_table = dft_table(own_start + within, within < own_count, time_len)
    row_piece = lax.all_gather(arrived, "nar", axis=0, tiled=True)
    rows_here = row_piece.shape[0]
    spectral = jnp.dot(
        row_piece.reshape(rows_here * NQ, time_len), own_table, preferred_element_type=jnp.float32
    )
    spectral = (spectral * dft_scale).astype(jnp.bfloat16).reshape(rows_here, NQ, bin_cap, 2)
    spectra = spectral.transpose(2, 1, 3, 0).reshape(bin_cap, 2 * NQ, rows_here)
    local_points = nar_count * slot_total

    def point_ids(vol_owner, flat_index):
        nar_source = flat_index // slot_total
        remain = flat_index % slot_total
        vol_source = remain // slot_width
        within_slot = remain % slot_width
        return (
            (vol_source * nar_count + nar_source) * vol_count + vol_owner
        ) * slot_width + within_slot

    norm_scale = 1.0 / math.sqrt(vol_count * nar_count * slot_total)
    facing = directions(observer_cells)
    share_rows = bin_cap // vol_count
    regrouped = lax.all_to_all(spectra, "vol", split_axis=0, concat_axis=2, tiled=True)
    bin_ids = own_start + vol_index * share_rows + jnp.arange(share_rows, dtype=jnp.int32)
    span_points = local_points * max(1, vol_count // 8)
    turn_count = vol_count * local_points // span_points

    def add_block(turn_index, running):
        first_point = turn_index * span_points
        spec_block = lax.dynamic_slice_in_dim(regrouped, first_point, span_points, 2)
        flat_index = first_point + jnp.arange(span_points, dtype=jnp.int32)
        point_list = point_ids(flat_index // local_points, flat_index % local_points)
        dotted = project(facing, positions(point_list))
        return running + apply_green(bin_ids, spec_block, dotted, facing, norm_scale)

    result = lax.fori_loop(
        0, turn_count, add_block, jnp.zeros((share_rows, 2, observer_cells.shape[1]), jnp.float32)
    )
    return result.reshape(1, share_rows, 2, result.shape[-1])


LANES = 128
TURN = 2.0 * math.pi

WIDE_SIN = (6.2831854820251465, -41.34170150756836, 81.60513305664062, -76.70301818847656,
            42.02592849731445, -14.899847030639648, 3.2381374835968018)
WIDE_COS = (1.0, -19.73920440673828, 64.93911743164062, -85.45014190673828,
            60.16762924194336, -25.967599868774414, 6.528658390045166)
NARROW_SIN = (6.2831854820251465, -41.34168243408203, 81.60247802734375, -76.58128356933594,
              39.76072311401367)
NARROW_COS = (1.0, -19.739208221435547, 64.93934631347656, -85.45356750488281,
              60.143951416015625, -24.981836318969727)


def horner(coefficients, z):
    total = jnp.full_like(z, coefficients[-1])
    for value in coefficients[-2::-1]:
        total = total * z + value
    return total


def cos_sin_turns(turns, narrow=False):
    if narrow:
        z = turns * turns
        return horner(NARROW_COS, z), horner(NARROW_SIN, z) * turns
    turns = turns - jnp.floor(turns + 0.5)
    z = turns * turns
    return horner(WIDE_COS, z), horner(WIDE_SIN, z) * turns


def slot_places(point_total):
    ids = np.arange(point_total, dtype=np.int64)
    angle = (ids * 1597 % 8191).astype(np.float64) * (TURN / 8191.0)
    axial = (ids // 128) * 0.5 + (ids * 613 % 127) * (0.37 / 127.0)
    place = np.stack([20.0 * np.cos(angle), 20.0 * np.sin(angle), axial])
    return place * (WAVE_STEP / TURN)


def dft_constant(time_len):
    turns = np.arange(time_len)[:, None] * (np.arange(NF) + 1)[None, :] % time_len
    angle = turns.astype(np.float32) * np.float32(TURN / time_len)
    grid = np.concatenate([np.cos(angle), -np.sin(angle)], axis=1)
    return grid.astype(jnp.bfloat16)


def own_bins(counts_ref, nar_count):
    nar_index = lax.axis_index("nar")
    start = jnp.int32(0)
    for m in range(nar_count - 1):
        start = start + jnp.where(m < nar_index, counts_ref[m], 0)
    return start, counts_ref[nar_index]


def swap_groups(blocks, width):
    blocks = list(blocks)
    amount = len(blocks)
    lanes = amount * width
    group = lax.broadcasted_iota(jnp.int32, blocks[0].shape, 1) // width
    step = 1
    while step < amount:
        high = (group & step) != 0
        for r in range(amount):
            if r & step == 0:
                x, y = blocks[r], blocks[r | step]
                blocks[r] = jnp.where(high, pltpu.roll(y, step * width, 1), x)
                blocks[r | step] = jnp.where(high, y, pltpu.roll(x, lanes - step * width, 1))
        step *= 2
    return blocks


def in_hbm(array):
    return pltpu.with_memory_space_constraint(array, pltpu.HBM)


def fetch_all(pairs, sems):
    copies = [
        pltpu.make_async_copy(source, target, sems.at[i])
        for i, (source, target) in enumerate(pairs)
    ]
    for copy in copies:
        copy.start()
    return copies


def pack_kernel(
    counts_hbm, rows_hbm, series_hbm, table_hbm, out_ref,
    counts_ref, rows_ref, series_ref, table_ref, sems, *, nar_count, width
):
    copies = fetch_all(
        [(rows_hbm, rows_ref), (series_hbm, series_ref), (table_hbm, table_ref), (counts_hbm, counts_ref)],
        sems,
    )
    row_total = series_ref.shape[0]
    slots = rows_ref.shape[2]
    time_len = series_ref.shape[1] // NQ
    row_ids = lax.broadcasted_iota(jnp.int32, (row_total, slots), 0)
    copies[0].wait()
    hot = jnp.where(row_ids == rows_ref[0], 1.0, 0.0).astype(jnp.bfloat16)
    copies[1].wait()
    picked = lax.dot_general(
        hot, series_ref[...], (((0,), (0,)), ((), ())), preferred_element_type=jnp.float32
    ).astype(jnp.bfloat16)
    stacked = jnp.concatenate(
        [picked[:, q * time_len:(q + 1) * time_len] for q in range(NQ)], axis=0
    )
    copies[2].wait()
    spectral = jnp.dot(stacked, table_ref[...], preferred_element_type=jnp.float32)
    spectral = spectral * (1.0 / math.sqrt(time_len))
    copies[3].wait()
    start = jnp.int32(0)
    for m in range(nar_count):
        blocks = []
        for part in range(2):
            half = spectral[:, part * NF:(part + 1) * NF]
            half = pltpu.roll(half, lax.rem(NF - start, NF), 1)[:, :LANES]
            half = half.astype(jnp.bfloat16)
            blocks += [half[q * slots:(q + 1) * slots] for q in range(NQ)]
        for v, chunk in enumerate(swap_groups(blocks, width)):
            first = (v * nar_count + m) * slots
            out_ref[first:first + slots, :] = chunk.astype(jnp.bfloat16)
        start = start + counts_ref[m]


def green_kernel(
    counts_hbm, cells_hbm, place_hbm,
    seed_ref, rest_hbm, far_hbm, facing_ref, amplitude_ref,
    counts_ref, cells_ref, place_ref, spread_ref, column_ref, rest_ref, far_ref, sems, far_sem, rest_sem,
    *, nar_count, share, narrow
):
    copies = fetch_all(
        [(counts_hbm, counts_ref), (cells_hbm, cells_ref), (place_hbm, place_ref)], sems
    )
    points = place_ref.shape[1]
    observers = cells_ref.shape[1]
    far = far_ref.shape[0]
    for copy in copies:
        copy.wait()
    start, count = own_bins(counts_ref, nar_count)
    within = lax.axis_index("vol") * share
    base_step = (start + within + 1).astype(jnp.float32)
    within = within + lax.broadcasted_iota(jnp.int32, amplitude_ref.shape, 0)
    amplitude = (start + within + 1).astype(jnp.float32) * (1.0 / (math.sqrt(points) * NF))
    amplitude_ref[...] = jnp.where(within < count, amplitude, 0.0)
    cells = cells_ref[...].astype(jnp.float32)
    cos_polar, sin_polar = cos_sin_turns((cells[0:1] + 0.5) * (1.0 / 256.0))
    cos_azimuth, sin_azimuth = cos_sin_turns(cells[1:2] * (1.0 / 128.0))
    facing = (sin_polar * cos_azimuth, sin_polar * sin_azimuth, cos_polar)
    for axis in range(3):
        facing_ref[axis:axis + 1, :] = facing[axis]
        spread_ref[axis] = jnp.broadcast_to(facing[axis], (8, observers))
    for tile in range(points // LANES):
        column_ref[tile * LANES:(tile + 1) * LANES, :] = (
            place_ref[:, tile * LANES:(tile + 1) * LANES].T
        )
    rows, lanes = 16, 256

    def tile_step(tile, seeds, offset):
        first = pl.multiple_of(tile * rows, rows)
        place = [column_ref[pl.ds(first, rows), axis:axis + 1] for axis in range(3)]
        for lane in range(0, observers, lanes):
            def seen(axis):
                return jnp.concatenate([spread_ref[axis, :, lane:lane + lanes]] * (rows // 8), axis=0)
            turns = seen(0) * place[0] + seen(1) * place[1]
            turns = turns + seen(2) * place[2]
            c_now, s_now = cos_sin_turns(turns * base_step)
            c_one, s_one = cos_sin_turns(turns, narrow)
            twice = c_one + c_one
            c_old = c_now * c_one + s_now * s_one
            s_old = s_now * c_one - c_now * s_one
            for j in range(far):
                far_ref[j, pl.ds(first, rows), lane:lane + lanes] = c_now.astype(jnp.bfloat16)
                far_ref[j, pl.ds(first + points, rows), lane:lane + lanes] = s_now.astype(jnp.bfloat16)
                c_now, c_old = twice * c_now - c_old, c_now
                s_now, s_old = twice * s_now - s_old, s_now
            spot = (pl.ds(first - offset, rows), slice(lane, lane + lanes))
            for k, value in enumerate((c_now, s_now, c_one, s_one)):
                seeds[k, *spot] = value

    step = 64
    lead = seed_ref.shape[1]
    for block in range(0, points, step):
        seeds, offset = (seed_ref, 0) if block < lead else (rest_ref, lead)
        def pair_step(pair, carry):
            for k in range(2):
                tile_step(pair * 2 + k, seeds, offset)
            return carry

        lax.fori_loop(block // rows // 2, (block + step) // rows // 2, pair_step, 0)
        for first in (block, points + block):
            pltpu.make_async_copy(
                far_ref.at[:, first:first + step, :], far_hbm.at[:, first:first + step, :], far_sem
            ).start()
    rest_copy = pltpu.make_async_copy(rest_ref, rest_hbm, rest_sem)
    rest_copy.start()
    pltpu.make_async_copy(far_ref, far_hbm, far_sem).wait()
    rest_copy.wait()


def moment_kernel(
    spectra_ref, seed_ref, rest_hbm, far_hbm, facing_ref, amplitude_ref, out_ref,
    left_ref, moment_ref, rest_ref, made_even, made_odd, far_ref, sems, rest_sem, *, share
):
    far = far_ref.shape[0]
    near = share - far
    lead, observers = seed_ref.shape[1:]
    points = spectra_ref.shape[0]
    half = NQ * share
    tiles = points // LANES

    def far_copy(j):
        return pltpu.make_async_copy(far_hbm.at[j], far_ref.at[j], sems.at[j])

    rest_copy = pltpu.make_async_copy(rest_hbm, rest_ref, rest_sem)
    for j in range(far):
        far_copy(j).start()
        if j == min(1, far - 1):
            rest_copy.start()
    made = (made_even, made_odd)
    rows, lanes = 16, 128

    for tile in range(tiles):
        turned = spectra_ref[tile * LANES:(tile + 1) * LANES, :].astype(jnp.float32).T
        left_ref[tile] = turned
        left_ref[tiles + tile, :half] = turned[half:]
        left_ref[tiles + tile, half:] = -turned[:half]

    def generate(block, part):
        seeds, offset = (seed_ref, block * LANES) if block * LANES < lead else (rest_ref, block * LANES - lead)
        spot = pl.multiple_of(part * rows, rows)
        into = made[block % 2]
        for lane in range(0, observers, lanes):
            c_now, s_now, c_one, s_one = (
                seeds[k, pl.ds(offset + spot, rows), lane:lane + lanes] for k in range(4)
            )
            twice = c_one + c_one
            c_old = c_now * c_one + s_now * s_one
            s_old = s_now * c_one - c_now * s_one
            for j in range(near):
                into[j, pl.ds(spot, rows), lane:lane + lanes] = c_now.astype(jnp.bfloat16)
                into[j, pl.ds(LANES + spot, rows), lane:lane + lanes] = s_now.astype(jnp.bfloat16)
                if j < near - 1:
                    c_now, c_old = twice * c_now - c_old, c_now
                    s_now, s_old = twice * s_now - s_old, s_now

    def multiply(j, which, green, fresh):
        own = pl.ds(j, 2 * NQ, stride=share)
        left = jnp.concatenate([left_ref[tile, own, :] for tile in which], axis=1)
        product = jnp.dot(left.astype(jnp.bfloat16), green, preferred_element_type=jnp.float32)
        spot = pl.ds(pl.multiple_of(2 * NQ * j, 2 * NQ), 2 * NQ)
        for piece in range(observers // LANES):
            value = product[:, piece * LANES:(piece + 1) * LANES]
            moment_ref[piece, spot, :] = value if fresh else moment_ref[piece, spot, :] + value

    parts = LANES // rows
    unroll = 4
    trips = parts // unroll
    early = tiles // 2
    for block in range(tiles):
        if block * LANES == lead:
            rest_copy.wait()

        if block >= early:
            far_copy(block - early).wait()
            spot = slice(2 * NQ * (block - early), 2 * NQ * (block - early + 1))
            moment_ref[:, spot, :] = jnp.zeros((observers // LANES, 2 * NQ, LANES), jnp.float32)

        def part_step(step, carry):
            if block:
                for j in [step * (near // trips) + k for k in range(near // trips)]:
                    multiply(
                        far + j, (block - 1, tiles + block - 1), made[(block - 1) % 2][j], block == 1
                    )
            if block >= early:
                span = 2 * tiles // trips
                first = step * span
                multiply(
                    block - early, [first + k for k in range(span)],
                    far_ref[block - early, pl.ds(pl.multiple_of(first * LANES, LANES), span * LANES), :],
                    False,
                )
            for part in [step * unroll + u for u in range(unroll)]:
                generate(block, part)
            return carry

        lax.fori_loop(0, trips, part_step, 0)
    taken = tiles - early
    middle = (taken + far) // 2
    for j in range(taken, middle):
        far_copy(j).wait()
    for j in range(near):
        multiply(far + j, (tiles - 1, 2 * tiles - 1), made[(tiles - 1) % 2][j], tiles == 1)
    for j in range(taken, middle):
        multiply(j, range(2 * tiles), far_ref[j], True)
    for j in range(middle, far):
        far_copy(j).wait()
    for j in range(middle, far):
        multiply(j, range(2 * tiles), far_ref[j], True)

    amplitude = amplitude_ref[...]
    for piece in range(observers // LANES):
        lane = slice(piece * LANES, (piece + 1) * LANES)
        sums = []
        for part in range(2):
            total = None
            for q in range(NQ):
                term = moment_ref[piece, pl.ds(part * NQ + q, share, stride=2 * NQ), :]
                if q:
                    term = term * facing_ref[q - 1:q, lane]
                total = term if total is None else total + term
            sums.append(total)
        out_ref[0, :, 0, lane] = -amplitude * sums[1]
        out_ref[0, :, 1, lane] = amplitude * sums[0]


def per_device(series, send_rows, bin_counts, observer_cells):
    vol_count = lax.axis_size("vol")
    nar_count = lax.axis_size("nar")
    share = max(1, 2 * NF // (nar_count * vol_count))
    slots = send_rows.shape[2]
    points = vol_count * nar_count * slots
    observers = observer_cells.shape[1]
    time_len = series.shape[1] // NQ
    fits = (
        vol_count == 2 * NQ
        and vol_count * share == LANES
        and slots % 16 == 0
        and points % LANES == 0
        and share == 2 * (LANES // 16)
        and observers % 256 == 0
        and share * points * observers <= 8 << 20
    )
    if not fits:
        return per_device_general(series, send_rows, bin_counts, observer_cells)
    vmem = pl.BlockSpec(memory_space=pltpu.VMEM)
    hbm = pl.BlockSpec(memory_space=pltpu.HBM)
    places = slot_places(points)
    reach = float(np.sqrt((places ** 2).sum(axis=0)).max())
    place_rows = np.zeros((8, points), np.float32)
    place_rows[:3] = places
    table = dft_constant(time_len)
    near = 3 * share // 4
    counts_scratch = pltpu.SMEM(bin_counts.shape, jnp.int32)

    packed = pl.pallas_call(
        lambda *refs: pack_kernel(*refs, nar_count=nar_count, width=share),
        out_shape=jax.ShapeDtypeStruct((points, LANES), jnp.bfloat16),
        in_specs=[hbm] * 4,
        out_specs=vmem,
        scratch_shapes=[
            counts_scratch,
            pltpu.VMEM(send_rows.shape, jnp.int32),
            pltpu.VMEM(series.shape, series.dtype),
            pltpu.VMEM(table.shape, jnp.bfloat16),
            pltpu.SemaphoreType.DMA((4,)),
        ],
        compiler_params=pltpu.CompilerParams(vmem_limit_bytes=8 << 20),
        name="pack_rows",
    )(*map(in_hbm, (bin_counts, send_rows, series, jnp.asarray(table))))
    spectra = lax.all_to_all(packed, ("vol", "nar"), split_axis=0, concat_axis=0, tiled=True)
    far_shape = (share - near, 2 * points, observers)
    rest_shape = (4, LANES, observers)
    made = pltpu.VMEM((near, 2 * LANES, observers), jnp.bfloat16)
    seeds, rest, far_green, facing, amplitude = pl.pallas_call(
        lambda *refs: green_kernel(
            *refs, nar_count=nar_count, share=share, narrow=reach < 0.249
        ),
        out_shape=(
            jax.ShapeDtypeStruct((4, points - LANES, observers), jnp.float32),
            pltpu.HBM(rest_shape, jnp.float32),
            pltpu.HBM(far_shape, jnp.bfloat16),
            jax.ShapeDtypeStruct((3, observers), jnp.float32),
            jax.ShapeDtypeStruct((share, LANES), jnp.float32),
        ),
        in_specs=[hbm] * 3,
        out_specs=(vmem, hbm, hbm, vmem, vmem),
        scratch_shapes=[
            counts_scratch,
            pltpu.VMEM(observer_cells.shape, jnp.int32),
            pltpu.VMEM(place_rows.shape, jnp.float32),
            pltpu.VMEM((3, 8, observers), jnp.float32),
            pltpu.VMEM((points, 8), jnp.float32),
            pltpu.VMEM(rest_shape, jnp.float32),
            pltpu.VMEM(far_shape, jnp.bfloat16),
            pltpu.SemaphoreType.DMA((3,)),
            pltpu.SemaphoreType.DMA,
            pltpu.SemaphoreType.DMA,
        ],
        compiler_params=pltpu.CompilerParams(vmem_limit_bytes=24 << 20),
        cost_estimate=pl.CostEstimate(
            flops=60 * share * points * observers, bytes_accessed=4 * share * points * observers,
            transcendentals=0,
        ),
        name="green_grid",
    )(*map(in_hbm, (bin_counts, observer_cells, jnp.asarray(place_rows))))
    return pl.pallas_call(
        lambda *refs: moment_kernel(*refs, share=share),
        out_shape=jax.ShapeDtypeStruct((1, share, 2, observers), jnp.float32),
        in_specs=[vmem, vmem, hbm, hbm, vmem, vmem],
        out_specs=vmem,
        scratch_shapes=[
            pltpu.VMEM((2 * points // LANES, LANES, LANES), jnp.float32),
            pltpu.VMEM((observers // LANES, LANES, LANES), jnp.float32),
            pltpu.VMEM(rest_shape, jnp.float32),
            made,
            made,
            pltpu.VMEM(far_shape, jnp.bfloat16),
            pltpu.SemaphoreType.DMA((share - near,)),
            pltpu.SemaphoreType.DMA,
        ],
        compiler_params=pltpu.CompilerParams(
            vmem_limit_bytes=24 << 20
        ),
        name="moments",
    )(spectra, seeds, in_hbm(rest), in_hbm(far_green), facing, amplitude)


def solution(mesh):
    placed = (P(("vol", "nar"), None), P("vol", "nar", None), P(), P())
    return jax.shard_map(
        per_device,
        mesh=mesh,
        in_specs=placed,
        out_specs=P("nar", "vol", None, None),
        check_vma=False,
    )
```
